128 devices in a mesh: lat: 8 (over y, core), lon: 16 (over x, z).
Axes of the slice: x: 4, y: 4, z: 4, core: 2. Of those that a mesh axis runs over, the one named last changes fastest.
Arguments:
- obs_pert: bfloat16 [8192, 128, 256], P(('lat', 'lon')), may hold values from -4 to 4
- obs_dep: bfloat16 [8192, 128], P(('lat', 'lon')), may hold values from -6 to 6
- valid_rows: int32 [8192], P(('lat', 'lon')), may hold values from 1 to 128
- local_lists: int32 [512, 24], P(('lat', 'lon')), may hold values from 0 to 8191, as said below
- state_mean: float32 [8, 262144], P(None, ('lat', 'lon')), may hold values from -6 to 6
- state_pert: bfloat16 [8, 262144, 256], P(None, ('lat', 'lon')), may hold values from -6 to 6
- interp_lists: int32 [8192, 4], P(('lat', 'lon')), may hold values from 0 to 511, as said below
- interp_coef: float32 [4, 262144], P(None, ('lat', 'lon')), may hold values from 0.1 to 0.6
Outputs:
- analysis: bfloat16 [8, 262144, 256], P(None, ('lat', 'lon'))
The draws below stay inside these ranges and needn't reach their ends.
Inputs may be any that keep to these rules, and one draw needn't show every extreme that they name: `local_lists`: device i of lat+lon stores blocks i * 64 to (i + 1) * 64 - 1. Among the lists of the 4 domains of one device, at most 2 entries name blocks stored on any one device, and on every owner some device serves exactly 2. Entries may repeat. `interp_lists`: domain g is owned by device g // 4 of lat+lon. Every domain named for a tile of device (a, b) is owned by a device whose lat index differs from a by at most 1 and whose lon index differs from b by at most 1 modulo the lon axis's size.
All inputs are finite; a program needn't handle non-finite values.
Results may differ from the reference program's by a relative error of at most 0.003.
Values may be sent and summed in bfloat16 or wider, within the bound.
A program may use at most 256 MiB of HBM per device.

```python
import jax
import jax.numpy as jnp
from jax import lax

MEMBERS = 256
BLOCK_ROWS = 128
BLK_DEV = 64
DOM_DEV = 4
LIST_LEN = 24
NS_ITERS = 4
LEV = 8
TILE = 32
INTERP = 4
CAP = 2
NBLK = 8192
DOMS = 512
COLS = 262144
TILES = 8192
N_LAT = 8
N_LON = 16


def draw_local_lists(key, part):
    n_devices = DOMS // DOM_DEV
    capacity = CAP
    entries = DOM_DEV * LIST_LEN
    pool_size = n_devices * capacity

    def owner_lists(owner_key):
        key_rest = jax.random.fold_in(owner_key, 11)
        key_perm = jax.random.fold_in(owner_key, 12)
        key_local = jax.random.fold_in(owner_key, 13)
        key_order = jax.random.fold_in(owner_key, 14)
        rest = jax.random.permutation(key_rest, pool_size - capacity)[:entries - capacity] + capacity
        slots = jnp.concatenate([jnp.arange(capacity, dtype=jnp.int32), rest.astype(jnp.int32)])
        device_perm = jax.random.permutation(key_perm, n_devices).astype(jnp.int32)
        source = device_perm[slots // capacity]
        local_index = jax.random.randint(key_local, (entries,), 0, BLK_DEV, dtype=jnp.int32)
        listed = source * BLK_DEV + local_index
        order = jax.random.permutation(key_order, entries)
        return listed[order]
    owner_keys = jax.random.split(jax.random.fold_in(key, 5), n_devices)
    result = jax.vmap(owner_lists)(owner_keys)
    return result.reshape(DOMS, LIST_LEN).astype(jnp.int32)


def draw_interp_lists(key, part):
    n_devices = DOMS // DOM_DEV
    tiles_dev = TILES // n_devices
    device = jnp.arange(TILES, dtype=jnp.int32) // tiles_dev
    lat_here = device // N_LON
    lon_here = device % N_LON
    lat_step = jax.random.randint(jax.random.fold_in(key, 21), (TILES, INTERP), -1, 2, dtype=jnp.int32)
    lon_step = jax.random.randint(jax.random.fold_in(key, 22), (TILES, INTERP), -1, 2, dtype=jnp.int32)
    within = jax.random.randint(jax.random.fold_in(key, 23), (TILES, INTERP), 0, DOM_DEV, dtype=jnp.int32)
    lat_there = jnp.clip(lat_here[:, None] + lat_step, 0, N_LAT - 1)
    lon_there = (lon_here[:, None] + lon_step) % N_LON
    return ((lat_there * N_LON + lon_there) * DOM_DEV + within).astype(jnp.int32)


def place_ends(drawn, key, least, largest):
    dims = drawn.shape
    place = [jax.random.randint(jax.random.fold_in(key, axis), (), 0, dims[axis]) for axis in range(len(dims))]
    drawn = drawn.at[tuple(place)].set(least)
    longest = dims.index(max(dims))
    place[longest] = (place[longest] + 1) % dims[longest]
    return drawn.at[tuple(place)].set(largest)


def level_of(stream_key, extent, cuts, smallest, high):
    level, own = 1.0, jax.random.fold_in(stream_key, 6)
    for position, parts in cuts:
        steps = jnp.exp(jax.random.uniform(jax.random.fold_in(own, position), (parts,), jnp.float32, smallest / len(cuts), high / len(cuts)))
        level = level * jnp.repeat(steps, extent[position] // parts).reshape([-1 if axis == position else 1 for axis in range(len(extent))])
    return level


def scatter_about(key, dims, scale, limit, cuts=(), held_as=jnp.bfloat16):
    values = scale * jax.random.normal(key, dims, jnp.float32)
    if cuts:
        values = values * level_of(key, dims, cuts, -0.22, 0.18)
    return jnp.clip(values, -limit, limit).astype(held_as)


def setup_inputs(seed: int = 0) -> dict:
    key_list = jax.random.split(jax.random.key(seed), 9)
    return {
        "obs_pert": scatter_about(key_list[0], (NBLK, BLOCK_ROWS, MEMBERS), 0.5, 4.0, ((0, 128),)),
        "obs_dep": scatter_about(key_list[1], (NBLK, BLOCK_ROWS), 1.0, 6.0, ((0, 128),)),
        "valid_rows": place_ends(jax.random.randint(key_list[2], (NBLK,), 1, BLOCK_ROWS + 1), jax.random.fold_in(key_list[2], 1), 1, BLOCK_ROWS).astype(jnp.int32),
        "local_lists": draw_local_lists(jax.random.fold_in(key_list[8], 71), 0),
        "state_mean": scatter_about(key_list[4], (LEV, COLS), 1.0, 6.0, ((1, 128),), jnp.float32),
        "state_pert": scatter_about(key_list[5], (LEV, COLS, MEMBERS), 1.0, 6.0, ((1, 128),)),
        "interp_lists": draw_interp_lists(jax.random.fold_in(key_list[8], 71), 0),
        "interp_coef": jnp.clip(0.1 + 0.5 * jax.random.uniform(key_list[7], (INTERP, COLS), jnp.float32) ** level_of(key_list[7], (INTERP, COLS), ((1, 128),), -0.2, 0.2), 0.1, 0.6),
    }


def make_weights(gram, innov, members):
    identity = jnp.eye(members, dtype=jnp.float32)
    system = (members - 1.0) * identity + gram
    scale = jnp.sqrt(lax.optimization_barrier(jnp.sum(system * system, axis=(-2, -1))))[..., None, None]
    approx = system / scale
    inverse_root = jnp.broadcast_to(identity, system.shape)
    for sweep in range(NS_ITERS):
        factor = 1.5 * identity - 0.5 * jnp.matmul(inverse_root, approx, precision=lax.Precision.HIGHEST)
        approx = jnp.matmul(approx, factor, precision=lax.Precision.HIGHEST)
        inverse_root = jnp.matmul(factor, inverse_root, precision=lax.Precision.HIGHEST)
    inner = jnp.matmul(inverse_root, innov[..., None], precision=lax.Precision.HIGHEST)
    mean_weight = jnp.matmul(inverse_root, inner, precision=lax.Precision.HIGHEST) / scale
    return (jnp.sqrt((members - 1.0) / scale) * inverse_root + mean_weight).astype(jnp.bfloat16)

def reference(obs_pert, obs_dep, valid_rows, local_lists, state_mean, state_pert, interp_lists, interp_coef):
    block_rows = obs_pert.shape[1]
    members = obs_pert.shape[2]
    keep = jnp.arange(block_rows)[None, :] < valid_rows[:, None]
    masked_pert = jnp.where(keep[:, :, None], obs_pert, jnp.zeros((), jnp.bfloat16))
    masked_dep = jnp.where(keep, obs_dep, jnp.zeros((), jnp.bfloat16))

    def one_domain(listed):
        blocks = masked_pert[listed].astype(jnp.float32)
        departs = masked_dep[listed].astype(jnp.float32)
        gram = jnp.einsum('lri,lrj->ij', blocks, blocks, precision=lax.Precision.HIGHEST)
        innov = jnp.einsum('lri,lr->i', blocks, departs, precision=lax.Precision.HIGHEST)
        return make_weights(gram, innov, members)
    weights = lax.map(one_domain, local_lists)
    levels = state_pert.shape[0]
    columns = state_pert.shape[1]
    groups = DOMS // DOM_DEV
    per_group = columns // groups
    tiles_group = per_group // TILE
    grouped_pert = jnp.transpose(state_pert.reshape(levels, groups, tiles_group, TILE, members), (1, 0, 2, 3, 4))
    grouped_mean = jnp.transpose(state_mean.reshape(levels, groups, tiles_group, TILE), (1, 0, 2, 3))
    grouped_coef = jnp.transpose(interp_coef.reshape(INTERP, groups, tiles_group, TILE), (1, 0, 2, 3))
    grouped_lists = interp_lists.reshape(groups, tiles_group, INTERP)

    def one_group(pieces):
        perturbed, mean_here, coef_here, lists_here = pieces
        pert_float = perturbed.astype(jnp.float32)
        total = mean_here[..., None]
        for corner in range(INTERP):
            chosen = weights[lists_here[:, corner]].astype(jnp.float32)
            product = jnp.einsum('ltci,tij->ltcj', pert_float, chosen, precision=lax.Precision.HIGHEST)
            total = total + coef_here[corner][None, :, :, None] * product
        return total.astype(jnp.bfloat16)
    result = lax.map(one_group, (grouped_pert, grouped_mean, grouped_coef, grouped_lists))
    return jnp.transpose(result, (1, 0, 2, 3, 4)).reshape(levels, columns, members)
```

```python
import functools

import jax
import jax.numpy as jnp
from jax import lax
from jax.experimental import pallas as pl
from jax.experimental.pallas import tpu as pltpu
from jax.sharding import PartitionSpec as P

NS_ITERS = 4
MESH = pl.DeviceIdType.MESH
BIG = 1 << 20
PARTS = ((96, jnp.bfloat16, "xyz"), (96, jnp.bfloat16, "yzx"), (64, jnp.bfloat16, "zxy"), (8, jnp.float32, "zxy"))


def coords():
    a = lax.axis_index("lat")
    b = lax.axis_index("lon")
    return {"y": a // 2, "c": a % 2, "x": b // 4, "z": b % 4}


def device(pos):
    return (pos["y"] * 2 + pos["c"], pos["x"] * 4 + pos["z"])


def shifted(pos, axis, step):
    size = 2 if axis == "c" else 4
    return device({**pos, axis: (pos[axis] + step) % size})


def greet(peers):
    barrier = pltpu.get_barrier_semaphore()
    for peer in peers:
        pl.semaphore_signal(barrier, inc=1, device_id=peer, device_id_type=MESH)
    pl.semaphore_wait(barrier, len(peers))


def lists_kernel(tile_ref, pert_ref, dep_ref, keys_ref, sib_tile_ref, sib_pert_ref, sib_dep_ref,
                 held, send_sem, recv_sem, sib_send, sib_recv):
    pos = coords()
    x, y, z = pos["x"], pos["y"], pos["z"]
    sibling = shifted(pos, "c", 1)
    greet([shifted(pos, axis, step) for axis in "zxy" for step in (1, 2, 3)] + [sibling])
    swaps = []
    for k, (src, dst) in enumerate(((pert_ref, sib_pert_ref), (dep_ref, sib_dep_ref), (tile_ref, sib_tile_ref))):
        swap = pltpu.make_async_remote_copy(
            src_ref=src, dst_ref=dst, send_sem=sib_send.at[k], recv_sem=sib_recv.at[k],
            device_id=sibling, device_id_type=MESH)
        swap.start()
        swaps.append(swap)
    held[y, x, z] = tile_ref[...]
    sent = []
    for phase, axis in enumerate("zxy"):
        view = held.at[y, x, z] if axis == "z" else (held.at[y, x] if axis == "x" else held.at[y])
        copies = []
        for step in (1, 2, 3):
            copy = pltpu.make_async_remote_copy(
                src_ref=view, dst_ref=view, send_sem=send_sem.at[phase, step - 1],
                recv_sem=recv_sem.at[phase, step - 1],
                device_id=shifted(pos, axis, step), device_id_type=MESH)
            copy.start()
            copies.append(copy)
        for copy in copies:
            copy.wait_recv()
        sent += copies
    me = device(pos)
    own = me[0] * 16 + me[1]
    other = sibling[0] * 16 + sibling[1]
    entry = held[...].reshape(64, 8, 128)
    lane = lax.broadcasted_iota(jnp.int32, (64, 8, 128), 2)
    row = lax.broadcasted_iota(jnp.int32, (64, 8, 128), 1)
    owner = entry >> 6
    local_index = entry & 63
    block = jnp.where(owner == own, local_index, local_index + 64)
    value = jnp.where(((owner == own) | (owner == other)) & (row < 4), lane * 128 + block, BIG)
    out = jnp.full((64, 8, 128), BIG, jnp.int32)
    for k in range(4):
        least = jnp.min(value, axis=2, keepdims=True)
        out = jnp.where(lane == k, least, out)
        value = jnp.where(value > least, value, BIG)
    keys_ref[...] = out
    for copy in sent:
        copy.wait_send()
    for swap in swaps:
        swap.wait()


def gather_lists(tile, pert, dep):
    any_spec = pl.BlockSpec(memory_space=pl.ANY)
    vmem = pl.BlockSpec(memory_space=pltpu.VMEM)
    return pl.pallas_call(
        lists_kernel,
        out_shape=(
            jax.ShapeDtypeStruct((64, 8, 128), jnp.int32),
            jax.ShapeDtypeStruct((8, 128), jnp.int32),
            jax.ShapeDtypeStruct(pert.shape, pert.dtype),
            jax.ShapeDtypeStruct(dep.shape, dep.dtype),
        ),
        in_specs=[vmem, any_spec, any_spec],
        out_specs=(vmem, vmem, any_spec, any_spec),
        scratch_shapes=[
            pltpu.VMEM((4, 4, 4, 8, 128), jnp.int32),
            pltpu.SemaphoreType.DMA((3, 3)),
            pltpu.SemaphoreType.DMA((3, 3)),
            pltpu.SemaphoreType.DMA((3,)),
            pltpu.SemaphoreType.DMA((3,)),
        ],
        compiler_params=pltpu.CompilerParams(collective_id=0, has_side_effects=True),
        name="lists",
    )(tile, pert, dep)


def gram_kernel(keys_ref, valid_ref, pert_ref, sib_ref, dep_ref, sib_dep_ref, out0, out1, out2, out3, blocks, deps, sems):
    step = pl.program_id(0)

    @pl.when(step == 0)
    def _():
        loads = [
            pltpu.make_async_copy(pert_ref, blocks.at[pl.ds(0, 64)], sems.at[0]),
            pltpu.make_async_copy(sib_ref, blocks.at[pl.ds(64, 64)], sems.at[1]),
        ]
        for load in loads:
            load.start()
        deps[pl.ds(0, 64)] = dep_ref[...].astype(jnp.float32)
        deps[pl.ds(64, 64)] = sib_dep_ref[...].astype(jnp.float32)
        for load in loads:
            load.wait()

    rows = lax.broadcasted_iota(jnp.int32, (128, 256), 0)
    tri_row = lax.broadcasted_iota(jnp.int32, (128, 128), 0)
    tri_col = lax.broadcasted_iota(jnp.int32, (128, 128), 1)

    def piece(block):
        count = valid_ref[block]
        held = blocks[block]
        held = jnp.where(rows < count, held, jnp.zeros((), jnp.bfloat16))
        left, right = held[:, :128], held[:, 128:]
        top = lax.dot_general(left, held, (((0,), (0,)), ((), ())), preferred_element_type=jnp.float32)
        g22 = lax.dot_general(right, right, (((0,), (0,)), ((), ())), preferred_element_type=jnp.float32)
        g11, g12 = top[:, :128], top[:, 128:]
        packed = jnp.where(tri_col >= tri_row, g11, g22)
        d1 = jnp.sum(jnp.where(tri_col == tri_row, g11, 0.0), axis=0, keepdims=True)
        d2 = jnp.sum(jnp.where(tri_col == tri_row, g22, 0.0), axis=0, keepdims=True)
        dep = jnp.broadcast_to(deps[pl.ds(block, 1), :], (8, 128)).astype(jnp.bfloat16)
        inn = jnp.dot(dep, held, preferred_element_type=jnp.float32)
        extra = jnp.concatenate([d1, d2, inn[:1, :128], inn[:1, 128:], jnp.zeros((4, 128), jnp.float32)], axis=0)
        return g12, packed, extra

    def put(zz, dom, g12, packed, extra, add):
        def merge(ref, index, value):
            if add:
                value = value + ref[index].astype(jnp.float32)
            ref[index] = value.astype(ref.dtype)
        merge(out0, (0, 0, zz, pl.ds(dom * 96, 96)), g12[:96])
        merge(out1, (0, zz, 0, pl.ds(dom * 96, 32)), g12[96:])
        merge(out1, (0, zz, 0, pl.ds(dom * 96 + 32, 64)), packed[:64])
        merge(out2, (zz, 0, 0, pl.ds(dom * 64, 64)), packed[64:])
        merge(out3, (zz, 0, 0, pl.ds(dom * 8, 8)), extra)

    for zz in range(4):
        xx, yy = step // 4, step % 4
        base = ((yy * 4 + xx) * 4 + zz) * 16
        for dom in range(4):
            first = keys_ref[base + dom * 4]

            @pl.when(first >= BIG)
            def _():
                out0[0, 0, zz, pl.ds(dom * 96, 96)] = jnp.zeros((96, 128), jnp.bfloat16)
                out1[0, zz, 0, pl.ds(dom * 96, 96)] = jnp.zeros((96, 128), jnp.bfloat16)
                out2[zz, 0, 0, pl.ds(dom * 64, 64)] = jnp.zeros((64, 128), jnp.bfloat16)
                out3[zz, 0, 0, pl.ds(dom * 8, 8)] = jnp.zeros((8, 128), jnp.float32)

    def body(server_dom, carry):
        zz, dom = server_dom // 4, server_dom % 4
        xx, yy = step // 4, step % 4
        base = ((yy * 4 + xx) * 4 + zz) * 16 + dom * 4

        @pl.when(keys_ref[base] < BIG)
        def _():
            put(zz, dom, *piece(keys_ref[base] % 128), add=False)
            for k in range(1, 4):
                @pl.when(keys_ref[base + k] < BIG)
                def _():
                    put(zz, dom, *piece(keys_ref[base + k] % 128), add=True)
        return carry

    lax.fori_loop(0, 16, body, 0)


def partial_grams(keys, valid, pert, sib_pert, dep, sib_dep):
    any_spec = pl.BlockSpec(memory_space=pl.ANY)
    full = pl.BlockSpec((64, 128), lambda i, *_: (0, 0))
    maps = (
        ((1, 1, 4), lambda i, *_: (i // 4, i % 4, 0, 0, 0)),
        ((1, 4, 1), lambda i, *_: (i % 4, 0, i // 4, 0, 0)),
        ((4, 1, 1), lambda i, *_: (0, i // 4, i % 4, 0, 0)),
        ((4, 1, 1), lambda i, *_: (0, i // 4, i % 4, 0, 0)),
    )
    return pl.pallas_call(
        gram_kernel,
        out_shape=tuple(jax.ShapeDtypeStruct((4, 4, 4, 4 * r, 128), t) for r, t, _ in PARTS),
        grid_spec=pltpu.PrefetchScalarGridSpec(
            num_scalar_prefetch=2,
            grid=(16,),
            in_specs=[any_spec, any_spec, full, full],
            out_specs=tuple(
                pl.BlockSpec(lead + (4 * r, 128), index) for (r, _, _), (lead, index) in zip(PARTS, maps)
            ),
            scratch_shapes=[
                pltpu.VMEM((128, 128, 256), jnp.bfloat16),
                pltpu.VMEM((128, 128), jnp.float32),
                pltpu.SemaphoreType.DMA((2,)),
            ],
        ),
        compiler_params=pltpu.CompilerParams(
            dimension_semantics=("arbitrary",), vmem_limit_bytes=40 << 20),
        name="grams",
    )(keys, valid, pert, sib_pert, dep, sib_dep)


def split(value):
    high = value.astype(jnp.bfloat16)
    return high, (value - high.astype(jnp.float32)).astype(jnp.bfloat16)


def product(left, right):
    (lh, ll), (rh, rl) = left, right
    dot = functools.partial(jnp.dot, preferred_element_type=jnp.float32)
    return dot(lh, rh) + (dot(lh, rl) + dot(ll, rh))


def weights_of(g12, packed, extra, members):
    half = members // 2
    row = lax.broadcasted_iota(jnp.int32, (half, half), 0)
    col = lax.broadcasted_iota(jnp.int32, (half, half), 1)
    turned = packed.T
    g11 = jnp.where(col > row, packed, turned)
    g22 = jnp.where(col < row, packed, turned)
    g11 = jnp.where(col == row, extra[0:1], g11)
    g22 = jnp.where(col == row, extra[1:2], g22)
    gram = jnp.concatenate(
        [jnp.concatenate([g11, g12], axis=1), jnp.concatenate([g12.T, g22], axis=1)], axis=0)
    wide_row = lax.broadcasted_iota(jnp.int32, (members, members), 0)
    wide_col = lax.broadcasted_iota(jnp.int32, (members, members), 1)
    identity = jnp.where(wide_row == wide_col, 1.0, 0.0).astype(jnp.float32)
    system = (members - 1.0) * identity + gram
    total = jnp.sum(jnp.sum(system * system, axis=0, keepdims=True), axis=1, keepdims=True)
    scale = jnp.sqrt(total)
    approx = system / scale
    factor = 1.5 * identity - 0.5 * approx
    root = factor
    approx = product(split(approx), split(factor))
    for sweep in range(1, NS_ITERS):
        root_parts = split(root)
        factor = 1.5 * identity - 0.5 * product(root_parts, split(approx))
        factor_parts = split(factor)
        if sweep < NS_ITERS - 1:
            approx = product(split(approx), factor_parts)
        root = product(factor_parts, root_parts)
    innov = jnp.concatenate([extra[2:3], extra[3:4]], axis=1)
    innov = jnp.broadcast_to(innov, (8, members))
    root_parts = split(root)
    inner = product(split(innov), root_parts)
    mean = product(split(inner), root_parts) / scale
    mean_cols = jnp.concatenate(
        [jnp.broadcast_to(mean[:1, :half], (half, half)).T, jnp.broadcast_to(mean[:1, half:], (half, half)).T], axis=0)
    mean_full = jnp.concatenate([mean_cols, mean_cols], axis=1)
    return (jnp.sqrt((members - 1.0) / scale) * root + mean_full).astype(jnp.bfloat16)


def reduce_kernel(p0, p1, p2, p3, near_ref, *scratch):
    n = len(PARTS)
    parts = (p0, p1, p2, p3)
    scratch = list(scratch)

    def take(count):
        taken, scratch[:count] = scratch[:count], []
        return taken
    acc = take(n)
    side_r, side_l = take(n), take(n)
    bufs = [[take(6) for _ in range(n)] for _ in range(3)]
    fins = take(n)
    own, send_sem, recv_sem, load_sem, halo_send, halo_recv, own_sem = scratch

    pos = coords()
    a, b = lax.axis_index("lat"), lax.axis_index("lon")
    lat_up, lat_down = ((a + 1) % 8, b), ((a + 7) % 8, b)
    lon_up, lon_down = (a, (b + 1) % 16), (a, (b + 15) % 16)
    loads = []
    for i, (_, _, order) in enumerate(PARTS):
        m = pos[order[0]]
        mine = [
            pltpu.make_async_copy(parts[i].at[(m + 1) % 4, pl.ds(0, 2)], side_r[i], load_sem.at[i, 0]),
            pltpu.make_async_copy(parts[i].at[(m + 3) % 4, pl.ds(2, 2)], side_l[i], load_sem.at[i, 1]),
            pltpu.make_async_copy(parts[i].at[m], acc[i], load_sem.at[i, 2]),
        ]
        for load in mine:
            load.start()
        loads.append(mine)
    greet([shifted(pos, axis, step) for axis in "xyz" for step in (1, 3)] + [lat_up, lat_down, lon_up, lon_down])

    sends = []

    def slab(i, phase, target, upper):
        rows = PARTS[i][0]
        order = PARTS[i][2]
        if phase == 0:
            return parts[i].at[target, pl.ds(2 * upper, 2)]
        if phase == 1:
            return acc[i].at[target, pl.ds(2 * upper, 2)]
        return acc[i].at[pos[order[1]], target, pl.ds(2 * rows * upper, 2 * rows)]

    for phase in range(3):
        def start(i, k, source, to_right):
            axis = PARTS[i][2][phase]
            copy = pltpu.make_async_remote_copy(
                src_ref=source, dst_ref=bufs[phase][i][k],
                send_sem=send_sem.at[phase, i, k], recv_sem=recv_sem.at[phase, i, k],
                device_id=shifted(pos, axis, 1 if to_right else 3), device_id_type=MESH)
            copy.start()
            sends.append(copy)
            return copy

        flights = [[None] * 6 for _ in range(n)]
        for i in range(n):
            m = pos[PARTS[i][2][phase]]
            flights[i][0] = start(i, 0, slab(i, phase, (m + 2) % 4, 0), True)
            flights[i][1] = start(i, 1, slab(i, phase, (m + 2) % 4, 1), False)
        for i in range(n):
            m = pos[PARTS[i][2][phase]]
            flights[i][2] = start(i, 2, slab(i, phase, (m + 1) % 4, 1), True)
            flights[i][3] = start(i, 3, slab(i, phase, (m + 3) % 4, 0), False)
        for i in range(n):
            rows, dtype, order = PARTS[i]
            m = pos[order[phase]]
            for k, (target, upper) in enumerate((((m + 1) % 4, 0), ((m + 3) % 4, 1))):
                flights[i][k].wait_recv()
                got = bufs[phase][i][k]
                if phase == 0:
                    loads[i][k].wait()
                    side = (side_r, side_l)[k][i]

                    def body(j, carry, got=got, side=side):
                        p, q = j // 4, j % 4
                        got[p, q] = (got[p, q].astype(jnp.float32) + side[p, q].astype(jnp.float32)).astype(got.dtype)
                        return carry
                    lax.fori_loop(0, 8, body, 0)
                elif phase == 1:
                    def body(j, carry, got=got, target=target, upper=upper, i=i):
                        got[j] = (got[j].astype(jnp.float32)
                                  + acc[i][target, 2 * upper + j].astype(jnp.float32)).astype(got.dtype)
                        return carry
                    lax.fori_loop(0, 2, body, 0)
                else:
                    mine = acc[i][pos[order[1]], target, pl.ds(2 * rows * upper, 2 * rows)]
                    got[...] = (got[...].astype(jnp.float32) + mine.astype(jnp.float32)).astype(got.dtype)
                flights[i][4 + k] = start(i, 4 + k, got, k == 0)
        for i in range(n):
            rows, dtype, order = PARTS[i]
            m = pos[order[phase]]
            for k in (2, 3, 4, 5):
                flights[i][k].wait_recv()
            buf = bufs[phase][i]
            pairs = ((4, 3), (2, 5))
            if phase == 0:
                loads[i][2].wait()
            for upper, (k0, k1) in enumerate(pairs):
                f, g = buf[k0], buf[k1]
                if phase == 0:
                    def body(j, carry, f=f, g=g, upper=upper, i=i):
                        p, q = j // 4, j % 4
                        total = (acc[i][2 * upper + p, q].astype(jnp.float32) + f[p, q].astype(jnp.float32)
                                 + g[p, q].astype(jnp.float32))
                        acc[i][2 * upper + p, q] = total.astype(acc[i].dtype)
                        return carry
                    lax.fori_loop(0, 8, body, 0)
                elif phase == 1:
                    def body(j, carry, f=f, g=g, upper=upper, i=i, m=m):
                        total = (acc[i][m, 2 * upper + j].astype(jnp.float32) + f[j].astype(jnp.float32)
                                 + g[j].astype(jnp.float32))
                        acc[i][m, 2 * upper + j] = total.astype(acc[i].dtype)
                        return carry
                    lax.fori_loop(0, 2, body, 0)
                else:
                    span = pl.ds(2 * rows * upper, 2 * rows)
                    fins[i][span] = (acc[i][pos[order[1]], m, span].astype(jnp.float32)
                                     + f[...].astype(jnp.float32) + g[...].astype(jnp.float32))

    def solve(d, carry):
        g12 = jnp.concatenate([fins[0][pl.ds(d * 96, 96)], fins[1][pl.ds(d * 96, 32)]], axis=0)
        packed = jnp.concatenate([fins[1][pl.ds(d * 96 + 32, 64)], fins[2][pl.ds(d * 64, 64)]], axis=0)
        own[d] = weights_of(g12, packed, fins[3][pl.ds(d * 8, 8)], 256)
        return carry
    lax.fori_loop(0, 4, solve, 0)

    keep = pltpu.make_async_copy(own, near_ref.at[1, 1], own_sem)
    keep.start()

    def halo(k, source, dst, target):
        copy = pltpu.make_async_remote_copy(
            src_ref=source, dst_ref=dst, send_sem=halo_send.at[k], recv_sem=halo_recv.at[k],
            device_id=target, device_id_type=MESH)
        copy.start()
        sends.append(copy)
        return copy
    east = halo(0, own, near_ref.at[1, 0], lon_up)
    west = halo(1, own, near_ref.at[1, 2], lon_down)
    arriving = [halo(2, own, near_ref.at[0, 1], lat_up), halo(3, own, near_ref.at[2, 1], lat_down)]
    east.wait_recv()
    arriving += [halo(4, near_ref.at[1, 0], near_ref.at[0, 0], lat_up),
                 halo(5, near_ref.at[1, 0], near_ref.at[2, 0], lat_down)]
    west.wait_recv()
    arriving += [halo(6, near_ref.at[1, 2], near_ref.at[0, 2], lat_up),
                 halo(7, near_ref.at[1, 2], near_ref.at[2, 2], lat_down)]
    for copy in arriving:
        copy.wait_recv()
    for copy in sends:
        copy.wait_send()
    keep.wait()


def near_weights(parts):
    n = len(PARTS)
    any_spec = pl.BlockSpec(memory_space=pl.ANY)
    def vmem(shape, kind):
        return pltpu.VMEM(shape, kind)
    scratch = [vmem((4, 4, 4 * r, 128), t) for r, t, _ in PARTS]
    scratch += [vmem((2, 4, 4 * r, 128), t) for r, t, _ in PARTS] * 2
    for phase in range(3):
        for r, t, _ in PARTS:
            shape = ((2, 4, 4 * r, 128), (2, 4 * r, 128), (2 * r, 128))[phase]
            scratch += [vmem(shape, t)] * 6
    scratch += [vmem((4 * r, 128), jnp.float32) for r, _, _ in PARTS]
    scratch += [
        vmem((4, 256, 256), jnp.bfloat16),
        pltpu.SemaphoreType.DMA((3, n, 6)),
        pltpu.SemaphoreType.DMA((3, n, 6)),
        pltpu.SemaphoreType.DMA((n, 3)),
        pltpu.SemaphoreType.DMA((8,)),
        pltpu.SemaphoreType.DMA((8,)),
        pltpu.SemaphoreType.DMA(()),
    ]
    return pl.pallas_call(
        reduce_kernel,
        out_shape=jax.ShapeDtypeStruct((3, 3, 4, 256, 256), jnp.bfloat16),
        in_specs=[any_spec] * n,
        out_specs=any_spec,
        scratch_shapes=scratch,
        compiler_params=pltpu.CompilerParams(
            collective_id=1, has_side_effects=True, vmem_limit_bytes=52 << 20),
        name="reduce",
    )(*parts)


STEP_TILES = 4


def interp_kernel(pos_ref, pert_ref, mean_ref, coef_ref, near_ref, out_ref):
    step = pl.program_id(0)
    mean_cols = mean_ref[...].T
    coef = coef_ref[...]
    coef_cols = jnp.concatenate([coef, coef], axis=0).T
    for tile in range(STEP_TILES):
        span = pl.ds(tile * 32, 32)
        held = pert_ref[:, span, :].reshape(256, 256)
        total = None
        for corner in range(4):
            where = pos_ref[(step * STEP_TILES + tile) * 4 + corner]
            prod = jnp.dot(held, near_ref[where], preferred_element_type=jnp.float32)
            factor = coef_cols[tile * 32:tile * 32 + 32, corner:corner + 1]
            term = prod.reshape(8, 32, 256) * factor[None]
            total = term if total is None else total + term
        for level in range(8):
            base = mean_cols[tile * 32:tile * 32 + 32, level:level + 1]
            out_ref[level, span, :] = (total[level] + base).astype(jnp.bfloat16)


def interpolate(position, pert, mean, coef, near):
    cols = STEP_TILES * 32
    steps = pert.shape[1] // cols
    return pl.pallas_call(
        interp_kernel,
        out_shape=jax.ShapeDtypeStruct(pert.shape, jnp.bfloat16),
        grid_spec=pltpu.PrefetchScalarGridSpec(
            num_scalar_prefetch=1,
            grid=(steps,),
            in_specs=[
                pl.BlockSpec((8, cols, 256), lambda i, *_: (0, i, 0)),
                pl.BlockSpec((8, cols), lambda i, *_: (0, i)),
                pl.BlockSpec((4, cols), lambda i, *_: (0, i)),
                pl.BlockSpec((36, 256, 256), lambda i, *_: (0, 0, 0), pipeline_mode=pl.Buffered(1)),
            ],
            out_specs=pl.BlockSpec((8, cols, 256), lambda i, *_: (0, i, 0)),
        ),
        compiler_params=pltpu.CompilerParams(
            dimension_semantics=("arbitrary",), vmem_limit_bytes=32 << 20),
        name="interp",
    )(position, pert, mean, coef, near)


def local(
    obs_pert, obs_dep, valid_rows, local_lists, state_mean, state_pert, interp_lists, interp_coef
):
    n_lon = lax.axis_size("lon")
    domains_here = local_lists.shape[0]
    tile = jnp.concatenate([
        jnp.pad(local_lists, ((0, 0), (0, 128 - local_lists.shape[1])), constant_values=-1),
        jnp.pad(valid_rows[None, :], ((0, 3), (0, 64))),
    ], axis=0)
    keys, sib_tile, sib_pert, sib_dep = gather_lists(tile, obs_pert, obs_dep)
    keys = keys[:, :4, :4].reshape(-1)
    valid = jnp.concatenate([valid_rows, sib_tile[4, :64]])
    parts = partial_grams(keys, valid, obs_pert, sib_pert, obs_dep, sib_dep)
    near = near_weights(parts)
    owner = interp_lists // domains_here
    within = interp_lists % domains_here
    lat_step = owner // n_lon - lax.axis_index("lat")
    lon_step = (owner % n_lon - lax.axis_index("lon") + 1) % n_lon - 1
    position = ((lat_step + 1) * 3 + lon_step + 1) * domains_here + within
    return interpolate(position.reshape(-1), state_pert, state_mean, interp_coef, near.reshape(36, 256, 256))


def solution(mesh):
    in_specs = (
        P(("lat", "lon"), None, None),
        P(("lat", "lon"), None),
        P(("lat", "lon")),
        P(("lat", "lon"), None),
        P(None, ("lat", "lon")),
        P(None, ("lat", "lon"), None),
        P(("lat", "lon"), None),
        P(None, ("lat", "lon")),
    )
    out_specs = P(None, ("lat", "lon"), None)
    return jax.shard_map(local, mesh=mesh, in_specs=in_specs, out_specs=out_specs, check_vma=False)
```

```python
import functools

import jax
import jax.numpy as jnp
from jax import lax
from jax.experimental import pallas as pl
from jax.experimental.pallas import tpu as pltpu
from jax.sharding import PartitionSpec as P

NS_ITERS = 4
MESH = pl.DeviceIdType.MESH
BIG = 1 << 20
PARTS = ((96, jnp.bfloat16, "xyz"), (96, jnp.bfloat16, "yzx"), (64, jnp.bfloat16, "zxy"), (8, jnp.float32, "zxy"))


def coords():
    a = lax.axis_index("lat")
    b = lax.axis_index("lon")
    return {"y": a // 2, "c": a % 2, "x": b // 4, "z": b % 4}


def device(pos):
    return (pos["y"] * 2 + pos["c"], pos["x"] * 4 + pos["z"])


def shifted(pos, axis, step):
    size = 2 if axis == "c" else 4
    return device({**pos, axis: (pos[axis] + step) % size})


def greet(peers):
    barrier = pltpu.get_barrier_semaphore()
    for peer in peers:
        pl.semaphore_signal(barrier, inc=1, device_id=peer, device_id_type=MESH)
    pl.semaphore_wait(barrier, len(peers))


def lists_kernel(tile_ref, pert_ref, dep_ref, keys_ref, sib_tile_ref, sib_pert_ref, sib_dep_ref,
                 held, send_sem, recv_sem, sib_send, sib_recv):
    pos = coords()
    x, y, z = pos["x"], pos["y"], pos["z"]
    sibling = shifted(pos, "c", 1)
    greet([shifted(pos, axis, step) for axis in "zxy" for step in (1, 2, 3)] + [sibling])
    swaps = []
    for k, (src, dst) in enumerate(((pert_ref, sib_pert_ref), (dep_ref, sib_dep_ref), (tile_ref, sib_tile_ref))):
        swap = pltpu.make_async_remote_copy(
            src_ref=src, dst_ref=dst, send_sem=sib_send.at[k], recv_sem=sib_recv.at[k],
            device_id=sibling, device_id_type=MESH)
        swap.start()
        swaps.append(swap)
    held[y, x, z] = tile_ref[...]
    sent = []
    for phase, axis in enumerate("zxy"):
        view = held.at[y, x, z] if axis == "z" else (held.at[y, x] if axis == "x" else held.at[y])
        copies = []
        for step in (1, 2, 3):
            copy = pltpu.make_async_remote_copy(
                src_ref=view, dst_ref=view, send_sem=send_sem.at[phase, step - 1],
                recv_sem=recv_sem.at[phase, step - 1],
                device_id=shifted(pos, axis, step), device_id_type=MESH)
            copy.start()
            copies.append(copy)
        for copy in copies:
            copy.wait_recv()
        sent += copies
    me = device(pos)
    own = me[0] * 16 + me[1]
    other = sibling[0] * 16 + sibling[1]
    entry = held[...].reshape(64, 8, 128)
    lane = lax.broadcasted_iota(jnp.int32, (64, 8, 128), 2)
    row = lax.broadcasted_iota(jnp.int32, (64, 8, 128), 1)
    owner = entry >> 6
    local_index = entry & 63
    block = jnp.where(owner == own, local_index, local_index + 64)
    value = jnp.where(((owner == own) | (owner == other)) & (row < 4), row * 4096 + lane * 128 + block, BIG)
    out = jnp.full((64, 8, 128), BIG, jnp.int32)
    for k in range(4):
        least = jnp.min(jnp.min(value, axis=2, keepdims=True), axis=1, keepdims=True)
        out = jnp.where(lane == k, least, out)
        value = jnp.where(value > least, value, BIG)
    keys_ref[...] = out
    for copy in sent:
        copy.wait_send()
    for swap in swaps:
        swap.wait()


def gather_lists(tile, pert, dep):
    any_spec = pl.BlockSpec(memory_space=pltpu.HBM)
    vmem = pl.BlockSpec(memory_space=pltpu.VMEM)
    return pl.pallas_call(
        lists_kernel,
        out_shape=(
            jax.ShapeDtypeStruct((64, 8, 128), jnp.int32),
            jax.ShapeDtypeStruct((8, 128), jnp.int32),
            jax.ShapeDtypeStruct(pert.shape, pert.dtype),
            jax.ShapeDtypeStruct(dep.shape, dep.dtype),
        ),
        in_specs=[vmem, any_spec, any_spec],
        out_specs=(vmem, vmem, any_spec, any_spec),
        scratch_shapes=[
            pltpu.VMEM((4, 4, 4, 8, 128), jnp.int32),
            pltpu.SemaphoreType.DMA((3, 3)),
            pltpu.SemaphoreType.DMA((3, 3)),
            pltpu.SemaphoreType.DMA((3,)),
            pltpu.SemaphoreType.DMA((3,)),
        ],
        compiler_params=pltpu.CompilerParams(collective_id=0, has_side_effects=True),
        name="lists",
    )(tile, pert, dep)


def split(value):
    high = value.astype(jnp.bfloat16)
    return high, (value - high.astype(jnp.float32)).astype(jnp.bfloat16)


def product(left, right):
    (lh, ll), (rh, rl) = left, right
    dot = functools.partial(jnp.dot, preferred_element_type=jnp.float32)
    return dot(lh, rh) + (dot(lh, rl) + dot(ll, rh))


def weights_of(g12, packed, extra, members):
    half = members // 2
    row = lax.broadcasted_iota(jnp.int32, (half, half), 0)
    col = lax.broadcasted_iota(jnp.int32, (half, half), 1)
    turned = packed.T
    g11 = jnp.where(col > row, packed, turned)
    g22 = jnp.where(col < row, packed, turned)
    g11 = jnp.where(col == row, extra[0:1], g11)
    g22 = jnp.where(col == row, extra[1:2], g22)
    gram = jnp.concatenate(
        [jnp.concatenate([g11, g12], axis=1), jnp.concatenate([g12.T, g22], axis=1)], axis=0)
    wide_row = lax.broadcasted_iota(jnp.int32, (members, members), 0)
    wide_col = lax.broadcasted_iota(jnp.int32, (members, members), 1)
    identity = jnp.where(wide_row == wide_col, 1.0, 0.0).astype(jnp.float32)
    system = (members - 1.0) * identity + gram
    total = jnp.sum(jnp.sum(system * system, axis=0, keepdims=True), axis=1, keepdims=True)
    scale = jnp.sqrt(total)
    approx = system / scale
    factor = 1.5 * identity - 0.5 * approx
    root = factor
    approx = product(split(approx), split(factor))
    for sweep in range(1, NS_ITERS):
        root_parts = split(root)
        factor = 1.5 * identity - 0.5 * product(root_parts, split(approx))
        factor_parts = split(factor)
        if sweep < NS_ITERS - 1:
            approx = product(split(approx), factor_parts)
        root = product(factor_parts, root_parts)
    innov = jnp.concatenate([extra[2:3], extra[3:4]], axis=1)
    innov = jnp.broadcast_to(innov, (8, members))
    root_parts = split(root)
    inner = product(split(innov), root_parts)
    mean = product(split(inner), root_parts) / scale
    mean_cols = jnp.concatenate(
        [jnp.broadcast_to(mean[:1, :half], (half, half)).T, jnp.broadcast_to(mean[:1, half:], (half, half)).T], axis=0)
    mean_full = jnp.concatenate([mean_cols, mean_cols], axis=1)
    return (jnp.sqrt((members - 1.0) / scale) * root + mean_full).astype(jnp.bfloat16)


def fill_server(place, keys_ref, valid_ref, blocks, deps, grams):
    px, py, pz = place
    base = ((py * 4 + px) * 4 + pz) * 4
    rows = lax.broadcasted_iota(jnp.int32, (128, 256), 0)
    row8 = lax.broadcasted_iota(jnp.int32, (8, 128), 0)
    tri_row = lax.broadcasted_iota(jnp.int32, (128, 128), 0)
    tri_col = lax.broadcasted_iota(jnp.int32, (128, 128), 1)
    held, turned, doms, departs = [], [], [], []
    for j in range(4):
        key = keys_ref[base + j]
        block = key & 127
        dom = key >> 12
        count = jnp.where(key < BIG, valid_ref[block], 0)
        values = jnp.where(rows < count, blocks[block], jnp.zeros((), jnp.bfloat16))
        held.append(values)
        turned.append(values.T)
        doms.append(dom)
        depart = jnp.broadcast_to(deps[pl.ds(block, 1), :], (8, 128))
        departs.append(jnp.where(row8 == dom, depart, 0.0).astype(jnp.bfloat16))
    stacked = jnp.concatenate(held, axis=0)
    inn = jnp.dot(jnp.concatenate(departs, axis=1), stacked, preferred_element_type=jnp.float32)
    for d in range(4):
        left = jnp.concatenate(
            [jnp.where(doms[j] == d, turned[j], jnp.zeros((), jnp.bfloat16)) for j in range(4)], axis=1)
        gram = jnp.dot(left, stacked, preferred_element_type=jnp.float32)
        g11, g12, g22 = gram[:128, :128], gram[:128, 128:], gram[128:, 128:]
        packed = jnp.where(tri_col >= tri_row, g11, g22).astype(jnp.bfloat16)
        g12 = g12.astype(jnp.bfloat16)
        d1 = jnp.sum(jnp.where(tri_col == tri_row, g11, 0.0), axis=0, keepdims=True)
        d2 = jnp.sum(jnp.where(tri_col == tri_row, g22, 0.0), axis=0, keepdims=True)
        grams[0][px, py, pz, pl.ds(d * 96, 96)] = g12[:96]
        grams[1][py, pz, px, pl.ds(d * 96, 32)] = g12[96:]
        grams[1][py, pz, px, pl.ds(d * 96 + 32, 64)] = packed[:64]
        grams[2][pz, px, py, pl.ds(d * 64, 64)] = packed[64:]
        grams[3][pz, px, py, pl.ds(d * 8, 8)] = jnp.concatenate(
            [d1, d2, inn[d:d + 1, :128], inn[d:d + 1, 128:], jnp.zeros((4, 128), jnp.float32)], axis=0)


def reduce_kernel(keys_ref, valid_ref, pert_ref, sib_ref, dep_ref, sib_dep_ref, near_ref, *scratch):
    n = len(PARTS)
    scratch = list(scratch)

    def take(count):
        taken, scratch[:count] = scratch[:count], []
        return taken
    blocks, deps = take(2)
    grams = take(n)
    bufs = [[take(6) for _ in range(n)] for _ in range(3)]
    fins = take(n)
    own, send_sem, recv_sem, load_sem, halo_send, halo_recv, own_sem = scratch

    pos = coords()
    a, b = lax.axis_index("lat"), lax.axis_index("lon")
    lat_up, lat_down = ((a + 1) % 8, b), ((a + 7) % 8, b)
    lon_up, lon_down = (a, (b + 1) % 16), (a, (b + 15) % 16)
    loads = [
        pltpu.make_async_copy(pert_ref, blocks.at[pl.ds(0, 64)], load_sem.at[0]),
        pltpu.make_async_copy(sib_ref, blocks.at[pl.ds(64, 64)], load_sem.at[1]),
    ]
    for load in loads:
        load.start()
    greet([shifted(pos, axis, step) for axis in "xyz" for step in (1, 3)] + [lat_up, lat_down, lon_up, lon_down])
    deps[pl.ds(0, 64)] = dep_ref[...].astype(jnp.float32)
    deps[pl.ds(64, 64)] = sib_dep_ref[...].astype(jnp.float32)
    for load in loads:
        load.wait()

    sends = []
    flights = [[[None] * 6 for _ in range(n)] for _ in range(3)]

    def prefix(i, phase):
        return tuple(pos[axis] for axis in PARTS[i][2][:phase])

    def half(i, phase, target, upper):
        count = (2, 2, 2 * PARTS[i][0])[phase]
        return prefix(i, phase) + (target, pl.ds(count * upper, count))

    def start(i, phase, k, source, to_right):
        copy = pltpu.make_async_remote_copy(
            src_ref=source, dst_ref=bufs[phase][i][k],
            send_sem=send_sem.at[phase, i, k], recv_sem=recv_sem.at[phase, i, k],
            device_id=shifted(pos, PARTS[i][2][phase], 1 if to_right else 3), device_id_type=MESH)
        copy.start()
        sends.append(copy)
        flights[phase][i][k] = copy

    def coord(i, phase):
        return pos[PARTS[i][2][phase]]

    def send_far(i, phase):
        target = (coord(i, phase) + 2) % 4
        start(i, phase, 0, grams[i].at[half(i, phase, target, 0)], True)
        start(i, phase, 1, grams[i].at[half(i, phase, target, 1)], False)

    def send_right(i, phase):
        start(i, phase, 2, grams[i].at[half(i, phase, (coord(i, phase) + 1) % 4, 1)], True)

    def send_left(i, phase):
        start(i, phase, 3, grams[i].at[half(i, phase, (coord(i, phase) + 3) % 4, 0)], False)

    def each(i, phase, body):
        if phase == 0:
            def step(j, carry):
                body((j // 4, j % 4))
                return carry
            lax.fori_loop(0, 8, step, 0)
        elif phase == 1:
            def step(j, carry):
                body((j,))
                return carry
            lax.fori_loop(0, 2, step, 0)
        else:
            body(())

    def local_index(i, phase, target, upper, lead):
        if phase == 2:
            return half(i, phase, target, upper)
        return prefix(i, phase) + (target, 2 * upper + lead[0]) + lead[1:]

    def forward(i, phase):
        m = coord(i, phase)
        for k, (target, upper) in enumerate((((m + 1) % 4, 0), ((m + 3) % 4, 1))):
            flights[phase][i][k].wait_recv()
            got = bufs[phase][i][k]

            def body(lead, got=got, target=target, upper=upper):
                mine = grams[i][local_index(i, phase, target, upper, lead)]
                at = lead if lead else (slice(None),)
                got[at] = (got[at].astype(jnp.float32) + mine.astype(jnp.float32)).astype(got.dtype)
            each(i, phase, body)
            start(i, phase, 4 + k, got, k == 0)

    def finish(i, phase):
        m = coord(i, phase)
        for k in (2, 3, 4, 5):
            flights[phase][i][k].wait_recv()
        for upper, pair in enumerate(((4, 3), (2, 5))):
            f, g = (bufs[phase][i][k] for k in pair)

            def body(lead, f=f, g=g, upper=upper):
                index = local_index(i, phase, m, upper, lead)
                at = lead if lead else (slice(None),)
                total = grams[i][index].astype(jnp.float32) + f[at].astype(jnp.float32) + g[at].astype(jnp.float32)
                if phase < 2:
                    grams[i][index] = total.astype(grams[i].dtype)
                else:
                    fins[i][pl.ds(2 * PARTS[i][0] * upper, 2 * PARTS[i][0])] = total
            each(i, phase, body)

    def fill(count, place):
        def step(j, carry):
            off = place(j)
            fill_server(tuple((pos[axis] + o) % 4 for axis, o in zip("xyz", off)),
                        keys_ref, valid_ref, blocks, deps, grams)
            return carry
        lax.fori_loop(0, count, step, 0)

    fill(16, lambda j: (2, j // 4, j % 4))
    send_far(0, 0)
    fill(12, lambda j: (3 + j // 4, 2, j % 4))
    send_far(1, 0)
    fill(9, lambda j: (3 + j // 3, 3 + j % 3, 2))
    send_far(2, 0)
    send_far(3, 0)
    fill(9, lambda j: (1, 3 + j // 3, 3 + j % 3))
    send_right(0, 0)
    fill(9, lambda j: (3, 3 + j // 3, 3 + j % 3))
    send_left(0, 0)
    fill(9, lambda j: (0, 3 + j // 3, 3 + j % 3))
    for i in range(1, n):
        send_right(i, 0)
        send_left(i, 0)
    for phase in range(3):
        if phase > 0:
            for i in range(n):
                send_far(i, phase)
            for i in range(n):
                send_right(i, phase)
                send_left(i, phase)
        for i in range(n):
            forward(i, phase)
        for i in range(n):
            finish(i, phase)

    def solve(d, carry):
        g12 = jnp.concatenate([fins[0][pl.ds(d * 96, 96)], fins[1][pl.ds(d * 96, 32)]], axis=0)
        packed = jnp.concatenate([fins[1][pl.ds(d * 96 + 32, 64)], fins[2][pl.ds(d * 64, 64)]], axis=0)
        own[d] = weights_of(g12, packed, fins[3][pl.ds(d * 8, 8)], 256)
        return carry
    lax.fori_loop(0, 4, solve, 0)

    keep = pltpu.make_async_copy(own, near_ref.at[1, 1], own_sem)
    keep.start()

    def halo(k, source, dst, target):
        copy = pltpu.make_async_remote_copy(
            src_ref=source, dst_ref=dst, send_sem=halo_send.at[k], recv_sem=halo_recv.at[k],
            device_id=target, device_id_type=MESH)
        copy.start()
        sends.append(copy)
        return copy
    east = halo(0, own, near_ref.at[1, 0], lon_up)
    west = halo(1, own, near_ref.at[1, 2], lon_down)
    arriving = [halo(2, own, near_ref.at[0, 1], lat_up), halo(3, own, near_ref.at[2, 1], lat_down)]
    east.wait_recv()
    arriving += [halo(4, near_ref.at[1, 0], near_ref.at[0, 0], lat_up),
                 halo(5, near_ref.at[1, 0], near_ref.at[2, 0], lat_down)]
    west.wait_recv()
    arriving += [halo(6, near_ref.at[1, 2], near_ref.at[0, 2], lat_up),
                 halo(7, near_ref.at[1, 2], near_ref.at[2, 2], lat_down)]
    for copy in arriving:
        copy.wait_recv()
    for copy in sends:
        copy.wait_send()
    keep.wait()


def near_weights(keys, valid, pert, sib_pert, dep, sib_dep):
    n = len(PARTS)
    hbm = pl.BlockSpec(memory_space=pltpu.HBM)
    smem = pl.BlockSpec(memory_space=pltpu.SMEM)
    full = pl.BlockSpec(memory_space=pltpu.VMEM)

    def vmem(shape, kind):
        return pltpu.VMEM(shape, kind)
    scratch = [vmem((128, 128, 256), jnp.bfloat16), vmem((128, 128), jnp.float32)]
    scratch += [vmem((4, 4, 4, 4 * r, 128), t) for r, t, _ in PARTS]
    for phase in range(3):
        for r, t, _ in PARTS:
            shape = ((2, 4, 4 * r, 128), (2, 4 * r, 128), (2 * r, 128))[phase]
            scratch += [vmem(shape, t)] * 6
    scratch += [vmem((4 * r, 128), jnp.float32) for r, _, _ in PARTS]
    scratch += [
        vmem((4, 256, 256), jnp.bfloat16),
        pltpu.SemaphoreType.DMA((3, n, 6)),
        pltpu.SemaphoreType.DMA((3, n, 6)),
        pltpu.SemaphoreType.DMA((2,)),
        pltpu.SemaphoreType.DMA((8,)),
        pltpu.SemaphoreType.DMA((8,)),
        pltpu.SemaphoreType.DMA(()),
    ]
    return pl.pallas_call(
        reduce_kernel,
        out_shape=jax.ShapeDtypeStruct((3, 3, 4, 256, 256), jnp.bfloat16),
        in_specs=[smem, smem, hbm, hbm, full, full],
        out_specs=hbm,
        scratch_shapes=scratch,
        compiler_params=pltpu.CompilerParams(
            collective_id=1, has_side_effects=True, vmem_limit_bytes=58 << 20),
        name="reduce",
    )(keys, valid, pert, sib_pert, dep, sib_dep)


STEP_TILES = 4


def interp_kernel(pos_ref, pert_ref, mean_ref, coef_ref, near_ref, out_ref):
    step = pl.program_id(0)
    mean_cols = mean_ref[...].T
    coef = coef_ref[...]
    coef_cols = jnp.concatenate([coef, coef], axis=0).T
    for tile in range(STEP_TILES):
        span = pl.ds(tile * 32, 32)
        held = pert_ref[:, span, :].reshape(256, 256)
        total = None
        for corner in range(4):
            where = pos_ref[(step * STEP_TILES + tile) * 4 + corner]
            prod = jnp.dot(held, near_ref[where], preferred_element_type=jnp.float32)
            factor = coef_cols[tile * 32:tile * 32 + 32, corner:corner + 1]
            term = prod.reshape(8, 32, 256) * factor[None]
            total = term if total is None else total + term
        for level in range(8):
            base = mean_cols[tile * 32:tile * 32 + 32, level:level + 1]
            out_ref[level, span, :] = (total[level] + base).astype(jnp.bfloat16)


def interpolate(position, pert, mean, coef, near):
    cols = STEP_TILES * 32
    steps = pert.shape[1] // cols
    return pl.pallas_call(
        interp_kernel,
        out_shape=jax.ShapeDtypeStruct(pert.shape, jnp.bfloat16),
        grid_spec=pltpu.PrefetchScalarGridSpec(
            num_scalar_prefetch=1,
            grid=(steps,),
            in_specs=[
                pl.BlockSpec((8, cols, 256), lambda i, *_: (0, i, 0)),
                pl.BlockSpec((8, cols), lambda i, *_: (0, i)),
                pl.BlockSpec((4, cols), lambda i, *_: (0, i)),
                pl.BlockSpec((36, 256, 256), lambda i, *_: (0, 0, 0), pipeline_mode=pl.Buffered(1)),
            ],
            out_specs=pl.BlockSpec((8, cols, 256), lambda i, *_: (0, i, 0)),
        ),
        compiler_params=pltpu.CompilerParams(
            dimension_semantics=("arbitrary",), vmem_limit_bytes=58 << 20),
        name="interp",
    )(position, pert, mean, coef, near)


def local(
    obs_pert, obs_dep, valid_rows, local_lists, state_mean, state_pert, interp_lists, interp_coef
):
    n_lon = lax.axis_size("lon")
    domains_here = local_lists.shape[0]
    tile = jnp.concatenate([
        jnp.pad(local_lists, ((0, 0), (0, 128 - local_lists.shape[1])), constant_values=-1),
        jnp.pad(valid_rows[None, :], ((0, 3), (0, 64))),
    ], axis=0)
    keys, sib_tile, sib_pert, sib_dep = gather_lists(tile, obs_pert, obs_dep)
    keys = keys[:, 0, :4].reshape(-1)
    valid = jnp.concatenate([valid_rows, sib_tile[4, :64]])
    near = near_weights(keys, valid, obs_pert, sib_pert, obs_dep, sib_dep)
    owner = interp_lists // domains_here
    within = interp_lists % domains_here
    lat_step = owner // n_lon - lax.axis_index("lat")
    lon_step = (owner % n_lon - lax.axis_index("lon") + 1) % n_lon - 1
    position = ((lat_step + 1) * 3 + lon_step + 1) * domains_here + within
    return interpolate(position.reshape(-1), state_pert, state_mean, interp_coef, near.reshape(36, 256, 256))


def solution(mesh):
    in_specs = (
        P(("lat", "lon"), None, None),
        P(("lat", "lon"), None),
        P(("lat", "lon")),
        P(("lat", "lon"), None),
        P(None, ("lat", "lon")),
        P(None, ("lat", "lon"), None),
        P(("lat", "lon"), None),
        P(None, ("lat", "lon")),
    )
    out_specs = P(None, ("lat", "lon"), None)
    return jax.shard_map(local, mesh=mesh, in_specs=in_specs, out_specs=out_specs, check_vma=False)
```

```python
import functools

import jax
import jax.numpy as jnp
from jax import lax
from jax.experimental import pallas as pl
from jax.experimental.pallas import tpu as pltpu
from jax.sharding import PartitionSpec as P

NS_ITERS = 4
MESH = pl.DeviceIdType.MESH
BIG = 1 << 20
PARTS = ((96, jnp.bfloat16, "xyz"), (96, jnp.bfloat16, "yzx"), (64, jnp.bfloat16, "zxy"), (8, jnp.float32, "zxy"))


def coords():
    a = lax.axis_index("lat")
    b = lax.axis_index("lon")
    return {"y": a // 2, "c": a % 2, "x": b // 4, "z": b % 4}


def device(pos):
    return (pos["y"] * 2 + pos["c"], pos["x"] * 4 + pos["z"])


def shifted(pos, axis, step):
    size = 2 if axis == "c" else 4
    return device({**pos, axis: (pos[axis] + step) % size})


def greet(peers):
    barrier = pltpu.get_barrier_semaphore()
    for peer in peers:
        pl.semaphore_signal(barrier, inc=1, device_id=peer, device_id_type=MESH)
    pl.semaphore_wait(barrier, len(peers))


def lists_kernel(tile_ref, pert_ref, dep_ref, keys_ref, sib_tile_ref, sib_pert_ref, sib_dep_ref,
                 held, send_sem, recv_sem, sib_send, sib_recv):
    pos = coords()
    x, y, z = pos["x"], pos["y"], pos["z"]
    sibling = shifted(pos, "c", 1)
    greet([shifted(pos, axis, step) for axis in "zxy" for step in (1, 2, 3)] + [sibling])
    swaps = []
    for k, (src, dst) in enumerate(((pert_ref, sib_pert_ref), (dep_ref, sib_dep_ref), (tile_ref, sib_tile_ref))):
        swap = pltpu.make_async_remote_copy(
            src_ref=src, dst_ref=dst, send_sem=sib_send.at[k], recv_sem=sib_recv.at[k],
            device_id=sibling, device_id_type=MESH)
        swap.start()
        swaps.append(swap)
    held[y, x, z] = tile_ref[...]
    sent = []
    for phase, axis in enumerate("zxy"):
        view = held.at[y, x, z] if axis == "z" else (held.at[y, x] if axis == "x" else held.at[y])
        copies = []
        for step in (1, 2, 3):
            copy = pltpu.make_async_remote_copy(
                src_ref=view, dst_ref=view, send_sem=send_sem.at[phase, step - 1],
                recv_sem=recv_sem.at[phase, step - 1],
                device_id=shifted(pos, axis, step), device_id_type=MESH)
            copy.start()
            copies.append(copy)
        for copy in copies:
            copy.wait_recv()
        sent += copies
    me = device(pos)
    own = me[0] * 16 + me[1]
    other = sibling[0] * 16 + sibling[1]
    entry = held[...].reshape(64, 8, 128)
    lane = lax.broadcasted_iota(jnp.int32, (64, 8, 128), 2)
    row = lax.broadcasted_iota(jnp.int32, (64, 8, 128), 1)
    owner = entry >> 6
    local_index = entry & 63
    block = jnp.where(owner == own, local_index, local_index + 64)
    value = jnp.where(((owner == own) | (owner == other)) & (row < 4), row * 4096 + lane * 128 + block, BIG)
    out = jnp.full((64, 8, 128), BIG, jnp.int32)
    for k in range(4):
        least = jnp.min(jnp.min(value, axis=2, keepdims=True), axis=1, keepdims=True)
        out = jnp.where(lane == k, least, out)
        value = jnp.where(value > least, value, BIG)
    keys_ref[...] = out
    for copy in sent:
        copy.wait_send()
    for swap in swaps:
        swap.wait()


def gather_lists(tile, pert, dep):
    any_spec = pl.BlockSpec(memory_space=pltpu.HBM)
    vmem = pl.BlockSpec(memory_space=pltpu.VMEM)
    return pl.pallas_call(
        lists_kernel,
        out_shape=(
            jax.ShapeDtypeStruct((64, 8, 128), jnp.int32),
            jax.ShapeDtypeStruct((8, 128), jnp.int32),
            jax.ShapeDtypeStruct(pert.shape, pert.dtype),
            jax.ShapeDtypeStruct(dep.shape, dep.dtype),
        ),
        in_specs=[vmem, any_spec, any_spec],
        out_specs=(vmem, vmem, any_spec, any_spec),
        scratch_shapes=[
            pltpu.VMEM((4, 4, 4, 8, 128), jnp.int32),
            pltpu.SemaphoreType.DMA((3, 3)),
            pltpu.SemaphoreType.DMA((3, 3)),
            pltpu.SemaphoreType.DMA((3,)),
            pltpu.SemaphoreType.DMA((3,)),
        ],
        compiler_params=pltpu.CompilerParams(collective_id=0, has_side_effects=True),
        name="lists",
    )(tile, pert, dep)


def split(value):
    high = value.astype(jnp.bfloat16)
    return high, (value - high.astype(jnp.float32)).astype(jnp.bfloat16)


def product(left, right):
    (lh, ll), (rh, rl) = left, right
    dot = functools.partial(jnp.dot, preferred_element_type=jnp.float32)
    return dot(lh, rh) + (dot(lh, rl) + dot(ll, rh))


def packed_weights(domains, members):
    half = members // 2
    row = lax.broadcasted_iota(jnp.int32, (half, half), 0)
    col = lax.broadcasted_iota(jnp.int32, (half, half), 1)
    wide_row = lax.broadcasted_iota(jnp.int32, (members, members), 0)
    wide_col = lax.broadcasted_iota(jnp.int32, (members, members), 1)
    identity = jnp.where(wide_row == wide_col, 1.0, 0.0).astype(jnp.float32)
    scales, approxes = [], []
    for g12, packed, extra in domains:
        turned = packed.T
        g11 = jnp.where(col > row, packed, turned)
        g22 = jnp.where(col < row, packed, turned)
        g11 = jnp.where(col == row, extra[0:1], g11)
        g22 = jnp.where(col == row, extra[1:2], g22)
        gram = jnp.concatenate(
            [jnp.concatenate([g11, g12], axis=1), jnp.concatenate([g12.T, g22], axis=1)], axis=0)
        system = (members - 1.0) * identity + gram
        scale = jnp.sqrt(jnp.sum(jnp.sum(system * system, axis=0, keepdims=True), axis=1, keepdims=True))
        scales.append(scale)
        approxes.append(system / scale)
    roots = [1.5 * identity - 0.5 * approx for approx in approxes]
    approxes = [product(split(approx), split(root)) for approx, root in zip(approxes, roots)]
    for sweep in range(1, NS_ITERS):
        root_parts = [split(root) for root in roots]
        factors = [split(1.5 * identity - 0.5 * product(parts, split(approx)))
                   for parts, approx in zip(root_parts, approxes)]
        if sweep < NS_ITERS - 1:
            approxes = [product(split(approx), factor) for approx, factor in zip(approxes, factors)]
        roots = [product(factor, parts) for factor, parts in zip(factors, root_parts)]
    root_parts = [split(root) for root in roots]
    innovs = [jnp.broadcast_to(jnp.concatenate([extra[2:3], extra[3:4]], axis=1), (8, members)) for _, _, extra in domains]
    inners = [product(split(innov), parts) for innov, parts in zip(innovs, root_parts)]
    means = [product(split(inner), parts) / scale for inner, parts, scale in zip(inners, root_parts, scales)]
    results = []
    for root, mean, scale in zip(roots, means, scales):
        root = jnp.sqrt((members - 1.0) / scale) * root
        t11, t12, t22 = root[:half, :half], root[:half, half:], root[half:, half:]
        d2 = jnp.sum(jnp.where(col == row, t22, 0.0), axis=0, keepdims=True)
        high = mean[:1].astype(jnp.bfloat16).astype(jnp.float32)
        low = mean[:1] - high
        rest = jnp.concatenate(
            [d2, high[:, :half], low[:, :half], high[:, half:], low[:, half:], jnp.zeros((11, half), jnp.float32)], axis=0)
        results.append((t12.astype(jnp.bfloat16), jnp.where(col >= row, t11, t22).astype(jnp.bfloat16),
                        rest.astype(jnp.bfloat16)))
    return results


def fill_server(place, keys_ref, valid_ref, blocks, deps, grams):
    px, py, pz = place
    base = ((py * 4 + px) * 4 + pz) * 4
    rows = lax.broadcasted_iota(jnp.int32, (128, 256), 0)
    row8 = lax.broadcasted_iota(jnp.int32, (8, 128), 0)
    tri_row = lax.broadcasted_iota(jnp.int32, (128, 128), 0)
    tri_col = lax.broadcasted_iota(jnp.int32, (128, 128), 1)
    held, turned, doms, departs = [], [], [], []
    for j in range(4):
        key = keys_ref[base + j]
        block = key & 127
        dom = key >> 12
        count = jnp.where(key < BIG, valid_ref[block], 0)
        values = jnp.where(rows < count, blocks[block], jnp.zeros((), jnp.bfloat16))
        held.append(values)
        turned.append(values.T)
        doms.append(dom)
        depart = jnp.broadcast_to(deps[pl.ds(block, 1), :], (8, 128))
        departs.append(jnp.where(row8 == dom, depart, 0.0).astype(jnp.bfloat16))
    stacked = jnp.concatenate(held, axis=0)
    inn = jnp.dot(jnp.concatenate(departs, axis=1), stacked, preferred_element_type=jnp.float32)
    for d in range(4):
        left = jnp.concatenate(
            [jnp.where(doms[j] == d, turned[j], jnp.zeros((), jnp.bfloat16)) for j in range(4)], axis=1)
        gram = jnp.dot(left, stacked, preferred_element_type=jnp.float32)
        g11, g12, g22 = gram[:128, :128], gram[:128, 128:], gram[128:, 128:]
        packed = jnp.where(tri_col >= tri_row, g11, g22).astype(jnp.bfloat16)
        g12 = g12.astype(jnp.bfloat16)
        d1 = jnp.sum(jnp.where(tri_col == tri_row, g11, 0.0), axis=0, keepdims=True)
        d2 = jnp.sum(jnp.where(tri_col == tri_row, g22, 0.0), axis=0, keepdims=True)
        grams[0][px, py, pz, pl.ds(d * 96, 96)] = g12[:96]
        grams[1][py, pz, px, pl.ds(d * 96, 32)] = g12[96:]
        grams[1][py, pz, px, pl.ds(d * 96 + 32, 64)] = packed[:64]
        grams[2][pz, px, py, pl.ds(d * 64, 64)] = packed[64:]
        grams[3][pz, px, py, pl.ds(d * 8, 8)] = jnp.concatenate(
            [d1, d2, inn[d:d + 1, :128], inn[d:d + 1, 128:], jnp.zeros((4, 128), jnp.float32)], axis=0)


def reduce_kernel(keys_ref, valid_ref, pert_ref, sib_ref, dep_ref, sib_dep_ref, near_ref, *scratch):
    n = len(PARTS)
    scratch = list(scratch)

    def take(count):
        taken, scratch[:count] = scratch[:count], []
        return taken
    blocks, deps = take(2)
    grams = take(n)
    bufs = [[take(6) for _ in range(n)] for _ in range(3)]
    fins = take(n)
    own, send_sem, recv_sem, load_sem, halo_send, halo_recv, own_sem = scratch

    pos = coords()
    a, b = lax.axis_index("lat"), lax.axis_index("lon")
    lat_up, lat_down = ((a + 1) % 8, b), ((a + 7) % 8, b)
    lon_up, lon_down = (a, (b + 1) % 16), (a, (b + 15) % 16)
    loads = [
        pltpu.make_async_copy(pert_ref, blocks.at[pl.ds(0, 64)], load_sem.at[0]),
        pltpu.make_async_copy(sib_ref, blocks.at[pl.ds(64, 64)], load_sem.at[1]),
    ]
    for load in loads:
        load.start()
    greet([shifted(pos, axis, step) for axis in "xyz" for step in (1, 3)] + [lat_up, lat_down, lon_up, lon_down])
    deps[pl.ds(0, 64)] = dep_ref[...].astype(jnp.float32)
    deps[pl.ds(64, 64)] = sib_dep_ref[...].astype(jnp.float32)
    for load in loads:
        load.wait()

    sends = []
    flights = [[[None] * 6 for _ in range(n)] for _ in range(3)]

    def prefix(i, phase):
        return tuple(pos[axis] for axis in PARTS[i][2][:phase])

    def half(i, phase, target, upper):
        count = (2, 2, 2 * PARTS[i][0])[phase]
        return prefix(i, phase) + (target, pl.ds(count * upper, count))

    def start(i, phase, k, source, to_right):
        copy = pltpu.make_async_remote_copy(
            src_ref=source, dst_ref=bufs[phase][i][k],
            send_sem=send_sem.at[phase, i, k], recv_sem=recv_sem.at[phase, i, k],
            device_id=shifted(pos, PARTS[i][2][phase], 1 if to_right else 3), device_id_type=MESH)
        copy.start()
        sends.append(copy)
        flights[phase][i][k] = copy

    def coord(i, phase):
        return pos[PARTS[i][2][phase]]

    def send_far(i, phase):
        target = (coord(i, phase) + 2) % 4
        start(i, phase, 0, grams[i].at[half(i, phase, target, 0)], True)
        start(i, phase, 1, grams[i].at[half(i, phase, target, 1)], False)

    def send_right(i, phase):
        start(i, phase, 2, grams[i].at[half(i, phase, (coord(i, phase) + 1) % 4, 1)], True)

    def send_left(i, phase):
        start(i, phase, 3, grams[i].at[half(i, phase, (coord(i, phase) + 3) % 4, 0)], False)

    def each(i, phase, body):
        if phase == 0:
            def step(j, carry):
                body((j // 4, j % 4))
                return carry
            lax.fori_loop(0, 8, step, 0)
        elif phase == 1:
            def step(j, carry):
                body((j,))
                return carry
            lax.fori_loop(0, 2, step, 0)
        else:
            body(())

    def local_index(i, phase, target, upper, lead):
        if phase == 2:
            return half(i, phase, target, upper)
        return prefix(i, phase) + (target, 2 * upper + lead[0]) + lead[1:]

    def forward(i, phase):
        m = coord(i, phase)
        for k, (target, upper) in enumerate((((m + 1) % 4, 0), ((m + 3) % 4, 1))):
            flights[phase][i][k].wait_recv()
            got = bufs[phase][i][k]

            def body(lead, got=got, target=target, upper=upper):
                mine = grams[i][local_index(i, phase, target, upper, lead)]
                at = lead if lead else (slice(None),)
                got[at] = (got[at].astype(jnp.float32) + mine.astype(jnp.float32)).astype(got.dtype)
            each(i, phase, body)
            start(i, phase, 4 + k, got, k == 0)

    def finish(i, phase):
        m = coord(i, phase)
        for k in (2, 3, 4, 5):
            flights[phase][i][k].wait_recv()
        for upper, pair in enumerate(((4, 3), (2, 5))):
            f, g = (bufs[phase][i][k] for k in pair)

            def body(lead, f=f, g=g, upper=upper):
                index = local_index(i, phase, m, upper, lead)
                at = lead if lead else (slice(None),)
                total = grams[i][index].astype(jnp.float32) + f[at].astype(jnp.float32) + g[at].astype(jnp.float32)
                if phase < 2:
                    grams[i][index] = total.astype(grams[i].dtype)
                else:
                    fins[i][pl.ds(2 * PARTS[i][0] * upper, 2 * PARTS[i][0])] = total
            each(i, phase, body)

    def fill(count, place):
        def step(j, carry):
            off = place(j)
            fill_server(tuple((pos[axis] + o) % 4 for axis, o in zip("xyz", off)),
                        keys_ref, valid_ref, blocks, deps, grams)
            return carry
        lax.fori_loop(0, count, step, 0)

    fill(16, lambda j: (2, j // 4, j % 4))
    send_far(0, 0)
    fill(12, lambda j: (3 + j // 4, 2, j % 4))
    send_far(1, 0)
    fill(9, lambda j: (3 + j // 3, 3 + j % 3, 2))
    send_far(2, 0)
    send_far(3, 0)
    fill(9, lambda j: (1, 3 + j // 3, 3 + j % 3))
    send_right(0, 0)
    fill(9, lambda j: (3, 3 + j // 3, 3 + j % 3))
    send_left(0, 0)
    fill(9, lambda j: (0, 3 + j // 3, 3 + j % 3))
    for i in range(1, n):
        send_right(i, 0)
        send_left(i, 0)
    for phase in range(3):
        if phase > 0:
            for i in range(n):
                send_far(i, phase)
            for i in range(n):
                send_right(i, phase)
                send_left(i, phase)
        for i in range(n):
            forward(i, phase)
        for i in range(n):
            finish(i, phase)

    def solve(pair):
        domains = []
        for d in pair:
            g12 = jnp.concatenate([fins[0][pl.ds(d * 96, 96)], fins[1][pl.ds(d * 96, 32)]], axis=0)
            packed = jnp.concatenate([fins[1][pl.ds(d * 96 + 32, 64)], fins[2][pl.ds(d * 64, 64)]], axis=0)
            domains.append((g12, packed, fins[3][pl.ds(d * 8, 8)]))
        for d, (t12, triangles, rest) in zip(pair, packed_weights(domains, 256)):
            own[d, pl.ds(0, 128)] = t12
            own[d, pl.ds(128, 128)] = triangles
            own[d, pl.ds(256, 16)] = rest

    def halo(chunk, k, source, to, target):
        copy = pltpu.make_async_remote_copy(
            src_ref=source, dst_ref=near_ref.at[to + (pl.ds(2 * chunk, 2),)],
            send_sem=halo_send.at[chunk, k], recv_sem=halo_recv.at[chunk, k],
            device_id=target, device_id_type=MESH)
        copy.start()
        sends.append(copy)
        return copy

    keeps, sides, arriving = [], [], []
    for chunk in range(2):
        solve((2 * chunk, 2 * chunk + 1))
        mine = own.at[pl.ds(2 * chunk, 2)]
        sides.append((halo(chunk, 0, mine, (1, 0), lon_up), halo(chunk, 1, mine, (1, 2), lon_down)))
        arriving += [halo(chunk, 2, mine, (0, 1), lat_up), halo(chunk, 3, mine, (2, 1), lat_down)]
        keep = pltpu.make_async_copy(mine, near_ref.at[1, 1, pl.ds(2 * chunk, 2)], own_sem.at[chunk])
        keep.start()
        keeps.append(keep)
    for chunk in range(2):
        for side, column in enumerate((0, 2)):
            sides[chunk][side].wait_recv()
            held = near_ref.at[1, column, pl.ds(2 * chunk, 2)]
            arriving += [halo(chunk, 4 + 2 * side, held, (0, column), lat_up),
                         halo(chunk, 5 + 2 * side, held, (2, column), lat_down)]
    for copy in arriving:
        copy.wait_recv()
    for copy in sends:
        copy.wait_send()
    for keep in keeps:
        keep.wait()


def near_weights(keys, valid, pert, sib_pert, dep, sib_dep):
    n = len(PARTS)
    hbm = pl.BlockSpec(memory_space=pltpu.HBM)
    smem = pl.BlockSpec(memory_space=pltpu.SMEM)
    full = pl.BlockSpec(memory_space=pltpu.VMEM)

    def vmem(shape, kind):
        return pltpu.VMEM(shape, kind)
    scratch = [vmem((128, 128, 256), jnp.bfloat16), vmem((128, 128), jnp.float32)]
    scratch += [vmem((4, 4, 4, 4 * r, 128), t) for r, t, _ in PARTS]
    for phase in range(3):
        for r, t, _ in PARTS:
            shape = ((2, 4, 4 * r, 128), (2, 4 * r, 128), (2 * r, 128))[phase]
            scratch += [vmem(shape, t)] * 6
    scratch += [vmem((4 * r, 128), jnp.float32) for r, _, _ in PARTS]
    scratch += [
        vmem((4, 272, 128), jnp.bfloat16),
        pltpu.SemaphoreType.DMA((3, n, 6)),
        pltpu.SemaphoreType.DMA((3, n, 6)),
        pltpu.SemaphoreType.DMA((2,)),
        pltpu.SemaphoreType.DMA((2, 8)),
        pltpu.SemaphoreType.DMA((2, 8)),
        pltpu.SemaphoreType.DMA((2,)),
    ]
    return pl.pallas_call(
        reduce_kernel,
        out_shape=jax.ShapeDtypeStruct((3, 3, 4, 272, 128), jnp.bfloat16),
        in_specs=[smem, smem, hbm, hbm, full, full],
        out_specs=hbm,
        scratch_shapes=scratch,
        compiler_params=pltpu.CompilerParams(
            collective_id=1, has_side_effects=True, vmem_limit_bytes=58 << 20),
        name="reduce",
    )(keys, valid, pert, sib_pert, dep, sib_dep)


STEP_TILES = 4


def interp_kernel(pos_ref, pert_ref, mean_ref, coef_ref, near_ref, out_ref, tiles):
    step = pl.program_id(0)

    @pl.when(step == 0)
    def _():
        row = lax.broadcasted_iota(jnp.int32, (128, 128), 0)
        col = lax.broadcasted_iota(jnp.int32, (128, 128), 1)

        def unpack(k, carry):
            t12 = near_ref[k, pl.ds(0, 128)]
            packed = near_ref[k, pl.ds(128, 128)]
            rest = near_ref[k, pl.ds(256, 16)].astype(jnp.float32)
            columns = rest.T
            first = columns[:, 1:2] + columns[:, 2:3]
            second = columns[:, 3:4] + columns[:, 4:5]
            packed = packed.astype(jnp.float32)
            turned = packed.T
            t11 = jnp.where(col >= row, packed, turned)
            t22 = jnp.where(col < row, packed, jnp.where(col == row, rest[0:1], turned))
            wide = t12.astype(jnp.float32)
            tiles[k, pl.ds(0, 128), pl.ds(0, 128)] = (t11 + first).astype(jnp.bfloat16)
            tiles[k, pl.ds(0, 128), pl.ds(128, 128)] = (wide + first).astype(jnp.bfloat16)
            tiles[k, pl.ds(128, 128), pl.ds(0, 128)] = (wide.T + second).astype(jnp.bfloat16)
            tiles[k, pl.ds(128, 128), pl.ds(128, 128)] = (t22 + second).astype(jnp.bfloat16)
            return carry
        lax.fori_loop(0, 36, unpack, 0)

    mean_cols = mean_ref[...].T
    coef = coef_ref[...]
    coef_cols = jnp.concatenate([coef, coef], axis=0).T
    for tile in range(STEP_TILES):
        span = pl.ds(tile * 32, 32)
        held = pert_ref[:, span, :].astype(jnp.float32)
        lefts, rights = [], []
        for corner in range(4):
            factor = coef_cols[tile * 32:tile * 32 + 32, corner:corner + 1]
            lefts.append((held * factor[None]).astype(jnp.bfloat16).reshape(256, 256))
            rights.append(tiles[pos_ref[(step * STEP_TILES + tile) * 4 + corner]])
        total = jnp.dot(jnp.concatenate(lefts, axis=1), jnp.concatenate(rights, axis=0),
                        preferred_element_type=jnp.float32).reshape(8, 32, 256)
        for level in range(8):
            base = mean_cols[tile * 32:tile * 32 + 32, level:level + 1]
            out_ref[level, span, :] = (total[level] + base).astype(jnp.bfloat16)


def interpolate(position, pert, mean, coef, near):
    cols = STEP_TILES * 32
    steps = pert.shape[1] // cols
    return pl.pallas_call(
        interp_kernel,
        out_shape=jax.ShapeDtypeStruct(pert.shape, jnp.bfloat16),
        grid_spec=pltpu.PrefetchScalarGridSpec(
            num_scalar_prefetch=1,
            grid=(steps,),
            in_specs=[
                pl.BlockSpec((8, cols, 256), lambda i, *_: (0, i, 0)),
                pl.BlockSpec((8, cols), lambda i, *_: (0, i)),
                pl.BlockSpec((4, cols), lambda i, *_: (0, i)),
                pl.BlockSpec((36, 272, 128), lambda i, *_: (0, 0, 0), pipeline_mode=pl.Buffered(1)),
            ],
            out_specs=pl.BlockSpec((8, cols, 256), lambda i, *_: (0, i, 0)),
            scratch_shapes=[pltpu.VMEM((36, 256, 256), jnp.bfloat16)],
        ),
        compiler_params=pltpu.CompilerParams(
            dimension_semantics=("arbitrary",), vmem_limit_bytes=58 << 20),
        name="interp",
    )(position, pert, mean, coef, near)


def local(
    obs_pert, obs_dep, valid_rows, local_lists, state_mean, state_pert, interp_lists, interp_coef
):
    n_lon = lax.axis_size("lon")
    domains_here = local_lists.shape[0]
    tile = jnp.concatenate([
        jnp.pad(local_lists, ((0, 0), (0, 128 - local_lists.shape[1])), constant_values=-1),
        jnp.pad(valid_rows[None, :], ((0, 3), (0, 64))),
    ], axis=0)
    keys, sib_tile, sib_pert, sib_dep = gather_lists(tile, obs_pert, obs_dep)
    keys = keys[:, 0, :4].reshape(-1)
    valid = jnp.concatenate([valid_rows, sib_tile[4, :64]])
    near = near_weights(keys, valid, obs_pert, sib_pert, obs_dep, sib_dep)
    owner = interp_lists // domains_here
    within = interp_lists % domains_here
    lat_step = owner // n_lon - lax.axis_index("lat")
    lon_step = (owner % n_lon - lax.axis_index("lon") + 1) % n_lon - 1
    position = ((lat_step + 1) * 3 + lon_step + 1) * domains_here + within
    return interpolate(position.reshape(-1), state_pert, state_mean, interp_coef, near.reshape(36, 272, 128))


def solution(mesh):
    in_specs = (
        P(("lat", "lon"), None, None),
        P(("lat", "lon"), None),
        P(("lat", "lon")),
        P(("lat", "lon"), None),
        P(None, ("lat", "lon")),
        P(None, ("lat", "lon"), None),
        P(("lat", "lon"), None),
        P(None, ("lat", "lon")),
    )
    out_specs = P(None, ("lat", "lon"), None)
    return jax.shard_map(local, mesh=mesh, in_specs=in_specs, out_specs=out_specs, check_vma=False)
```

```python
import functools

import jax
import jax.numpy as jnp
from jax import lax
from jax.experimental import pallas as pl
from jax.experimental.pallas import tpu as pltpu
from jax.sharding import PartitionSpec as P

NS_ITERS = 4
MESH = pl.DeviceIdType.MESH
BIG = 1 << 20
PARTS = ((400, jnp.bfloat16, "xyz"), (352, jnp.bfloat16, "yzx"), (272, jnp.bfloat16, "zxy"), (16, jnp.float32, "zxy"))
STARTS = (0, 400, 752)


def coords():
    a = lax.axis_index("lat")
    b = lax.axis_index("lon")
    return {"y": a // 2, "c": a % 2, "x": b // 4, "z": b % 4}


def device(pos):
    return (pos["y"] * 2 + pos["c"], pos["x"] * 4 + pos["z"])


def shifted(pos, axis, step):
    size = 2 if axis == "c" else 4
    return device({**pos, axis: (pos[axis] + step) % size})


def greet(peers):
    barrier = pltpu.get_barrier_semaphore()
    for peer in peers:
        pl.semaphore_signal(barrier, inc=1, device_id=peer, device_id_type=MESH)
    pl.semaphore_wait(barrier, len(peers))


def split(value):
    high = value.astype(jnp.bfloat16)
    return high, (value - high.astype(jnp.float32)).astype(jnp.bfloat16)


def product(left, right):
    (lh, ll), (rh, rl) = left, right
    dot = functools.partial(jnp.dot, preferred_element_type=jnp.float32)
    return dot(lh, rh) + (dot(lh, rl) + dot(ll, rh))


def packed_weights(domains, members, between):
    half = members // 2
    row = lax.broadcasted_iota(jnp.int32, (half, half), 0)
    col = lax.broadcasted_iota(jnp.int32, (half, half), 1)
    wide_row = lax.broadcasted_iota(jnp.int32, (members, members), 0)
    wide_col = lax.broadcasted_iota(jnp.int32, (members, members), 1)
    identity = jnp.where(wide_row == wide_col, 1.0, 0.0).astype(jnp.float32)
    scales, approxes = [], []
    for g12, packed, extra in domains:
        turned = packed.T
        g11 = jnp.where(col > row, packed, turned)
        g22 = jnp.where(col < row, packed, turned)
        g11 = jnp.where(col == row, extra[0:1], g11)
        g22 = jnp.where(col == row, extra[1:2], g22)
        gram = jnp.concatenate(
            [jnp.concatenate([g11, g12], axis=1), jnp.concatenate([g12.T, g22], axis=1)], axis=0)
        system = (members - 1.0) * identity + gram
        scale = jnp.sqrt(jnp.sum(jnp.sum(system * system, axis=0, keepdims=True), axis=1, keepdims=True))
        scales.append(scale)
        approxes.append(system / scale)
    roots = [1.5 * identity - 0.5 * approx for approx in approxes]
    approxes = [product(split(approx), split(root)) for approx, root in zip(approxes, roots)]
    for sweep in range(1, NS_ITERS):
        root_parts = [split(root) for root in roots]
        factors = [split(1.5 * identity - 0.5 * product(parts, split(approx)))
                   for parts, approx in zip(root_parts, approxes)]
        if sweep < NS_ITERS - 1:
            approxes = [product(split(approx), factor) for approx, factor in zip(approxes, factors)]
        roots = [product(factor, parts) for factor, parts in zip(factors, root_parts)]
        if sweep == 2:
            between()
    root_parts = [split(root) for root in roots]
    innovs = [jnp.broadcast_to(jnp.concatenate([extra[2:3], extra[3:4]], axis=1), (8, members)) for _, _, extra in domains]
    inners = [product(split(innov), parts) for innov, parts in zip(innovs, root_parts)]
    means = [product(split(inner), parts) / scale for inner, parts, scale in zip(inners, root_parts, scales)]
    results = []
    for root, mean, scale in zip(roots, means, scales):
        root = jnp.sqrt((members - 1.0) / scale) * root
        t11, t12, t22 = root[:half, :half], root[:half, half:], root[half:, half:]
        exact = [jnp.sum(jnp.where(col == row, t, 0.0), axis=0, keepdims=True) for t in (t11, t22)]
        exact += [mean[:1, :half], mean[:1, half:]]
        highs = [value.astype(jnp.bfloat16).astype(jnp.float32) for value in exact]
        lows = [value - high for value, high in zip(exact, highs)]
        rest = jnp.concatenate(highs + lows + [jnp.zeros((8, half), jnp.float32)], axis=0)
        results.append((t12.astype(jnp.bfloat16), jnp.where(col >= row, t11, t22).astype(jnp.bfloat16),
                        rest.astype(jnp.bfloat16)))
    return results


def store_rows(refs, index, first, value):
    count = value.shape[0]
    for i, start in enumerate(STARTS):
        low, high = max(first, start), min(first + count, start + PARTS[i][0])
        if low < high:
            refs[i][index[i] + (pl.ds(low - start, high - low),)] = value[low - first:high - first]


def fill_server(place, keys_ref, valid_ref, blocks, deps, grams):
    px, py, pz = place
    server = (py * 4 + px) * 4 + pz
    index = ((px, py, pz), (py, pz, px), (pz, px, py))
    rows = lax.broadcasted_iota(jnp.int32, (128, 256), 0)
    row8 = lax.broadcasted_iota(jnp.int32, (8, 128), 0)
    tri_row = lax.broadcasted_iota(jnp.int32, (128, 128), 0)
    tri_col = lax.broadcasted_iota(jnp.int32, (128, 128), 1)
    held, turned, doms, departs = [], [], [], []
    for j in range(4):
        key = keys_ref[server, j]
        block = key & 127
        dom = key >> 12
        count = jnp.where(key < BIG, valid_ref[block >> 6, 4, block & 63], 0)
        values = jnp.where(rows < count, blocks[block], jnp.zeros((), jnp.bfloat16))
        held.append(values)
        turned.append(values.T)
        doms.append(dom)
        depart = jnp.broadcast_to(deps[pl.ds(block, 1), :], (8, 128))
        departs.append(jnp.where(row8 == dom, depart, 0.0).astype(jnp.bfloat16))
    stacked = jnp.concatenate(held, axis=0)
    inn = jnp.dot(jnp.concatenate(departs, axis=1), stacked, preferred_element_type=jnp.float32)
    for d in range(4):
        left = jnp.concatenate(
            [jnp.where(doms[j] == d, turned[j], jnp.zeros((), jnp.bfloat16)) for j in range(4)], axis=1)
        gram = jnp.dot(left, stacked, preferred_element_type=jnp.float32)
        g11, g12, g22 = gram[:128, :128], gram[:128, 128:], gram[128:, 128:]
        packed = jnp.where(tri_col >= tri_row, g11, g22).astype(jnp.bfloat16)
        g12 = g12.astype(jnp.bfloat16)
        d1 = jnp.sum(jnp.where(tri_col == tri_row, g11, 0.0), axis=0, keepdims=True)
        d2 = jnp.sum(jnp.where(tri_col == tri_row, g22, 0.0), axis=0, keepdims=True)
        store_rows(grams, index, d * 256, g12)
        store_rows(grams, index, d * 256 + 128, packed)
        grams[3][pz, px, py, pl.ds(d * 4, 4)] = jnp.concatenate(
            [d1, d2, inn[d:d + 1, :128], inn[d:d + 1, 128:]], axis=0)


def listed_keys(held, own, other):
    lane = lax.broadcasted_iota(jnp.int32, (64, 128), 1)
    values = []
    for dom in range(4):
        entry = held[:, dom, :]
        owner, local_index = entry >> 6, entry & 63
        block = jnp.where(owner == own, local_index, local_index + 64)
        values.append(jnp.where((owner == own) | (owner == other), dom * 4096 + lane * 128 + block, BIG))
    out = jnp.full((64, 128), BIG, jnp.int32)
    for k in range(4):
        least = functools.reduce(jnp.minimum, values)
        least = jnp.min(least, axis=1, keepdims=True)
        out = jnp.where(lane == k, least, out)
        values = [jnp.where(value > least, value, BIG) for value in values]
    return out


def full_weights(packed_ref, index, tiles, k):
    row = lax.broadcasted_iota(jnp.int32, (128, 128), 0)
    col = lax.broadcasted_iota(jnp.int32, (128, 128), 1)
    wide = packed_ref[index + (pl.ds(0, 128),)].astype(jnp.float32)
    packed = packed_ref[index + (pl.ds(128, 128),)].astype(jnp.float32)
    rest = packed_ref[index + (pl.ds(256, 16),)].astype(jnp.float32)
    rest = rest[:4] + rest[4:8]
    columns = jnp.concatenate([rest, rest], axis=0).T
    first, second = columns[:, 2:3], columns[:, 3:4]
    turned = packed.T
    t11 = jnp.where(col > row, packed, jnp.where(col == row, rest[0:1], turned))
    t22 = jnp.where(col < row, packed, jnp.where(col == row, rest[1:2], turned))
    left, right = pl.ds(0, 128), pl.ds(128, 128)
    tiles[2 * k, :, left] = (t11 + first).astype(jnp.bfloat16)
    tiles[2 * k, :, right] = (wide + first).astype(jnp.bfloat16)
    tiles[2 * k + 1, :, left] = (wide.T + second).astype(jnp.bfloat16)
    tiles[2 * k + 1, :, right] = (t22 + second).astype(jnp.bfloat16)


def reduce_kernel(tile_ref, pert_ref, dep_ref, out_ref, *scratch):
    n = len(PARTS)
    scratch = list(scratch)

    def take(count):
        taken, scratch[:count] = scratch[:count], []
        return taken
    held, keys_vmem, keys_ref, valid_ref, sib_tile, sib_dep, blocks, deps, near, fin, fin_extra = take(11)
    grams = take(n)
    bufs = [[take(6) for _ in range(n)] for _ in range(2)] + [[take(3) for _ in range(n)]]
    send_sem, recv_sem, load_sem, list_send, list_recv, sib_send, sib_recv, halo_send, halo_recv, out_sem = scratch

    pos = coords()
    x, y, z = pos["x"], pos["y"], pos["z"]
    a, b = lax.axis_index("lat"), lax.axis_index("lon")
    lat_up, lat_down = ((a + 1) % 8, b), ((a + 7) % 8, b)
    lon_up, lon_down = (a, (b + 1) % 16), (a, (b + 15) % 16)
    sibling = shifted(pos, "c", 1)
    load = pltpu.make_async_copy(pert_ref, blocks.at[pl.ds(0, 64)], load_sem.at[0])
    load.start()
    own_valid = pltpu.make_async_copy(tile_ref, valid_ref.at[0], load_sem.at[1])
    own_valid.start()
    me = (y * 4 + x) * 4 + z
    held[me] = tile_ref[...]
    deps[pl.ds(0, 64)] = dep_ref[...].astype(jnp.float32)
    greet([shifted(pos, axis, step) for axis in "zxy" for step in (1, 2, 3)]
          + [sibling, lat_up, lat_down, lon_up, lon_down])

    sends = []

    def swap(k, src, dst):
        copy = pltpu.make_async_remote_copy(
            src_ref=src, dst_ref=dst, send_sem=sib_send.at[k], recv_sem=sib_recv.at[k],
            device_id=sibling, device_id_type=MESH)
        copy.start()
        sends.append(copy)
        return copy
    swaps = [swap(0, tile_ref, sib_tile), swap(1, dep_ref, sib_dep), swap(2, pert_ref, blocks.at[pl.ds(64, 64)])]
    for phase, (axis, first, count) in enumerate((("z", me, 1), ("x", (y * 4 + x) * 4, 4), ("y", y * 16, 16))):
        view = held.at[pl.ds(first, count)]
        copies = []
        for step in (1, 2, 3):
            copy = pltpu.make_async_remote_copy(
                src_ref=view, dst_ref=view, send_sem=list_send.at[phase, step - 1],
                recv_sem=list_recv.at[phase, step - 1],
                device_id=shifted(pos, axis, step), device_id_type=MESH)
            copy.start()
            copies.append(copy)
        for copy in copies:
            copy.wait_recv()
        sends += copies
    keys_vmem[...] = listed_keys(held, a * 16 + b, sibling[0] * 16 + sibling[1])
    keys_copy = pltpu.make_async_copy(keys_vmem, keys_ref, load_sem.at[2])
    keys_copy.start()
    swaps[0].wait_recv()
    sib_valid = pltpu.make_async_copy(sib_tile, valid_ref.at[1], load_sem.at[3])
    sib_valid.start()
    swaps[1].wait_recv()
    deps[pl.ds(64, 64)] = sib_dep[...].astype(jnp.float32)
    for copy in (own_valid, keys_copy, sib_valid, load):
        copy.wait()
    swaps[2].wait_recv()

    flights = [[[None] * 6 for _ in range(n)] for _ in range(2)]

    def prefix(i, phase):
        return tuple(pos[axis] for axis in PARTS[i][2][:phase])

    def half(i, phase, target, upper):
        return prefix(i, phase) + (target, pl.ds(2 * upper, 2))

    def start(i, phase, k, source, to_right):
        copy = pltpu.make_async_remote_copy(
            src_ref=source, dst_ref=bufs[phase][i][k],
            send_sem=send_sem.at[phase, i, k], recv_sem=recv_sem.at[phase, i, k],
            device_id=shifted(pos, PARTS[i][2][phase], 1 if to_right else 3), device_id_type=MESH)
        copy.start()
        sends.append(copy)
        flights[phase][i][k] = copy

    def coord(i, phase):
        return pos[PARTS[i][2][phase]]

    def send_far(i, phase, sides=(0, 1)):
        target = (coord(i, phase) + 2) % 4
        for side in sides:
            start(i, phase, side, grams[i].at[half(i, phase, target, side)], side == 0)

    def send_right(i, phase):
        start(i, phase, 2, grams[i].at[half(i, phase, (coord(i, phase) + 1) % 4, 1)], True)

    def send_left(i, phase):
        start(i, phase, 3, grams[i].at[half(i, phase, (coord(i, phase) + 3) % 4, 0)], False)

    def each(phase, body):
        def step(j, carry):
            body((j // 4, j % 4) if phase == 0 else (j,))
            return carry
        lax.fori_loop(0, 8 if phase == 0 else 2, step, 0)

    def local_index(i, phase, target, upper, lead):
        return prefix(i, phase) + (target, 2 * upper + lead[0]) + lead[1:]

    def forward(i, phase):
        m = coord(i, phase)
        for k, (target, upper) in enumerate((((m + 1) % 4, 0), ((m + 3) % 4, 1))):
            flights[phase][i][k].wait_recv()
            got = bufs[phase][i][k]

            def body(lead, got=got, target=target, upper=upper):
                mine = grams[i][local_index(i, phase, target, upper, lead)]
                got[lead] = (got[lead].astype(jnp.float32) + mine.astype(jnp.float32)).astype(got.dtype)
            each(phase, body)
            start(i, phase, 4 + k, got, k == 0)

    def finish(i, phase):
        m = coord(i, phase)
        for k in (2, 3, 4, 5):
            flights[phase][i][k].wait_recv()
        for upper, pair in enumerate(((4, 3), (2, 5))):
            f, g = (bufs[phase][i][k] for k in pair)

            def body(lead, f=f, g=g, upper=upper):
                index = local_index(i, phase, m, upper, lead)
                total = grams[i][index].astype(jnp.float32) + f[lead].astype(jnp.float32) + g[lead].astype(jnp.float32)
                grams[i][index] = total.astype(grams[i].dtype)
            each(phase, body)

    def send_last(i):
        copies = []
        for step in (1, 2, 3):
            copy = pltpu.make_async_remote_copy(
                src_ref=grams[i].at[prefix(i, 2) + ((coord(i, 2) + step) % 4,)], dst_ref=bufs[2][i][step - 1],
                send_sem=send_sem.at[2, i, step - 1], recv_sem=recv_sem.at[2, i, step - 1],
                device_id=shifted(pos, PARTS[i][2][2], step), device_id_type=MESH)
            copy.start()
            copies.append(copy)
        sends.extend(copies)
        return copies

    def finish_last(i, copies):
        for copy in copies:
            copy.wait_recv()
        total = grams[i][prefix(i, 2) + (coord(i, 2),)].astype(jnp.float32)
        for got in bufs[2][i]:
            total = total + got[...].astype(jnp.float32)
        if i < 3:
            fin[pl.ds(STARTS[i], PARTS[i][0])] = total
        else:
            fin_extra[...] = total

    def fill(count, place):
        def step(j, carry):
            fill_server(tuple(at % 4 for at in place(j)), keys_ref, valid_ref, blocks, deps, grams)
            return carry
        lax.fori_loop(0, count, step, 0)

    fill(8, lambda j: (x + 2, j // 4, z + j))
    send_far(0, 0, (0,))
    fill(8, lambda j: (x + 2, 2 + j // 4, z + j))
    send_far(0, 0, (1,))
    fill(6, lambda j: (x + 3 + j % 3, y + 2, j // 3))
    send_far(1, 0, (0,))
    fill(6, lambda j: (x + 3 + j % 3, y + 2, 2 + j // 3))
    send_far(1, 0, (1,))
    fill(9, lambda j: (x + 3 + j // 3, y + 3 + j % 3, z + 2))
    send_far(2, 0)
    send_far(3, 0)
    fill(9, lambda j: (x + 1, y + 3 + j // 3, z + 3 + j % 3))
    send_right(0, 0)
    fill(9, lambda j: (x + 3, y + 3 + j // 3, z + 3 + j % 3))
    send_left(0, 0)
    fill(3, lambda j: (x, y + 1, z + 3 + j))
    send_right(1, 0)
    fill(3, lambda j: (x, y + 3, z + 3 + j))
    send_left(1, 0)
    fill(3, lambda j: (x, y, z + 3 + j))
    for i in (2, 3):
        send_right(i, 0)
        send_left(i, 0)
    for i in range(n):
        forward(i, 0)
    for i in range(n):
        finish(i, 0)
        send_far(i, 1)
        send_right(i, 1)
        send_left(i, 1)
    for i in range(n):
        forward(i, 1)
    last = []
    for i in range(n):
        finish(i, 1)
        last.append(send_last(i))
    for i in range(n):
        finish_last(i, last[i])

    def solve(pair, between):
        domains = [(fin[pl.ds(d * 256, 128)], fin[pl.ds(d * 256 + 128, 128)], fin_extra[pl.ds(d * 4, 4)]) for d in pair]
        for d, (t12, triangles, rest) in zip(pair, packed_weights(domains, 256, between)):
            near[1, 1, d, pl.ds(0, 128)] = t12
            near[1, 1, d, pl.ds(128, 128)] = triangles
            near[1, 1, d, pl.ds(256, 16)] = rest

    halos = {}

    def halo(chunk, k, origin, to, target):
        span = pl.ds(2 * chunk, 2)
        copy = pltpu.make_async_remote_copy(
            src_ref=near.at[origin + (span,)], dst_ref=near.at[to + (span,)],
            send_sem=halo_send.at[chunk, k], recv_sem=halo_recv.at[chunk, k],
            device_id=target, device_id_type=MESH)
        copy.start()
        sends.append(copy)
        halos[chunk, to] = copy

    outs = []

    def unpack(chunk, at):
        first = (at[0] * 3 + at[1]) * 4 + 2 * chunk
        for k in range(2):
            full_weights(near, at + (2 * chunk + k,), blocks, first + k)
        copy = pltpu.make_async_copy(
            blocks.at[pl.ds(2 * first, 4)], out_ref.at[pl.ds(2 * first, 4)], out_sem.at[len(outs)])
        copy.start()
        outs.append(copy)

    def own_halo(chunk):
        halo(chunk, 0, (1, 1), (1, 0), lon_up)
        halo(chunk, 1, (1, 1), (1, 2), lon_down)
        halo(chunk, 2, (1, 1), (0, 1), lat_up)
        halo(chunk, 3, (1, 1), (2, 1), lat_down)

    def corner_halo(chunk):
        for column, k in ((0, 4), (2, 6)):
            halos[chunk, (1, column)].wait_recv()
            halo(chunk, k, (1, column), (0, column), lat_up)
            halo(chunk, k + 1, (1, column), (2, column), lat_down)

    solve((0, 1), lambda: None)
    own_halo(0)
    solve((2, 3), lambda: corner_halo(0))
    own_halo(1)
    for chunk in range(2):
        unpack(chunk, (1, 1))
    for column in (0, 2):
        unpack(0, (1, column))
    corner_halo(1)
    for column in (0, 2):
        unpack(1, (1, column))
    for chunk in range(2):
        for column in (1, 0, 2):
            for line in (0, 2):
                halos[chunk, (line, column)].wait_recv()
                unpack(chunk, (line, column))
    for copy in sends:
        copy.wait_send()
    for copy in outs:
        copy.wait()


def near_weights(tile, pert, dep):
    n = len(PARTS)
    hbm = pl.BlockSpec(memory_space=pltpu.HBM)
    full = pl.BlockSpec(memory_space=pltpu.VMEM)

    def vmem(shape, kind):
        return pltpu.VMEM(shape, kind)
    scratch = [
        vmem((64, 8, 128), jnp.int32),
        vmem((64, 128), jnp.int32),
        pltpu.SMEM((64, 128), jnp.int32),
        pltpu.SMEM((2, 8, 128), jnp.int32),
        vmem((8, 128), jnp.int32),
        vmem((64, 128), jnp.bfloat16),
        vmem((128, 128, 256), jnp.bfloat16),
        vmem((128, 128), jnp.float32),
        vmem((3, 3, 4, 272, 128), jnp.bfloat16),
        vmem((1024, 128), jnp.float32),
        vmem((16, 128), jnp.float32),
    ]
    scratch += [vmem((4, 4, 4, r, 128), t) for r, t, _ in PARTS]
    for shape in ((2, 4), (2,)):
        for r, t, _ in PARTS:
            scratch += [vmem(shape + (r, 128), t)] * 6
    for r, t, _ in PARTS:
        scratch += [vmem((r, 128), t)] * 3
    scratch += [pltpu.SemaphoreType.DMA(shape) for shape in (
        (3, n, 6), (3, n, 6), (4,), (3, 3), (3, 3), (3,), (3,), (2, 8), (2, 8), (18,))]
    return pl.pallas_call(
        reduce_kernel,
        out_shape=jax.ShapeDtypeStruct((72, 128, 256), jnp.bfloat16),
        in_specs=[full, hbm, full],
        out_specs=hbm,
        scratch_shapes=scratch,
        compiler_params=pltpu.CompilerParams(
            collective_id=1, has_side_effects=True, vmem_limit_bytes=58 << 20),
        name="reduce",
    )(tile, pert, dep)


STEP_TILES = 4


def interp_kernel(pos_ref, pert_ref, mean_ref, coef_ref, near_ref, out_ref):
    step = pl.program_id(0)
    mean_cols = mean_ref[...].T
    coef = coef_ref[...]
    coef_cols = jnp.concatenate([coef, coef], axis=0).T
    for tile in range(STEP_TILES):
        span = pl.ds(tile * 32, 32)
        held = pert_ref[:, span, :].reshape(256, 256)
        total = None
        for pair in ((0, 1), (2, 3)):
            near = [near_ref[pos_ref[(step * STEP_TILES + tile) * 4 + corner]] for corner in pair]
            both = jnp.dot(held, jnp.concatenate(near, axis=1), preferred_element_type=jnp.float32)
            for k, corner in enumerate(pair):
                factor = coef_cols[tile * 32:tile * 32 + 32, corner:corner + 1]
                term = both[:, 256 * k:256 * k + 256].reshape(8, 32, 256) * factor[None]
                total = term if total is None else total + term
        for level in range(8):
            base = mean_cols[tile * 32:tile * 32 + 32, level:level + 1]
            out_ref[level, span, :] = (total[level] + base).astype(jnp.bfloat16)


def interpolate(position, pert, mean, coef, near):
    cols = STEP_TILES * 32
    steps = pert.shape[1] // cols
    return pl.pallas_call(
        interp_kernel,
        out_shape=jax.ShapeDtypeStruct(pert.shape, jnp.bfloat16),
        grid_spec=pltpu.PrefetchScalarGridSpec(
            num_scalar_prefetch=1,
            grid=(steps,),
            in_specs=[
                pl.BlockSpec((8, cols, 256), lambda i, *_: (0, i, 0)),
                pl.BlockSpec((8, cols), lambda i, *_: (0, i)),
                pl.BlockSpec((4, cols), lambda i, *_: (0, i)),
                pl.BlockSpec((36, 256, 256), lambda i, *_: (0, 0, 0), pipeline_mode=pl.Buffered(1)),
            ],
            out_specs=pl.BlockSpec((8, cols, 256), lambda i, *_: (0, i, 0)),
        ),
        compiler_params=pltpu.CompilerParams(
            dimension_semantics=("arbitrary",), vmem_limit_bytes=58 << 20),
        name="interp",
    )(position, pert, mean, coef, near)


def local(
    obs_pert, obs_dep, valid_rows, local_lists, state_mean, state_pert, interp_lists, interp_coef
):
    n_lon = lax.axis_size("lon")
    domains_here = local_lists.shape[0]
    tile = jnp.concatenate([
        jnp.pad(local_lists, ((0, 0), (0, 128 - local_lists.shape[1])), constant_values=-1),
        jnp.pad(valid_rows[None, :], ((0, 3), (0, 64))),
    ], axis=0)
    near = near_weights(tile, obs_pert, obs_dep)
    owner = interp_lists // domains_here
    within = interp_lists % domains_here
    lat_step = owner // n_lon - lax.axis_index("lat")
    lon_step = (owner % n_lon - lax.axis_index("lon") + 1) % n_lon - 1
    position = ((lat_step + 1) * 3 + lon_step + 1) * domains_here + within
    return interpolate(position.reshape(-1), state_pert, state_mean, interp_coef, near.reshape(36, 256, 256))


def solution(mesh):
    in_specs = (
        P(("lat", "lon"), None, None),
        P(("lat", "lon"), None),
        P(("lat", "lon")),
        P(("lat", "lon"), None),
        P(None, ("lat", "lon")),
        P(None, ("lat", "lon"), None),
        P(("lat", "lon"), None),
        P(None, ("lat", "lon")),
    )
    out_specs = P(None, ("lat", "lon"), None)
    return jax.shard_map(local, mesh=mesh, in_specs=in_specs, out_specs=out_specs, check_vma=False)
```

```python
import functools

import jax
import jax.numpy as jnp
from jax import lax
from jax.experimental import pallas as pl
from jax.experimental.pallas import tpu as pltpu
from jax.sharding import PartitionSpec as P

NS_ITERS = 4
MESH = pl.DeviceIdType.MESH
BIG = 1 << 20
PARTS = ((400, jnp.bfloat16, "xyz"), (352, jnp.bfloat16, "yzx"), (272, jnp.bfloat16, "zxy"), (16, jnp.float32, "zxy"))
STARTS = (0, 400, 752)


def coords():
    a = lax.axis_index("lat")
    b = lax.axis_index("lon")
    return {"y": a // 2, "c": a % 2, "x": b // 4, "z": b % 4}


def device(pos):
    return (pos["y"] * 2 + pos["c"], pos["x"] * 4 + pos["z"])


def shifted(pos, axis, step):
    size = 2 if axis == "c" else 4
    return device({**pos, axis: (pos[axis] + step) % size})


def greet(peers):
    barrier = pltpu.get_barrier_semaphore()
    for peer in peers:
        pl.semaphore_signal(barrier, inc=1, device_id=peer, device_id_type=MESH)
    pl.semaphore_wait(barrier, len(peers))


def split(value):
    high = value.astype(jnp.bfloat16)
    return high, (value - high.astype(jnp.float32)).astype(jnp.bfloat16)


def product(left, right):
    (lh, ll), (rh, rl) = left, right
    dot = functools.partial(jnp.dot, preferred_element_type=jnp.float32)
    return dot(lh, rh) + (dot(lh, rl) + dot(ll, rh))


def packed_weights(domains, members, between):
    half = members // 2
    row = lax.broadcasted_iota(jnp.int32, (half, half), 0)
    col = lax.broadcasted_iota(jnp.int32, (half, half), 1)
    wide_row = lax.broadcasted_iota(jnp.int32, (members, members), 0)
    wide_col = lax.broadcasted_iota(jnp.int32, (members, members), 1)
    identity = jnp.where(wide_row == wide_col, 1.0, 0.0).astype(jnp.float32)
    scales, approxes = [], []
    for g12, packed, extra in domains:
        turned = packed.T
        g11 = jnp.where(col > row, packed, turned)
        g22 = jnp.where(col < row, packed, turned)
        g11 = jnp.where(col == row, extra[0:1], g11)
        g22 = jnp.where(col == row, extra[1:2], g22)
        gram = jnp.concatenate(
            [jnp.concatenate([g11, g12], axis=1), jnp.concatenate([g12.T, g22], axis=1)], axis=0)
        system = (members - 1.0) * identity + gram
        scale = jnp.sqrt(jnp.sum(jnp.sum(system * system, axis=0, keepdims=True), axis=1, keepdims=True))
        scales.append(scale)
        approxes.append(system / scale)
    roots = [1.5 * identity - 0.5 * approx for approx in approxes]
    approxes = [product(split(approx), split(root)) for approx, root in zip(approxes, roots)]
    for sweep in range(1, NS_ITERS):
        root_parts = [split(root) for root in roots]
        factors = [split(1.5 * identity - 0.5 * product(parts, split(approx)))
                   for parts, approx in zip(root_parts, approxes)]
        if sweep < NS_ITERS - 1:
            approxes = [product(split(approx), factor) for approx, factor in zip(approxes, factors)]
        roots = [product(factor, parts) for factor, parts in zip(factors, root_parts)]
        if sweep == 2:
            between()
    root_parts = [split(root) for root in roots]
    innovs = [jnp.broadcast_to(jnp.concatenate([extra[2:3], extra[3:4]], axis=1), (8, members)) for _, _, extra in domains]
    inners = [product(split(innov), parts) for innov, parts in zip(innovs, root_parts)]
    means = [product(split(inner), parts) / scale for inner, parts, scale in zip(inners, root_parts, scales)]
    results = []
    for root, mean, scale in zip(roots, means, scales):
        root = jnp.sqrt((members - 1.0) / scale) * root
        t11, t12, t22 = root[:half, :half], root[:half, half:], root[half:, half:]
        exact = [jnp.sum(jnp.where(col == row, t, 0.0), axis=0, keepdims=True) for t in (t11, t22)]
        exact += [mean[:1, :half], mean[:1, half:]]
        highs = [value.astype(jnp.bfloat16).astype(jnp.float32) for value in exact]
        lows = [value - high for value, high in zip(exact, highs)]
        rest = jnp.concatenate(highs + lows + [jnp.zeros((8, half), jnp.float32)], axis=0)
        results.append((t12.astype(jnp.bfloat16), jnp.where(col >= row, t11, t22).astype(jnp.bfloat16),
                        rest.astype(jnp.bfloat16)))
    return results


def store_rows(refs, index, first, value):
    count = value.shape[0]
    for i, start in enumerate(STARTS):
        low, high = max(first, start), min(first + count, start + PARTS[i][0])
        if low < high:
            refs[i][index[i] + (pl.ds(low - start, high - low),)] = value[low - first:high - first]


def fill_server(place, keys_ref, valid_ref, blocks, deps, grams):
    px, py, pz = place
    server = (py * 4 + px) * 4 + pz
    index = ((px, py, pz), (py, pz, px), (pz, px, py))
    rows = lax.broadcasted_iota(jnp.int32, (128, 256), 0)
    row8 = lax.broadcasted_iota(jnp.int32, (8, 128), 0)
    tri_row = lax.broadcasted_iota(jnp.int32, (128, 128), 0)
    tri_col = lax.broadcasted_iota(jnp.int32, (128, 128), 1)
    held, turned, doms, departs = [], [], [], []
    for j in range(4):
        key = keys_ref[server, j]
        block = key & 127
        dom = key >> 12
        count = jnp.where(key < BIG, valid_ref[block >> 6, 4, block & 63], 0)
        values = jnp.where(rows < count, blocks[block], jnp.zeros((), jnp.bfloat16))
        held.append(values)
        turned.append(values.T)
        doms.append(dom)
        depart = jnp.broadcast_to(deps[pl.ds(block, 1), :], (8, 128))
        departs.append(jnp.where(row8 == dom, depart, 0.0).astype(jnp.bfloat16))
    stacked = jnp.concatenate(held, axis=0)
    inn = jnp.dot(jnp.concatenate(departs, axis=1), stacked, preferred_element_type=jnp.float32)
    for d in range(4):
        left = jnp.concatenate(
            [jnp.where(doms[j] == d, turned[j], jnp.zeros((), jnp.bfloat16)) for j in range(4)], axis=1)
        gram = jnp.dot(left, stacked, preferred_element_type=jnp.float32)
        g11, g12, g22 = gram[:128, :128], gram[:128, 128:], gram[128:, 128:]
        packed = jnp.where(tri_col >= tri_row, g11, g22).astype(jnp.bfloat16)
        g12 = g12.astype(jnp.bfloat16)
        d1 = jnp.sum(jnp.where(tri_col == tri_row, g11, 0.0), axis=0, keepdims=True)
        d2 = jnp.sum(jnp.where(tri_col == tri_row, g22, 0.0), axis=0, keepdims=True)
        store_rows(grams, index, d * 256, g12)
        store_rows(grams, index, d * 256 + 128, packed)
        grams[3][pz, px, py, pl.ds(d * 4, 4)] = jnp.concatenate(
            [d1, d2, inn[d:d + 1, :128], inn[d:d + 1, 128:]], axis=0)


def listed_keys(held, own, other):
    lane = lax.broadcasted_iota(jnp.int32, (64, 128), 1)
    values = []
    for dom in range(4):
        entry = held[:, dom, :]
        owner, local_index = entry >> 6, entry & 63
        block = jnp.where(owner == own, local_index, local_index + 64)
        values.append(jnp.where((owner == own) | (owner == other), dom * 4096 + lane * 128 + block, BIG))
    out = jnp.full((64, 128), BIG, jnp.int32)
    for k in range(4):
        least = functools.reduce(jnp.minimum, values)
        least = jnp.min(least, axis=1, keepdims=True)
        out = jnp.where(lane == k, least, out)
        values = [jnp.where(value > least, value, BIG) for value in values]
    return out


def full_weights(packed_ref, index, tiles, k):
    row = lax.broadcasted_iota(jnp.int32, (128, 128), 0)
    col = lax.broadcasted_iota(jnp.int32, (128, 128), 1)
    wide = packed_ref[index + (pl.ds(0, 128),)].astype(jnp.float32)
    packed = packed_ref[index + (pl.ds(128, 128),)].astype(jnp.float32)
    rest = packed_ref[index + (pl.ds(256, 16),)].astype(jnp.float32)
    rest = rest[:4] + rest[4:8]
    columns = jnp.concatenate([rest, rest], axis=0).T
    first, second = columns[:, 2:3], columns[:, 3:4]
    turned = packed.T
    t11 = jnp.where(col > row, packed, jnp.where(col == row, rest[0:1], turned))
    t22 = jnp.where(col < row, packed, jnp.where(col == row, rest[1:2], turned))
    left, right = pl.ds(0, 128), pl.ds(128, 128)
    tiles[2 * k, :, left] = (t11 + first).astype(jnp.bfloat16)
    tiles[2 * k, :, right] = (wide + first).astype(jnp.bfloat16)
    tiles[2 * k + 1, :, left] = (wide.T + second).astype(jnp.bfloat16)
    tiles[2 * k + 1, :, right] = (t22 + second).astype(jnp.bfloat16)


def reduce_kernel(lists_ref, rows_ref, pert_ref, dep_ref, out_ref, *scratch):
    n = len(PARTS)
    scratch = list(scratch)

    def take(count):
        taken, scratch[:count] = scratch[:count], []
        return taken
    tile_ref, held, keys_vmem, keys_ref, valid_ref, sib_tile, sib_dep, blocks, deps, near, fin, fin_extra = take(12)
    grams = take(n)
    bufs = [[take(6) for _ in range(n)] for _ in range(2)] + [[take(3) for _ in range(n)]]
    send_sem, recv_sem, load_sem, list_send, list_recv, sib_send, sib_recv, halo_send, halo_recv, out_sem = scratch

    pos = coords()
    x, y, z = pos["x"], pos["y"], pos["z"]
    a, b = lax.axis_index("lat"), lax.axis_index("lon")
    lat_up, lat_down = ((a + 1) % 8, b), ((a + 7) % 8, b)
    lon_up, lon_down = (a, (b + 1) % 16), (a, (b + 15) % 16)
    sibling = shifted(pos, "c", 1)
    load = pltpu.make_async_copy(pert_ref, blocks.at[pl.ds(0, 64)], load_sem.at[0])
    load.start()
    tile_ref[...] = jnp.full((8, 128), -1, jnp.int32)
    tile_ref[pl.ds(0, 4), pl.ds(0, 24)] = lists_ref[...]
    tile_ref[pl.ds(4, 1), pl.ds(0, 64)] = rows_ref[...]
    own_valid = pltpu.make_async_copy(tile_ref, valid_ref.at[0], load_sem.at[1])
    own_valid.start()
    me = (y * 4 + x) * 4 + z
    held[me] = tile_ref[...]
    deps[pl.ds(0, 64)] = dep_ref[...].astype(jnp.float32)
    greet([shifted(pos, axis, step) for axis in "zxy" for step in (1, 2, 3)]
          + [sibling, lat_up, lat_down, lon_up, lon_down])

    sends = []

    def swap(k, src, dst):
        copy = pltpu.make_async_remote_copy(
            src_ref=src, dst_ref=dst, send_sem=sib_send.at[k], recv_sem=sib_recv.at[k],
            device_id=sibling, device_id_type=MESH)
        copy.start()
        sends.append(copy)
        return copy
    swaps = [swap(0, tile_ref, sib_tile), swap(1, dep_ref, sib_dep), swap(2, pert_ref, blocks.at[pl.ds(64, 64)])]
    for phase, (axis, first, count) in enumerate((("z", me, 1), ("x", (y * 4 + x) * 4, 4), ("y", y * 16, 16))):
        view = held.at[pl.ds(first, count)]
        copies = []
        for step in (1, 2, 3):
            copy = pltpu.make_async_remote_copy(
                src_ref=view, dst_ref=view, send_sem=list_send.at[phase, step - 1],
                recv_sem=list_recv.at[phase, step - 1],
                device_id=shifted(pos, axis, step), device_id_type=MESH)
            copy.start()
            copies.append(copy)
        for copy in copies:
            copy.wait_recv()
        sends += copies
    keys_vmem[...] = listed_keys(held, a * 16 + b, sibling[0] * 16 + sibling[1])
    keys_copy = pltpu.make_async_copy(keys_vmem, keys_ref, load_sem.at[2])
    keys_copy.start()
    swaps[0].wait_recv()
    sib_valid = pltpu.make_async_copy(sib_tile, valid_ref.at[1], load_sem.at[3])
    sib_valid.start()
    swaps[1].wait_recv()
    deps[pl.ds(64, 64)] = sib_dep[...].astype(jnp.float32)
    for copy in (own_valid, keys_copy, sib_valid, load):
        copy.wait()
    swaps[2].wait_recv()

    flights = [[[None] * 6 for _ in range(n)] for _ in range(2)]

    def prefix(i, phase):
        return tuple(pos[axis] for axis in PARTS[i][2][:phase])

    def half(i, phase, target, upper):
        return prefix(i, phase) + (target, pl.ds(2 * upper, 2))

    def start(i, phase, k, source, to_right):
        copy = pltpu.make_async_remote_copy(
            src_ref=source, dst_ref=bufs[phase][i][k],
            send_sem=send_sem.at[phase, i, k], recv_sem=recv_sem.at[phase, i, k],
            device_id=shifted(pos, PARTS[i][2][phase], 1 if to_right else 3), device_id_type=MESH)
        copy.start()
        sends.append(copy)
        flights[phase][i][k] = copy

    def coord(i, phase):
        return pos[PARTS[i][2][phase]]

    def send_far(i, phase, sides=(0, 1)):
        target = (coord(i, phase) + 2) % 4
        for side in sides:
            start(i, phase, side, grams[i].at[half(i, phase, target, side)], side == 0)

    def send_right(i, phase):
        start(i, phase, 2, grams[i].at[half(i, phase, (coord(i, phase) + 1) % 4, 1)], True)

    def send_left(i, phase):
        start(i, phase, 3, grams[i].at[half(i, phase, (coord(i, phase) + 3) % 4, 0)], False)

    def each(phase, body):
        def step(j, carry):
            body((j // 4, j % 4) if phase == 0 else (j,))
            return carry
        lax.fori_loop(0, 8 if phase == 0 else 2, step, 0)

    def local_index(i, phase, target, upper, lead):
        return prefix(i, phase) + (target, 2 * upper + lead[0]) + lead[1:]

    def forward(i, phase):
        m = coord(i, phase)
        for k, (target, upper) in enumerate((((m + 1) % 4, 0), ((m + 3) % 4, 1))):
            flights[phase][i][k].wait_recv()
            got = bufs[phase][i][k]

            def body(lead, got=got, target=target, upper=upper):
                mine = grams[i][local_index(i, phase, target, upper, lead)]
                got[lead] = (got[lead].astype(jnp.float32) + mine.astype(jnp.float32)).astype(got.dtype)
            each(phase, body)
            start(i, phase, 4 + k, got, k == 0)

    def finish(i, phase):
        m = coord(i, phase)
        for k in (2, 3, 4, 5):
            flights[phase][i][k].wait_recv()
        for upper, pair in enumerate(((4, 3), (2, 5))):
            f, g = (bufs[phase][i][k] for k in pair)

            def body(lead, f=f, g=g, upper=upper):
                index = local_index(i, phase, m, upper, lead)
                total = grams[i][index].astype(jnp.float32) + f[lead].astype(jnp.float32) + g[lead].astype(jnp.float32)
                grams[i][index] = total.astype(grams[i].dtype)
            each(phase, body)

    def send_last(i):
        copies = []
        for step in (1, 2, 3):
            copy = pltpu.make_async_remote_copy(
                src_ref=grams[i].at[prefix(i, 2) + ((coord(i, 2) + step) % 4,)], dst_ref=bufs[2][i][step - 1],
                send_sem=send_sem.at[2, i, step - 1], recv_sem=recv_sem.at[2, i, step - 1],
                device_id=shifted(pos, PARTS[i][2][2], step), device_id_type=MESH)
            copy.start()
            copies.append(copy)
        sends.extend(copies)
        return copies

    def finish_last(i, copies):
        for copy in copies:
            copy.wait_recv()
        total = grams[i][prefix(i, 2) + (coord(i, 2),)].astype(jnp.float32)
        for got in bufs[2][i]:
            total = total + got[...].astype(jnp.float32)
        if i < 3:
            fin[pl.ds(STARTS[i], PARTS[i][0])] = total
        else:
            fin_extra[...] = total

    def fill(count, place):
        together = 3 if count % 3 == 0 else 2

        def step(j, carry):
            for k in range(together):
                fill_server(tuple(at % 4 for at in place(j * together + k)), keys_ref, valid_ref, blocks, deps, grams)
            return carry
        lax.fori_loop(0, count // together, step, 0)

    fill(8, lambda j: (x + 2, j // 4, z + j))
    send_far(0, 0, (0,))
    fill(8, lambda j: (x + 2, 2 + j // 4, z + j))
    send_far(0, 0, (1,))
    fill(6, lambda j: (x + 3 + j % 3, y + 2, j // 3))
    send_far(1, 0, (0,))
    fill(6, lambda j: (x + 3 + j % 3, y + 2, 2 + j // 3))
    send_far(1, 0, (1,))
    fill(9, lambda j: (x + 3 + j // 3, y + 3 + j % 3, z + 2))
    send_far(2, 0)
    send_far(3, 0)
    fill(9, lambda j: (x + 1, y + 3 + j // 3, z + 3 + j % 3))
    send_right(0, 0)
    fill(9, lambda j: (x + 3, y + 3 + j // 3, z + 3 + j % 3))
    send_left(0, 0)
    fill(3, lambda j: (x, y + 1, z + 3 + j))
    send_right(1, 0)
    fill(3, lambda j: (x, y + 3, z + 3 + j))
    send_left(1, 0)
    fill(3, lambda j: (x, y, z + 3 + j))
    for i in (2, 3):
        send_right(i, 0)
        send_left(i, 0)
    for i in range(n):
        forward(i, 0)
    for i in range(n):
        finish(i, 0)
        send_far(i, 1)
        send_right(i, 1)
        send_left(i, 1)
    for i in range(n):
        forward(i, 1)
    last = []
    for i in range(n):
        finish(i, 1)
        last.append(send_last(i))
    for i in range(n):
        finish_last(i, last[i])

    def solve(pair, between):
        domains = [(fin[pl.ds(d * 256, 128)], fin[pl.ds(d * 256 + 128, 128)], fin_extra[pl.ds(d * 4, 4)]) for d in pair]
        for d, (t12, triangles, rest) in zip(pair, packed_weights(domains, 256, between)):
            near[1, 1, d, pl.ds(0, 128)] = t12
            near[1, 1, d, pl.ds(128, 128)] = triangles
            near[1, 1, d, pl.ds(256, 16)] = rest

    halos = {}

    def halo(chunk, k, origin, to, target):
        span = pl.ds(2 * chunk, 2)
        copy = pltpu.make_async_remote_copy(
            src_ref=near.at[origin + (span,)], dst_ref=near.at[to + (span,)],
            send_sem=halo_send.at[chunk, k], recv_sem=halo_recv.at[chunk, k],
            device_id=target, device_id_type=MESH)
        copy.start()
        sends.append(copy)
        halos[chunk, to] = copy

    outs = []

    def unpack(chunk, at):
        first = (at[0] * 3 + at[1]) * 4 + 2 * chunk
        for k in range(2):
            full_weights(near, at + (2 * chunk + k,), blocks, first + k)
        copy = pltpu.make_async_copy(
            blocks.at[pl.ds(2 * first, 4)], out_ref.at[pl.ds(2 * first, 4)], out_sem.at[len(outs)])
        copy.start()
        outs.append(copy)

    def own_halo(chunk):
        halo(chunk, 0, (1, 1), (1, 0), lon_up)
        halo(chunk, 1, (1, 1), (1, 2), lon_down)
        halo(chunk, 2, (1, 1), (0, 1), lat_up)
        halo(chunk, 3, (1, 1), (2, 1), lat_down)

    def corner_halo(chunk):
        for column, k in ((0, 4), (2, 6)):
            halos[chunk, (1, column)].wait_recv()
            halo(chunk, k, (1, column), (0, column), lat_up)
            halo(chunk, k + 1, (1, column), (2, column), lat_down)

    solve((0, 1), lambda: None)
    own_halo(0)
    solve((2, 3), lambda: corner_halo(0))
    own_halo(1)
    for chunk in range(2):
        unpack(chunk, (1, 1))
    for column in (0, 2):
        unpack(0, (1, column))
    corner_halo(1)
    for column in (0, 2):
        unpack(1, (1, column))
    for chunk in range(2):
        for column in (1, 0, 2):
            for line in (0, 2):
                halos[chunk, (line, column)].wait_recv()
                unpack(chunk, (line, column))
    for copy in sends:
        copy.wait_send()
    for copy in outs:
        copy.wait()


def near_weights(lists, rows, pert, dep):
    n = len(PARTS)
    hbm = pl.BlockSpec(memory_space=pltpu.HBM)
    full = pl.BlockSpec(memory_space=pltpu.VMEM)

    def vmem(shape, kind):
        return pltpu.VMEM(shape, kind)
    scratch = [
        vmem((8, 128), jnp.int32),
        vmem((64, 8, 128), jnp.int32),
        vmem((64, 128), jnp.int32),
        pltpu.SMEM((64, 128), jnp.int32),
        pltpu.SMEM((2, 8, 128), jnp.int32),
        vmem((8, 128), jnp.int32),
        vmem((64, 128), jnp.bfloat16),
        vmem((128, 128, 256), jnp.bfloat16),
        vmem((128, 128), jnp.float32),
        vmem((3, 3, 4, 272, 128), jnp.bfloat16),
        vmem((1024, 128), jnp.float32),
        vmem((16, 128), jnp.float32),
    ]
    scratch += [vmem((4, 4, 4, r, 128), t) for r, t, _ in PARTS]
    for shape in ((2, 4), (2,)):
        for r, t, _ in PARTS:
            scratch += [vmem(shape + (r, 128), t)] * 6
    for r, t, _ in PARTS:
        scratch += [vmem((r, 128), t)] * 3
    scratch += [pltpu.SemaphoreType.DMA(shape) for shape in (
        (3, n, 6), (3, n, 6), (4,), (3, 3), (3, 3), (3,), (3,), (2, 8), (2, 8), (18,))]
    return pl.pallas_call(
        reduce_kernel,
        out_shape=jax.ShapeDtypeStruct((72, 128, 256), jnp.bfloat16),
        in_specs=[full, full, hbm, full],
        out_specs=hbm,
        scratch_shapes=scratch,
        compiler_params=pltpu.CompilerParams(
            collective_id=1, has_side_effects=True, vmem_limit_bytes=58 << 20),
        name="reduce",
    )(lists, rows, pert, dep)


CHUNK = 256


def interp_kernel(lists_ref, mean_ref, coef_ref, pert_ref, near_ref, out_ref, held, near, done, near_sem, in_sem, out_sem):
    chunks = held.shape[1] // CHUNK
    a, b = lax.axis_index("lat"), lax.axis_index("lon")
    fetch_near = [pltpu.make_async_copy(near_ref.at[pl.ds(9 * k, 9)], near.at[pl.ds(9 * k, 9)], near_sem.at[k])
                  for k in range(4)]
    for copy in fetch_near:
        copy.start()

    def place(tile, corner):
        domain = lists_ref[corner, tile]
        lat, lon = domain // 64, (domain // 4) % 16
        return ((lat - a + 1) * 3 + (lon - b + 17) % 16) * 4 + domain % 4

    def fetch(c):
        span = pl.ds(pl.multiple_of(c * CHUNK, CHUNK), CHUNK)
        return pltpu.make_async_copy(pert_ref.at[:, span], held.at[:, span], in_sem.at[c])

    def write(c):
        span = pl.ds(pl.multiple_of(c * CHUNK, CHUNK), CHUNK)
        return pltpu.make_async_copy(done.at[:, span], out_ref.at[:, span], out_sem.at[c])

    for c in range(2):
        fetch(c).start()
    for copy in fetch_near:
        copy.wait()

    @pl.loop(2, chunks)
    def _(c):
        fetch(c).start()

    @pl.loop(0, chunks)
    def _(c):
        first = pl.multiple_of(c * CHUNK, CHUNK)
        mean_cols = mean_ref[:, pl.ds(first, CHUNK)].T
        coef = coef_ref[:, pl.ds(first, CHUNK)]
        coef_cols = jnp.concatenate([coef, coef], axis=0).T
        fetch(c).wait()
        for tile in range(CHUNK // 32):
            span = pl.ds(pl.multiple_of(first + tile * 32, 32), 32)
            left = held[:, span, :].reshape(256, 256)
            total = None
            for corner in range(4):
                prod = jnp.dot(left, near[place(c * (CHUNK // 32) + tile, corner)], preferred_element_type=jnp.float32)
                factor = coef_cols[tile * 32:tile * 32 + 32, corner:corner + 1]
                term = prod.reshape(8, 32, 256) * factor[None]
                total = term if total is None else total + term
            for level in range(8):
                base = mean_cols[tile * 32:tile * 32 + 32, level:level + 1]
                done[level, span, :] = (total[level] + base).astype(jnp.bfloat16)
        write(c).start()

    @pl.loop(0, chunks)
    def _(c):
        write(c).wait()


def interpolate(lists, pert, mean, coef, near):
    hbm = pl.BlockSpec(memory_space=pltpu.HBM)
    full = pl.BlockSpec(memory_space=pltpu.VMEM)
    chunks = pert.shape[1] // CHUNK
    return pl.pallas_call(
        interp_kernel,
        out_shape=jax.ShapeDtypeStruct(pert.shape, jnp.bfloat16),
        in_specs=[pl.BlockSpec(memory_space=pltpu.SMEM), full, full, hbm, hbm],
        out_specs=hbm,
        scratch_shapes=[
            pltpu.VMEM(pert.shape, jnp.bfloat16),
            pltpu.VMEM(near.shape, jnp.bfloat16),
            pltpu.VMEM(pert.shape, jnp.bfloat16),
            pltpu.SemaphoreType.DMA((4,)),
            pltpu.SemaphoreType.DMA((chunks,)),
            pltpu.SemaphoreType.DMA((chunks,)),
        ],
        compiler_params=pltpu.CompilerParams(vmem_limit_bytes=58 << 20),
        name="interp",
    )(lists, mean, coef, pert, near)


def local(
    obs_pert, obs_dep, valid_rows, local_lists, state_mean, state_pert, interp_lists, interp_coef
):
    near = near_weights(local_lists, valid_rows[None, :], obs_pert, obs_dep)
    return interpolate(interp_lists.T, state_pert, state_mean, interp_coef, near.reshape(36, 256, 256))


def solution(mesh):
    in_specs = (
        P(("lat", "lon"), None, None),
        P(("lat", "lon"), None),
        P(("lat", "lon")),
        P(("lat", "lon"), None),
        P(None, ("lat", "lon")),
        P(None, ("lat", "lon"), None),
        P(("lat", "lon"), None),
        P(None, ("lat", "lon")),
    )
    out_specs = P(None, ("lat", "lon"), None)
    return jax.shard_map(local, mesh=mesh, in_specs=in_specs, out_specs=out_specs, check_vma=False)
```

```python
import functools

import jax
import jax.numpy as jnp
from jax import lax
from jax.experimental import pallas as pl
from jax.experimental.pallas import tpu as pltpu
from jax.sharding import PartitionSpec as P

NS_ITERS = 4
MESH = pl.DeviceIdType.MESH
BIG = 1 << 20
PARTS = ((400, jnp.bfloat16, "xyz"), (352, jnp.bfloat16, "yzx"), (272, jnp.bfloat16, "zxy"), (16, jnp.float32, "zxy"))
STARTS = (0, 400, 752)
SPANS = ((0, 2), (2, 1), (3, 1))


def coords():
    a = lax.axis_index("lat")
    b = lax.axis_index("lon")
    return {"y": a // 2, "c": a % 2, "x": b // 4, "z": b % 4}


def device(pos):
    return (pos["y"] * 2 + pos["c"], pos["x"] * 4 + pos["z"])


def shifted(pos, axis, step):
    size = 2 if axis == "c" else 4
    return device({**pos, axis: (pos[axis] + step) % size})


def greet(peers):
    barrier = pltpu.get_barrier_semaphore()
    for peer in peers:
        pl.semaphore_signal(barrier, inc=1, device_id=peer, device_id_type=MESH)
    pl.semaphore_wait(barrier, len(peers))


def split(value):
    high = value.astype(jnp.bfloat16)
    return high, (value - high.astype(jnp.float32)).astype(jnp.bfloat16)


def product(left, right):
    (lh, ll), (rh, rl) = left, right
    dot = functools.partial(jnp.dot, preferred_element_type=jnp.float32)
    return dot(lh, rh) + (dot(lh, rl) + dot(ll, rh))


def packed_weights(domains, members, between):
    half = members // 2
    row = lax.broadcasted_iota(jnp.int32, (half, half), 0)
    col = lax.broadcasted_iota(jnp.int32, (half, half), 1)
    wide_row = lax.broadcasted_iota(jnp.int32, (members, members), 0)
    wide_col = lax.broadcasted_iota(jnp.int32, (members, members), 1)
    identity = jnp.where(wide_row == wide_col, 1.0, 0.0).astype(jnp.float32)
    scales, approxes = [], []
    for g12, packed, extra in domains:
        turned = packed.T
        g11 = jnp.where(col > row, packed, turned)
        g22 = jnp.where(col < row, packed, turned)
        g11 = jnp.where(col == row, extra[0:1], g11)
        g22 = jnp.where(col == row, extra[1:2], g22)
        gram = jnp.concatenate(
            [jnp.concatenate([g11, g12], axis=1), jnp.concatenate([g12.T, g22], axis=1)], axis=0)
        system = (members - 1.0) * identity + gram
        scale = jnp.sqrt(jnp.sum(jnp.sum(system * system, axis=0, keepdims=True), axis=1, keepdims=True))
        scales.append(scale)
        approxes.append(system / scale)
    roots = [1.5 * identity - 0.5 * approx for approx in approxes]
    approxes = [product(split(approx), split(root)) for approx, root in zip(approxes, roots)]
    for sweep in range(1, NS_ITERS):
        root_parts = [split(root) for root in roots]
        factors = [split(1.5 * identity - 0.5 * product(parts, split(approx)))
                   for parts, approx in zip(root_parts, approxes)]
        if sweep < NS_ITERS - 1:
            approxes = [product(split(approx), factor) for approx, factor in zip(approxes, factors)]
        roots = [product(factor, parts) for factor, parts in zip(factors, root_parts)]
        if sweep == 2:
            between()
    root_parts = [split(root) for root in roots]
    innovs = [jnp.broadcast_to(jnp.concatenate([extra[2:3], extra[3:4]], axis=1), (8, members)) for _, _, extra in domains]
    inners = [product(split(innov), parts) for innov, parts in zip(innovs, root_parts)]
    means = [product(split(inner), parts) / scale for inner, parts, scale in zip(inners, root_parts, scales)]
    results = []
    for root, mean, scale in zip(roots, means, scales):
        root = jnp.sqrt((members - 1.0) / scale) * root
        t11, t12, t22 = root[:half, :half], root[:half, half:], root[half:, half:]
        exact = [jnp.sum(jnp.where(col == row, t, 0.0), axis=0, keepdims=True) for t in (t11, t22)]
        exact += [mean[:1, :half], mean[:1, half:]]
        highs = [value.astype(jnp.bfloat16).astype(jnp.float32) for value in exact]
        lows = [value - high for value, high in zip(exact, highs)]
        rest = jnp.concatenate(highs + lows + [jnp.zeros((8, half), jnp.float32)], axis=0)
        results.append((t12.astype(jnp.bfloat16), jnp.where(col >= row, t11, t22).astype(jnp.bfloat16),
                        rest.astype(jnp.bfloat16)))
    return results


def store_rows(refs, index, first, value):
    count = value.shape[0]
    for i, start in enumerate(STARTS):
        low, high = max(first, start), min(first + count, start + PARTS[i][0])
        if low < high:
            refs[i][index[i] + (pl.ds(low - start, high - low),)] = value[low - first:high - first]


def fill_server(place, keys_ref, valid_ref, blocks, deps, grams):
    px, py, pz = place
    server = (py * 4 + px) * 4 + pz
    index = ((px, py, pz), (py, pz, px), (pz, px, py))
    rows = lax.broadcasted_iota(jnp.int32, (128, 256), 0)
    row8 = lax.broadcasted_iota(jnp.int32, (8, 128), 0)
    tri_row = lax.broadcasted_iota(jnp.int32, (128, 128), 0)
    tri_col = lax.broadcasted_iota(jnp.int32, (128, 128), 1)
    held, turned, doms, departs = [], [], [], []
    for j in range(4):
        key = keys_ref[server, j]
        block = key & 127
        dom = key >> 12
        count = jnp.where(key < BIG, valid_ref[block >> 6, 4, block & 63], 0)
        values = jnp.where(rows < count, blocks[block], jnp.zeros((), jnp.bfloat16))
        held.append(values)
        turned.append(values.T)
        doms.append(dom)
        depart = jnp.broadcast_to(deps[pl.ds(block, 1), :], (8, 128))
        departs.append(jnp.where(row8 == dom, depart, 0.0).astype(jnp.bfloat16))
    stacked = jnp.concatenate(held, axis=0)
    inn = jnp.dot(jnp.concatenate(departs, axis=1), stacked, preferred_element_type=jnp.float32)
    for d in range(4):
        left = jnp.concatenate(
            [jnp.where(doms[j] == d, turned[j], jnp.zeros((), jnp.bfloat16)) for j in range(4)], axis=1)
        gram = jnp.dot(left, stacked, preferred_element_type=jnp.float32)
        g11, g12, g22 = gram[:128, :128], gram[:128, 128:], gram[128:, 128:]
        packed = jnp.where(tri_col >= tri_row, g11, g22).astype(jnp.bfloat16)
        g12 = g12.astype(jnp.bfloat16)
        d1 = jnp.sum(jnp.where(tri_col == tri_row, g11, 0.0), axis=0, keepdims=True)
        d2 = jnp.sum(jnp.where(tri_col == tri_row, g22, 0.0), axis=0, keepdims=True)
        store_rows(grams, index, d * 256, g12)
        store_rows(grams, index, d * 256 + 128, packed)
        grams[3][pz, px, py, pl.ds(d * 4, 4)] = jnp.concatenate(
            [d1, d2, inn[d:d + 1, :128], inn[d:d + 1, 128:]], axis=0)


def listed_keys(held, own, other):
    lane = lax.broadcasted_iota(jnp.int32, (64, 128), 1)
    dom = lane // 24
    entry = held[:, 0, :]
    owner, local_index = entry >> 6, entry & 63
    block = jnp.where(owner == own, local_index, local_index + 64)
    mine = ((owner == own) | (owner == other)) & (lane < 96)
    value = jnp.where(mine, dom * 4096 + (lane - 24 * dom) * 128 + block, BIG)
    out = jnp.full((64, 128), BIG, jnp.int32)
    for k in range(4):
        least = jnp.min(value, axis=1, keepdims=True)
        out = jnp.where(lane == k, least, out)
        value = jnp.where(value > least, value, BIG)
    return out


def full_weights(packed_ref, index, tiles, k):
    row = lax.broadcasted_iota(jnp.int32, (128, 128), 0)
    col = lax.broadcasted_iota(jnp.int32, (128, 128), 1)
    wide = packed_ref[index + (pl.ds(0, 128),)].astype(jnp.float32)
    packed = packed_ref[index + (pl.ds(128, 128),)].astype(jnp.float32)
    rest = packed_ref[index + (pl.ds(256, 16),)].astype(jnp.float32)
    rest = rest[:4] + rest[4:8]
    first, second = rest[2:3], rest[3:4]
    turned = packed.T
    t11 = jnp.where(col > row, packed, jnp.where(col == row, rest[0:1], turned))
    t22 = jnp.where(col < row, packed, jnp.where(col == row, rest[1:2], turned))
    left, right = pl.ds(0, 128), pl.ds(128, 128)
    tiles[2 * k, :, left] = (t11 + first).astype(jnp.bfloat16)
    tiles[2 * k, :, right] = (wide + second).astype(jnp.bfloat16)
    tiles[2 * k + 1, :, left] = (wide.T + first).astype(jnp.bfloat16)
    tiles[2 * k + 1, :, right] = (t22 + second).astype(jnp.bfloat16)


def reduce_kernel(lists_ref, rows_ref, pert_ref, dep_ref, out_ref, *scratch):
    n = len(PARTS)
    scratch = list(scratch)

    def take(count):
        taken, scratch[:count] = scratch[:count], []
        return taken
    tile_ref, held, keys_vmem, keys_ref, valid_ref, sib_tile, sib_dep, blocks, deps, near, fin, fin_extra = take(12)
    grams = take(n)
    bufs = [[take(6) for _ in range(n)] for _ in range(2)] + [[take(3) for _ in range(n)]]
    send_sem, recv_sem, load_sem, list_send, list_recv, sib_send, sib_recv, halo_send, halo_recv, out_sem = scratch

    pos = coords()
    x, y, z = pos["x"], pos["y"], pos["z"]
    a, b = lax.axis_index("lat"), lax.axis_index("lon")
    lat_up, lat_down = ((a + 1) % 8, b), ((a + 7) % 8, b)
    lon_up, lon_down = (a, (b + 1) % 16), (a, (b + 15) % 16)
    sibling = shifted(pos, "c", 1)
    load = pltpu.make_async_copy(pert_ref, blocks.at[pl.ds(0, 64)], load_sem.at[0])
    load.start()
    tile_ref[...] = jnp.zeros((8, 128), jnp.int32)
    tile_ref[pl.ds(0, 4), pl.ds(0, 24)] = lists_ref[...]
    tile_ref[pl.ds(4, 1), pl.ds(0, 64)] = rows_ref[...]
    own_valid = pltpu.make_async_copy(tile_ref, valid_ref.at[0], load_sem.at[1])
    own_valid.start()
    me = (y * 4 + x) * 4 + z
    entries = tile_ref[...]
    listed = entries
    for d in range(1, 4):
        listed = listed + pltpu.roll(jnp.roll(entries, -d, 0), 24 * d, 1)
    held[me] = listed[0:1]
    deps[pl.ds(0, 64)] = dep_ref[...].astype(jnp.float32)
    greet([shifted(pos, axis, step) for axis in "zxy" for step in (1, 2, 3)]
          + [sibling, lat_up, lat_down, lon_up, lon_down])

    sends = []

    def swap(k, src, dst):
        copy = pltpu.make_async_remote_copy(
            src_ref=src, dst_ref=dst, send_sem=sib_send.at[k], recv_sem=sib_recv.at[k],
            device_id=sibling, device_id_type=MESH)
        copy.start()
        sends.append(copy)
        return copy
    swaps = [swap(0, tile_ref, sib_tile), swap(1, dep_ref, sib_dep), swap(2, pert_ref, blocks.at[pl.ds(64, 64)])]
    for phase, (axis, first, count) in enumerate((("z", me, 1), ("x", (y * 4 + x) * 4, 4), ("y", y * 16, 16))):
        view = held.at[pl.ds(first, count)]
        copies = []
        for step in (1, 2, 3):
            copy = pltpu.make_async_remote_copy(
                src_ref=view, dst_ref=view, send_sem=list_send.at[phase, step - 1],
                recv_sem=list_recv.at[phase, step - 1],
                device_id=shifted(pos, axis, step), device_id_type=MESH)
            copy.start()
            copies.append(copy)
        for copy in copies:
            copy.wait_recv()
        sends += copies
    keys_vmem[...] = listed_keys(held, a * 16 + b, sibling[0] * 16 + sibling[1])
    keys_copy = pltpu.make_async_copy(keys_vmem, keys_ref, load_sem.at[2])
    keys_copy.start()
    swaps[0].wait_recv()
    sib_valid = pltpu.make_async_copy(sib_tile, valid_ref.at[1], load_sem.at[3])
    sib_valid.start()
    swaps[1].wait_recv()
    deps[pl.ds(64, 64)] = sib_dep[...].astype(jnp.float32)
    for copy in (own_valid, keys_copy, sib_valid, load):
        copy.wait()
    swaps[2].wait_recv()

    flights = [[[None] * 6 for _ in range(n)] for _ in range(2)]

    def prefix(i, phase):
        return tuple(pos[axis] for axis in PARTS[i][2][:phase])

    def half(i, phase, target, upper):
        return prefix(i, phase) + (target, pl.ds(2 * upper, 2))

    def start(i, phase, k, source, to_right):
        copy = pltpu.make_async_remote_copy(
            src_ref=source, dst_ref=bufs[phase][i][k],
            send_sem=send_sem.at[phase, i, k], recv_sem=recv_sem.at[phase, i, k],
            device_id=shifted(pos, PARTS[i][2][phase], 1 if to_right else 3), device_id_type=MESH)
        copy.start()
        sends.append(copy)
        flights[phase][i][k] = copy

    def coord(i, phase):
        return pos[PARTS[i][2][phase]]

    def send_far(i, phase, sides=(0, 1)):
        target = (coord(i, phase) + 2) % 4
        for side in sides:
            start(i, phase, side, grams[i].at[half(i, phase, target, side)], side == 0)

    def send_right(i, phase):
        start(i, phase, 2, grams[i].at[half(i, phase, (coord(i, phase) + 1) % 4, 1)], True)

    def send_left(i, phase):
        start(i, phase, 3, grams[i].at[half(i, phase, (coord(i, phase) + 3) % 4, 0)], False)

    def each(phase, body):
        def step(j, carry):
            body((j // 4, j % 4) if phase == 0 else (j,))
            return carry
        lax.fori_loop(0, 8 if phase == 0 else 2, step, 0)

    def local_index(i, phase, target, upper, lead):
        return prefix(i, phase) + (target, 2 * upper + lead[0]) + lead[1:]

    def forward(i, phase):
        m = coord(i, phase)
        for k, (target, upper) in enumerate((((m + 1) % 4, 0), ((m + 3) % 4, 1))):
            flights[phase][i][k].wait_recv()
            got = bufs[phase][i][k]

            def body(lead, got=got, target=target, upper=upper):
                mine = grams[i][local_index(i, phase, target, upper, lead)]
                got[lead] = (got[lead].astype(jnp.float32) + mine.astype(jnp.float32)).astype(got.dtype)
            each(phase, body)
            start(i, phase, 4 + k, got, k == 0)

    def finish(i, phase):
        m = coord(i, phase)
        for k in (2, 3, 4, 5):
            flights[phase][i][k].wait_recv()
        for upper, pair in enumerate(((4, 3), (2, 5))):
            f, g = (bufs[phase][i][k] for k in pair)

            def body(lead, f=f, g=g, upper=upper):
                index = local_index(i, phase, m, upper, lead)
                total = grams[i][index].astype(jnp.float32) + f[lead].astype(jnp.float32) + g[lead].astype(jnp.float32)
                grams[i][index] = total.astype(grams[i].dtype)
            each(phase, body)

    def send_last(i):
        copies = []
        for step in (1, 2, 3):
            copy = pltpu.make_async_remote_copy(
                src_ref=grams[i].at[prefix(i, 2) + ((coord(i, 2) + step) % 4,)], dst_ref=bufs[2][i][step - 1],
                send_sem=send_sem.at[2, i, step - 1], recv_sem=recv_sem.at[2, i, step - 1],
                device_id=shifted(pos, PARTS[i][2][2], step), device_id_type=MESH)
            copy.start()
            copies.append(copy)
        sends.extend(copies)
        return copies

    def finish_last(i, copies):
        for copy in copies:
            copy.wait_recv()
        total = grams[i][prefix(i, 2) + (coord(i, 2),)].astype(jnp.float32)
        for got in bufs[2][i]:
            total = total + got[...].astype(jnp.float32)
        if i < 3:
            fin[pl.ds(STARTS[i], PARTS[i][0])] = total
        else:
            fin_extra[...] = total

    def fill(count, place):
        together = 3 if count % 3 == 0 else 2

        def step(j, carry):
            for k in range(together):
                fill_server(tuple(at % 4 for at in place(j * together + k)), keys_ref, valid_ref, blocks, deps, grams)
            return carry
        lax.fori_loop(0, count // together, step, 0)

    fill(8, lambda j: (x + 2, j // 4, z + j))
    send_far(0, 0, (0,))
    fill(8, lambda j: (x + 2, 2 + j // 4, z + j))
    send_far(0, 0, (1,))
    fill(6, lambda j: (x + 3 + j % 3, y + 2, j // 3))
    send_far(1, 0, (0,))
    fill(6, lambda j: (x + 3 + j % 3, y + 2, 2 + j // 3))
    send_far(1, 0, (1,))
    fill(9, lambda j: (x + 3 + j // 3, y + 3 + j % 3, z + 2))
    send_far(2, 0)
    send_far(3, 0)
    fill(9, lambda j: (x + 1, y + 3 + j // 3, z + 3 + j % 3))
    send_right(0, 0)
    fill(9, lambda j: (x + 3, y + 3 + j // 3, z + 3 + j % 3))
    send_left(0, 0)
    fill(3, lambda j: (x, y + 1, z + 3 + j))
    send_right(1, 0)
    fill(3, lambda j: (x, y + 3, z + 3 + j))
    send_left(1, 0)
    fill(3, lambda j: (x, y, z + 3 + j))
    for i in (2, 3):
        send_right(i, 0)
        send_left(i, 0)
    for i in range(n):
        forward(i, 0)
    for i in range(n):
        finish(i, 0)
        send_far(i, 1)
        send_right(i, 1)
        send_left(i, 1)
    for i in range(n):
        forward(i, 1)
    last = []
    for i in range(n):
        finish(i, 1)
        last.append(send_last(i))
    for i in range(n):
        finish_last(i, last[i])

    def solve(pair, between):
        domains = [(fin[pl.ds(d * 256, 128)], fin[pl.ds(d * 256 + 128, 128)], fin_extra[pl.ds(d * 4, 4)]) for d in pair]
        for d, (t12, triangles, rest) in zip(pair, packed_weights(domains, 256, between)):
            near[1, 1, d, pl.ds(0, 128)] = t12
            near[1, 1, d, pl.ds(128, 128)] = triangles
            near[1, 1, d, pl.ds(256, 16)] = rest

    halos = {}

    def halo(chunk, k, origin, to, target):
        span = pl.ds(*SPANS[chunk])
        copy = pltpu.make_async_remote_copy(
            src_ref=near.at[origin + (span,)], dst_ref=near.at[to + (span,)],
            send_sem=halo_send.at[chunk, k], recv_sem=halo_recv.at[chunk, k],
            device_id=target, device_id_type=MESH)
        copy.start()
        sends.append(copy)
        halos[chunk, to] = copy

    outs = []

    def unpack(chunk, at):
        start_dom, count = SPANS[chunk]
        first = (at[0] * 3 + at[1]) * 4 + start_dom
        for k in range(count):
            full_weights(near, at + (start_dom + k,), blocks, first + k)
        span = pl.ds(2 * first, 2 * count)
        copy = pltpu.make_async_copy(blocks.at[span], out_ref.at[span], out_sem.at[len(outs)])
        copy.start()
        outs.append(copy)

    def own_halo(chunk):
        halo(chunk, 0, (1, 1), (1, 0), lon_up)
        halo(chunk, 1, (1, 1), (1, 2), lon_down)
        halo(chunk, 2, (1, 1), (0, 1), lat_up)
        halo(chunk, 3, (1, 1), (2, 1), lat_down)

    def corner_halo(chunk):
        for column, k in ((0, 4), (2, 6)):
            halos[chunk, (1, column)].wait_recv()
            halo(chunk, k, (1, column), (0, column), lat_up)
            halo(chunk, k + 1, (1, column), (2, column), lat_down)

    solve((0, 1), lambda: None)
    own_halo(0)
    solve((2, 3), lambda: corner_halo(0))
    own_halo(1)
    own_halo(2)
    for chunk in range(3):
        unpack(chunk, (1, 1))
    for column in (0, 2):
        unpack(0, (1, column))
    for chunk in (1, 2):
        corner_halo(chunk)
        for column in (0, 2):
            unpack(chunk, (1, column))
    for chunk in range(3):
        for column in (1, 0, 2):
            for line in (0, 2):
                halos[chunk, (line, column)].wait_recv()
                unpack(chunk, (line, column))
    for copy in sends:
        copy.wait_send()
    for copy in outs:
        copy.wait()


def near_weights(lists, rows, pert, dep):
    n = len(PARTS)
    hbm = pl.BlockSpec(memory_space=pltpu.HBM)
    full = pl.BlockSpec(memory_space=pltpu.VMEM)

    def vmem(shape, kind):
        return pltpu.VMEM(shape, kind)
    scratch = [
        vmem((8, 128), jnp.int32),
        vmem((64, 1, 128), jnp.int32),
        vmem((64, 128), jnp.int32),
        pltpu.SMEM((64, 128), jnp.int32),
        pltpu.SMEM((2, 8, 128), jnp.int32),
        vmem((8, 128), jnp.int32),
        vmem((64, 128), jnp.bfloat16),
        vmem((128, 128, 256), jnp.bfloat16),
        vmem((128, 128), jnp.float32),
        vmem((3, 3, 4, 272, 128), jnp.bfloat16),
        vmem((1024, 128), jnp.float32),
        vmem((16, 128), jnp.float32),
    ]
    scratch += [vmem((4, 4, 4, r, 128), t) for r, t, _ in PARTS]
    for shape in ((2, 4), (2,)):
        for r, t, _ in PARTS:
            scratch += [vmem(shape + (r, 128), t)] * 6
    for r, t, _ in PARTS:
        scratch += [vmem((r, 128), t)] * 3
    scratch += [pltpu.SemaphoreType.DMA(shape) for shape in (
        (3, n, 6), (3, n, 6), (4,), (3, 3), (3, 3), (3,), (3,), (3, 8), (3, 8), (27,))]
    return pl.pallas_call(
        reduce_kernel,
        out_shape=jax.ShapeDtypeStruct((72, 128, 256), jnp.bfloat16),
        in_specs=[full, full, hbm, full],
        out_specs=hbm,
        scratch_shapes=scratch,
        compiler_params=pltpu.CompilerParams(
            collective_id=1, has_side_effects=True, vmem_limit_bytes=58 << 20),
        name="reduce",
    )(lists, rows, pert, dep)


CHUNK = 256


def interp_kernel(lists_ref, mean_ref, coef_ref, pert_ref, near_ref, out_ref, held, near, done, near_sem, in_sem, out_sem):
    chunks = held.shape[1] // CHUNK
    a, b = lax.axis_index("lat"), lax.axis_index("lon")
    fetch_near = [pltpu.make_async_copy(near_ref.at[pl.ds(9 * k, 9)], near.at[pl.ds(9 * k, 9)], near_sem.at[k])
                  for k in range(4)]
    for copy in fetch_near:
        copy.start()

    def place(tile, corner):
        domain = lists_ref[corner, tile]
        lat, lon = domain // 64, (domain // 4) % 16
        return ((lat - a + 1) * 3 + (lon - b + 17) % 16) * 4 + domain % 4

    def fetch(c):
        span = pl.ds(pl.multiple_of(c * CHUNK, CHUNK), CHUNK)
        return pltpu.make_async_copy(pert_ref.at[:, span], held.at[:, span], in_sem.at[c])

    def write(c):
        span = pl.ds(pl.multiple_of(c * CHUNK, CHUNK), CHUNK)
        return pltpu.make_async_copy(done.at[:, span], out_ref.at[:, span], out_sem.at[c])

    for c in range(2):
        fetch(c).start()
    for copy in fetch_near:
        copy.wait()

    @pl.loop(2, chunks)
    def _(c):
        fetch(c).start()

    @pl.loop(0, chunks)
    def _(c):
        first = pl.multiple_of(c * CHUNK, CHUNK)
        fetch(c).wait()
        lane = lax.broadcasted_iota(jnp.int32, (8, 128), 1)
        level = lax.broadcasted_iota(jnp.int32, (8, 128), 0)

        def spread(value, group):
            value = jnp.where(lane // 32 == group, value, 0.0)
            value = value + pltpu.roll(value, 32, 1)
            return value + pltpu.roll(value, 64, 1)

        for tile in range(CHUNK // 32):
            span = pl.ds(pl.multiple_of(first + tile * 32, 32), 32)
            lanes = pl.ds(pl.multiple_of(first + tile // 4 * 128, 128), 128)
            means = spread(mean_ref[:, lanes], tile % 4)
            coef = coef_ref[:, lanes]
            coefs = spread(jnp.concatenate([coef, coef], axis=0), tile % 4)
            total = jnp.concatenate(
                [jnp.sum(jnp.where(level == lane // 32 + 4 * k, means, 0.0), axis=0, keepdims=True) for k in range(2)], axis=1)
            right = held[:, span, :].reshape(256, 256)
            for corner in range(4):
                prod = lax.dot_general(near[place(c * (CHUNK // 32) + tile, corner)], right, (((1,), (1,)), ((), ())), preferred_element_type=jnp.float32)
                row = coefs[corner:corner + 1]
                total = total + prod * jnp.concatenate([row, row], axis=1)
            done[:, span, :] = total.astype(jnp.bfloat16).T.reshape(8, 32, 256)
        write(c).start()

    @pl.loop(0, chunks)
    def _(c):
        write(c).wait()


def interpolate(lists, pert, mean, coef, near):
    hbm = pl.BlockSpec(memory_space=pltpu.HBM)
    full = pl.BlockSpec(memory_space=pltpu.VMEM)
    chunks = pert.shape[1] // CHUNK
    return pl.pallas_call(
        interp_kernel,
        out_shape=jax.ShapeDtypeStruct(pert.shape, jnp.bfloat16),
        in_specs=[pl.BlockSpec(memory_space=pltpu.SMEM), full, full, hbm, hbm],
        out_specs=hbm,
        scratch_shapes=[
            pltpu.VMEM(pert.shape, jnp.bfloat16),
            pltpu.VMEM(near.shape, jnp.bfloat16),
            pltpu.VMEM(pert.shape, jnp.bfloat16),
            pltpu.SemaphoreType.DMA((4,)),
            pltpu.SemaphoreType.DMA((chunks,)),
            pltpu.SemaphoreType.DMA((chunks,)),
        ],
        compiler_params=pltpu.CompilerParams(vmem_limit_bytes=58 << 20),
        name="interp",
    )(lists, mean, coef, pert, near)


def local(
    obs_pert, obs_dep, valid_rows, local_lists, state_mean, state_pert, interp_lists, interp_coef
):
    near = near_weights(local_lists, valid_rows[None, :], obs_pert, obs_dep)
    return interpolate(interp_lists.T, state_pert, state_mean, interp_coef, near.reshape(36, 256, 256))


def solution(mesh):
    in_specs = (
        P(("lat", "lon"), None, None),
        P(("lat", "lon"), None),
        P(("lat", "lon")),
        P(("lat", "lon"), None),
        P(None, ("lat", "lon")),
        P(None, ("lat", "lon"), None),
        P(("lat", "lon"), None),
        P(None, ("lat", "lon")),
    )
    out_specs = P(None, ("lat", "lon"), None)
    return jax.shard_map(local, mesh=mesh, in_specs=in_specs, out_specs=out_specs, check_vma=False)
```

```python
import functools

import jax
import jax.numpy as jnp
from jax import lax
from jax.experimental import pallas as pl
from jax.experimental.pallas import tpu as pltpu
from jax.sharding import PartitionSpec as P

NS_ITERS = 4
MESH = pl.DeviceIdType.MESH
BIG = 1 << 20
PARTS = ((400, jnp.bfloat16, "xyz"), (352, jnp.bfloat16, "yzx"), (272, jnp.bfloat16, "zxy"), (16, jnp.float32, "zxy"))
STARTS = (0, 400, 752)
SPANS = ((0, 2), (2, 1), (3, 1))


def coords():
    a = lax.axis_index("lat")
    b = lax.axis_index("lon")
    return {"y": a // 2, "c": a % 2, "x": b // 4, "z": b % 4}


def device(pos):
    return (pos["y"] * 2 + pos["c"], pos["x"] * 4 + pos["z"])


def shifted(pos, axis, step):
    size = 2 if axis == "c" else 4
    return device({**pos, axis: (pos[axis] + step) % size})


def greet(peers):
    barrier = pltpu.get_barrier_semaphore()
    for peer in peers:
        pl.semaphore_signal(barrier, inc=1, device_id=peer, device_id_type=MESH)
    pl.semaphore_wait(barrier, len(peers))


def split(value):
    high = value.astype(jnp.bfloat16)
    return high, (value - high.astype(jnp.float32)).astype(jnp.bfloat16)


def product(left, right):
    (lh, ll), (rh, rl) = left, right
    dot = functools.partial(jnp.dot, preferred_element_type=jnp.float32)
    return dot(lh, rh) + (dot(lh, rl) + dot(ll, rh))


def packed_weights(domains, members, between):
    half = members // 2
    row = lax.broadcasted_iota(jnp.int32, (half, half), 0)
    col = lax.broadcasted_iota(jnp.int32, (half, half), 1)
    wide_row = lax.broadcasted_iota(jnp.int32, (members, members), 0)
    wide_col = lax.broadcasted_iota(jnp.int32, (members, members), 1)
    identity = jnp.where(wide_row == wide_col, 1.0, 0.0).astype(jnp.float32)
    scales, approxes = [], []
    for g12, packed, extra in domains:
        turned = packed.T
        g11 = jnp.where(col > row, packed, turned)
        g22 = jnp.where(col < row, packed, turned)
        g11 = jnp.where(col == row, extra[0:1], g11)
        g22 = jnp.where(col == row, extra[1:2], g22)
        gram = jnp.concatenate(
            [jnp.concatenate([g11, g12], axis=1), jnp.concatenate([g12.T, g22], axis=1)], axis=0)
        system = (members - 1.0) * identity + gram
        scale = jnp.sqrt(jnp.sum(jnp.sum(system * system, axis=0, keepdims=True), axis=1, keepdims=True))
        scales.append(scale)
        approxes.append(system / scale)
    roots = [1.5 * identity - 0.5 * approx for approx in approxes]
    approxes = [product(split(approx), split(root)) for approx, root in zip(approxes, roots)]
    for sweep in range(1, NS_ITERS):
        root_parts = [split(root) for root in roots]
        factors = [split(1.5 * identity - 0.5 * product(parts, split(approx)))
                   for parts, approx in zip(root_parts, approxes)]
        if sweep < NS_ITERS - 1:
            approxes = [product(split(approx), factor) for approx, factor in zip(approxes, factors)]
        roots = [product(factor, parts) for factor, parts in zip(factors, root_parts)]
        if sweep == 2:
            between()
    root_parts = [split(root) for root in roots]
    innovs = [jnp.broadcast_to(jnp.concatenate([extra[2:3], extra[3:4]], axis=1), (8, members)) for _, _, extra in domains]
    inners = [product(split(innov), parts) for innov, parts in zip(innovs, root_parts)]
    means = [product(split(inner), parts) / scale for inner, parts, scale in zip(inners, root_parts, scales)]
    results = []
    for root, mean, scale in zip(roots, means, scales):
        root = jnp.sqrt((members - 1.0) / scale) * root
        t11, t12, t22 = root[:half, :half], root[:half, half:], root[half:, half:]
        exact = [jnp.sum(jnp.where(col == row, t, 0.0), axis=0, keepdims=True) for t in (t11, t22)]
        exact += [mean[:1, :half], mean[:1, half:]]
        highs = [value.astype(jnp.bfloat16).astype(jnp.float32) for value in exact]
        lows = [value - high for value, high in zip(exact, highs)]
        rest = jnp.concatenate(highs + lows + [jnp.zeros((8, half), jnp.float32)], axis=0)
        results.append((t12.astype(jnp.bfloat16), jnp.where(col >= row, t11, t22).astype(jnp.bfloat16),
                        rest.astype(jnp.bfloat16)))
    return results


def store_rows(refs, index, first, value):
    count = value.shape[0]
    for i, start in enumerate(STARTS):
        low, high = max(first, start), min(first + count, start + PARTS[i][0])
        if low < high:
            refs[i][index[i] + (pl.ds(low - start, high - low),)] = value[low - first:high - first]


def fill_server(place, keys_ref, valid_ref, blocks, deps, grams):
    px, py, pz = place
    server = (py * 4 + px) * 4 + pz
    index = ((px, py, pz), (py, pz, px), (pz, px, py))
    rows = lax.broadcasted_iota(jnp.int32, (128, 256), 0)
    row8 = lax.broadcasted_iota(jnp.int32, (8, 128), 0)
    tri_row = lax.broadcasted_iota(jnp.int32, (128, 128), 0)
    tri_col = lax.broadcasted_iota(jnp.int32, (128, 128), 1)
    held, turned, doms, departs = [], [], [], []
    for j in range(4):
        key = keys_ref[server, j]
        block = key & 127
        dom = key >> 12
        count = jnp.where(key < BIG, valid_ref[block >> 6, 4, block & 63], 0)
        values = jnp.where(rows < count, blocks[block], jnp.zeros((), jnp.bfloat16))
        held.append(values)
        turned.append(values.T)
        doms.append(dom)
        depart = jnp.broadcast_to(deps[pl.ds(block, 1), :], (8, 128))
        departs.append(jnp.where(row8 == dom, depart, 0.0).astype(jnp.bfloat16))
    stacked = jnp.concatenate(held, axis=0)
    inn = jnp.dot(jnp.concatenate(departs, axis=1), stacked, preferred_element_type=jnp.float32)
    for d in range(4):
        left = jnp.concatenate(
            [jnp.where(doms[j] == d, turned[j], jnp.zeros((), jnp.bfloat16)) for j in range(4)], axis=1)
        gram = jnp.dot(left, stacked, preferred_element_type=jnp.float32)
        g11, g12, g22 = gram[:128, :128], gram[:128, 128:], gram[128:, 128:]
        packed = jnp.where(tri_col >= tri_row, g11, g22).astype(jnp.bfloat16)
        g12 = g12.astype(jnp.bfloat16)
        d1 = jnp.sum(jnp.where(tri_col == tri_row, g11, 0.0), axis=0, keepdims=True)
        d2 = jnp.sum(jnp.where(tri_col == tri_row, g22, 0.0), axis=0, keepdims=True)
        store_rows(grams, index, d * 256, g12)
        store_rows(grams, index, d * 256 + 128, packed)
        grams[3][pz, px, py, pl.ds(d * 4, 4)] = jnp.concatenate(
            [d1, d2, inn[d:d + 1, :128], inn[d:d + 1, 128:]], axis=0)


def listed_keys(held, own, other):
    lane = lax.broadcasted_iota(jnp.int32, (64, 128), 1)
    dom = lane // 24
    entry = held[:, 0, :]
    owner, local_index = entry >> 6, entry & 63
    block = jnp.where(owner == own, local_index, local_index + 64)
    mine = ((owner == own) | (owner == other)) & (lane < 96)
    value = jnp.where(mine, dom * 4096 + (lane - 24 * dom) * 128 + block, BIG)
    out = jnp.full((64, 128), BIG, jnp.int32)
    for k in range(4):
        least = jnp.min(value, axis=1, keepdims=True)
        out = jnp.where(lane == k, least, out)
        value = jnp.where(value > least, value, BIG)
    return out


def full_weights(packed_ref, index, tiles, k):
    row = lax.broadcasted_iota(jnp.int32, (128, 128), 0)
    col = lax.broadcasted_iota(jnp.int32, (128, 128), 1)
    wide = packed_ref[index + (pl.ds(0, 128),)].astype(jnp.float32)
    packed = packed_ref[index + (pl.ds(128, 128),)].astype(jnp.float32)
    rest = packed_ref[index + (pl.ds(256, 16),)].astype(jnp.float32)
    rest = rest[:4] + rest[4:8]
    first, second = rest[2:3], rest[3:4]
    turned = packed.T
    t11 = jnp.where(col > row, packed, jnp.where(col == row, rest[0:1], turned))
    t22 = jnp.where(col < row, packed, jnp.where(col == row, rest[1:2], turned))
    left, right = pl.ds(0, 128), pl.ds(128, 128)
    tiles[2 * k, :, left] = (t11 + first).astype(jnp.bfloat16)
    tiles[2 * k, :, right] = (wide + second).astype(jnp.bfloat16)
    tiles[2 * k + 1, :, left] = (wide.T + first).astype(jnp.bfloat16)
    tiles[2 * k + 1, :, right] = (t22 + second).astype(jnp.bfloat16)


def reduce_kernel(lists_ref, rows_ref, pert_ref, dep_ref, out_ref, *scratch):
    n = len(PARTS)
    scratch = list(scratch)

    def take(count):
        taken, scratch[:count] = scratch[:count], []
        return taken
    tile_ref, held, keys_vmem, keys_ref, valid_ref, sib_tile, sib_dep, blocks, deps, near, fin, fin_extra = take(12)
    grams = take(n)
    bufs = [[take(4) for _ in range(n)] for _ in range(2)] + [[take(3) for _ in range(n)]]
    send_sem, recv_sem, load_sem, list_send, list_recv, sib_send, sib_recv, halo_send, halo_recv, out_sem = scratch

    pos = coords()
    x, y, z = pos["x"], pos["y"], pos["z"]
    a, b = lax.axis_index("lat"), lax.axis_index("lon")
    lat_up, lat_down = ((a + 1) % 8, b), ((a + 7) % 8, b)
    lon_up, lon_down = (a, (b + 1) % 16), (a, (b + 15) % 16)
    sibling = shifted(pos, "c", 1)
    load = pltpu.make_async_copy(pert_ref, blocks.at[pl.ds(0, 64)], load_sem.at[0])
    load.start()
    tile_ref[...] = jnp.zeros((8, 128), jnp.int32)
    tile_ref[pl.ds(0, 4), pl.ds(0, 24)] = lists_ref[...]
    tile_ref[pl.ds(4, 1), pl.ds(0, 64)] = rows_ref[...]
    own_valid = pltpu.make_async_copy(tile_ref, valid_ref.at[0], load_sem.at[1])
    own_valid.start()
    me = (y * 4 + x) * 4 + z
    entries = tile_ref[...]
    listed = entries
    for d in range(1, 4):
        listed = listed + pltpu.roll(jnp.roll(entries, -d, 0), 24 * d, 1)
    held[me] = listed[0:1]
    deps[pl.ds(0, 64)] = dep_ref[...].astype(jnp.float32)
    greet([shifted(pos, axis, step) for axis in "zxy" for step in (1, 2, 3)]
          + [sibling, lat_up, lat_down, lon_up, lon_down])

    sends = []

    def swap(k, src, dst):
        copy = pltpu.make_async_remote_copy(
            src_ref=src, dst_ref=dst, send_sem=sib_send.at[k], recv_sem=sib_recv.at[k],
            device_id=sibling, device_id_type=MESH)
        copy.start()
        sends.append(copy)
        return copy
    swaps = [swap(0, tile_ref, sib_tile), swap(1, dep_ref, sib_dep), swap(2, pert_ref, blocks.at[pl.ds(64, 64)])]
    for phase, (axis, first, count) in enumerate((("z", me, 1), ("x", (y * 4 + x) * 4, 4), ("y", y * 16, 16))):
        view = held.at[pl.ds(first, count)]
        copies = []
        for step in (1, 2, 3):
            copy = pltpu.make_async_remote_copy(
                src_ref=view, dst_ref=view, send_sem=list_send.at[phase, step - 1],
                recv_sem=list_recv.at[phase, step - 1],
                device_id=shifted(pos, axis, step), device_id_type=MESH)
            copy.start()
            copies.append(copy)
        for copy in copies:
            copy.wait_recv()
        sends += copies
    keys_vmem[...] = listed_keys(held, a * 16 + b, sibling[0] * 16 + sibling[1])
    keys_copy = pltpu.make_async_copy(keys_vmem, keys_ref, load_sem.at[2])
    keys_copy.start()
    swaps[0].wait_recv()
    sib_valid = pltpu.make_async_copy(sib_tile, valid_ref.at[1], load_sem.at[3])
    sib_valid.start()
    swaps[1].wait_recv()
    deps[pl.ds(64, 64)] = sib_dep[...].astype(jnp.float32)
    for copy in (own_valid, keys_copy, sib_valid, load):
        copy.wait()
    swaps[2].wait_recv()

    flights = [[[None] * 6 for _ in range(n)] for _ in range(2)]

    def prefix(i, phase):
        return tuple(pos[axis] for axis in PARTS[i][2][:phase])

    def half(i, phase, target, upper):
        return prefix(i, phase) + (target, pl.ds(2 * upper, 2))

    def landing(i, phase, k):
        if k < 2:
            return bufs[phase][i][k]
        which, upper = {2: (3, 1), 3: (3, 0), 4: (2, 0), 5: (2, 1)}[k]
        return bufs[phase][i][which].at[pl.ds(2 * upper, 2)]

    def start(i, phase, k, source, to_right):
        copy = pltpu.make_async_remote_copy(
            src_ref=source, dst_ref=landing(i, phase, k),
            send_sem=send_sem.at[phase, i, k], recv_sem=recv_sem.at[phase, i, k],
            device_id=shifted(pos, PARTS[i][2][phase], 1 if to_right else 3), device_id_type=MESH)
        copy.start()
        sends.append(copy)
        flights[phase][i][k] = copy

    def coord(i, phase):
        return pos[PARTS[i][2][phase]]

    def send_far(i, phase, sides=(0, 1)):
        target = (coord(i, phase) + 2) % 4
        for side in sides:
            start(i, phase, side, grams[i].at[half(i, phase, target, side)], side == 0)

    def send_right(i, phase):
        start(i, phase, 2, grams[i].at[half(i, phase, (coord(i, phase) + 1) % 4, 1)], True)

    def send_left(i, phase):
        start(i, phase, 3, grams[i].at[half(i, phase, (coord(i, phase) + 3) % 4, 0)], False)

    def each(phase, body):
        def step(j, carry):
            body((j // 4, j % 4) if phase == 0 else (j,))
            return carry
        lax.fori_loop(0, 8 if phase == 0 else 2, step, 0)

    def local_index(i, phase, target, upper, lead):
        return prefix(i, phase) + (target, 2 * upper + lead[0]) + lead[1:]

    def forward(i, phase):
        m = coord(i, phase)
        for k, (target, upper) in enumerate((((m + 1) % 4, 0), ((m + 3) % 4, 1))):
            flights[phase][i][k].wait_recv()
            got = bufs[phase][i][k]

            def body(lead, got=got, target=target, upper=upper):
                mine = grams[i][local_index(i, phase, target, upper, lead)]
                got[lead] = (got[lead].astype(jnp.float32) + mine.astype(jnp.float32)).astype(got.dtype)
            each(phase, body)
            start(i, phase, 4 + k, got, k == 0)

    def arrived(i, phase):
        for k in (2, 3, 4, 5):
            flights[phase][i][k].wait_recv()

    def finish(i, phase, target):
        pairs, singles = bufs[phase][i][2:]

        def body(lead):
            index = prefix(i, phase + 1) + lead
            total = (grams[i][index].astype(jnp.float32) + pairs[lead].astype(jnp.float32)
                     + singles[lead].astype(jnp.float32))
            grams[i][index] = total.astype(grams[i].dtype)
        if phase == 1:
            body((target,))
            return

        def step(j, carry):
            body((target, j))
            return carry
        lax.fori_loop(0, 4, step, 0)

    def send_last(i, step):
        copy = pltpu.make_async_remote_copy(
            src_ref=grams[i].at[prefix(i, 2) + ((coord(i, 2) + step) % 4,)], dst_ref=bufs[2][i][step - 1],
            send_sem=send_sem.at[2, i, step - 1], recv_sem=recv_sem.at[2, i, step - 1],
            device_id=shifted(pos, PARTS[i][2][2], step), device_id_type=MESH)
        copy.start()
        sends.append(copy)
        return copy

    def finish_last(i, copies):
        for copy in copies:
            copy.wait_recv()
        total = grams[i][prefix(i, 2) + (coord(i, 2),)].astype(jnp.float32)
        for got in bufs[2][i]:
            total = total + got[...].astype(jnp.float32)
        if i < 3:
            fin[pl.ds(STARTS[i], PARTS[i][0])] = total
        else:
            fin_extra[...] = total

    def fill(count, place):
        together = 3 if count % 3 == 0 else 2

        def step(j, carry):
            for k in range(together):
                fill_server(tuple(at % 4 for at in place(j * together + k)), keys_ref, valid_ref, blocks, deps, grams)
            return carry
        lax.fori_loop(0, count // together, step, 0)

    fill(8, lambda j: (x + 2, j // 4, z + j))
    send_far(0, 0, (0,))
    fill(8, lambda j: (x + 2, 2 + j // 4, z + j))
    send_far(0, 0, (1,))
    fill(6, lambda j: (x + 3 + j % 3, y + 2, j // 3))
    send_far(1, 0, (0,))
    fill(6, lambda j: (x + 3 + j % 3, y + 2, 2 + j // 3))
    send_far(1, 0, (1,))
    fill(9, lambda j: (x + 3 + j // 3, y + 3 + j % 3, z + 2))
    send_far(2, 0)
    send_far(3, 0)
    fill(9, lambda j: (x + 1, y + 3 + j // 3, z + 3 + j % 3))
    send_right(0, 0)
    fill(9, lambda j: (x + 3, y + 3 + j // 3, z + 3 + j % 3))
    send_left(0, 0)
    fill(3, lambda j: (x, y + 1, z + 3 + j))
    send_right(1, 0)
    fill(3, lambda j: (x, y + 3, z + 3 + j))
    send_left(1, 0)
    fill(3, lambda j: (x, y, z + 3 + j))
    for i in (2, 3):
        send_right(i, 0)
        send_left(i, 0)
    for i in range(n):
        forward(i, 0)
    for i in range(n):
        arrived(i, 0)
        m = coord(i, 1)
        finish(i, 0, (m + 2) % 4)
        send_far(i, 1)
        finish(i, 0, (m + 1) % 4)
        send_right(i, 1)
        finish(i, 0, (m + 3) % 4)
        send_left(i, 1)
    for i in range(n):
        finish(i, 0, coord(i, 1))
        forward(i, 1)
    last = []
    for i in range(n):
        arrived(i, 1)
        copies = []
        for step in (2, 1, 3):
            finish(i, 1, (coord(i, 2) + step) % 4)
            copies.append(send_last(i, step))
        finish(i, 1, coord(i, 2))
        last.append(copies)
    for i in range(n):
        finish_last(i, last[i])

    def solve(pair, between):
        domains = [(fin[pl.ds(d * 256, 128)], fin[pl.ds(d * 256 + 128, 128)], fin_extra[pl.ds(d * 4, 4)]) for d in pair]
        for d, (t12, triangles, rest) in zip(pair, packed_weights(domains, 256, between)):
            near[1, 1, d, pl.ds(0, 128)] = t12
            near[1, 1, d, pl.ds(128, 128)] = triangles
            near[1, 1, d, pl.ds(256, 16)] = rest

    halos = {}

    def halo(chunk, k, origin, to, target):
        span = pl.ds(*SPANS[chunk])
        copy = pltpu.make_async_remote_copy(
            src_ref=near.at[origin + (span,)], dst_ref=near.at[to + (span,)],
            send_sem=halo_send.at[chunk, k], recv_sem=halo_recv.at[chunk, k],
            device_id=target, device_id_type=MESH)
        copy.start()
        sends.append(copy)
        halos[chunk, to] = copy

    outs = []

    def unpack(chunk, at):
        start_dom, count = SPANS[chunk]
        first = (at[0] * 3 + at[1]) * 4 + start_dom
        for k in range(count):
            full_weights(near, at + (start_dom + k,), blocks, first + k)
        span = pl.ds(2 * first, 2 * count)
        copy = pltpu.make_async_copy(blocks.at[span], out_ref.at[span], out_sem.at[len(outs)])
        copy.start()
        outs.append(copy)

    def own_halo(chunk):
        halo(chunk, 0, (1, 1), (1, 0), lon_up)
        halo(chunk, 1, (1, 1), (1, 2), lon_down)
        halo(chunk, 2, (1, 1), (0, 1), lat_up)
        halo(chunk, 3, (1, 1), (2, 1), lat_down)

    def corner_halo(chunk):
        for column, k in ((0, 4), (2, 6)):
            halos[chunk, (1, column)].wait_recv()
            halo(chunk, k, (1, column), (0, column), lat_up)
            halo(chunk, k + 1, (1, column), (2, column), lat_down)

    solve((0, 1), lambda: None)
    own_halo(0)
    solve((2, 3), lambda: corner_halo(0))
    own_halo(1)
    own_halo(2)
    for chunk in range(3):
        unpack(chunk, (1, 1))
    for column in (0, 2):
        unpack(0, (1, column))
    for chunk in (1, 2):
        corner_halo(chunk)
        for column in (0, 2):
            unpack(chunk, (1, column))
    for chunk in range(3):
        for column in (1, 0, 2):
            for line in (0, 2):
                halos[chunk, (line, column)].wait_recv()
                unpack(chunk, (line, column))
    for copy in sends:
        copy.wait_send()
    for copy in outs:
        copy.wait()


def near_weights(lists, rows, pert, dep):
    n = len(PARTS)
    hbm = pl.BlockSpec(memory_space=pltpu.HBM)
    full = pl.BlockSpec(memory_space=pltpu.VMEM)

    def vmem(shape, kind):
        return pltpu.VMEM(shape, kind)
    scratch = [
        vmem((8, 128), jnp.int32),
        vmem((64, 1, 128), jnp.int32),
        vmem((64, 128), jnp.int32),
        pltpu.SMEM((64, 128), jnp.int32),
        pltpu.SMEM((2, 8, 128), jnp.int32),
        vmem((8, 128), jnp.int32),
        vmem((64, 128), jnp.bfloat16),
        vmem((128, 128, 256), jnp.bfloat16),
        vmem((128, 128), jnp.float32),
        vmem((3, 3, 4, 272, 128), jnp.bfloat16),
        vmem((1024, 128), jnp.float32),
        vmem((16, 128), jnp.float32),
    ]
    scratch += [vmem((4, 4, 4, r, 128), t) for r, t, _ in PARTS]
    for shape in ((2, 4), (2,)):
        for r, t, _ in PARTS:
            scratch += [vmem(shape + (r, 128), t)] * 2 + [vmem((4,) + shape[1:] + (r, 128), t)] * 2
    for r, t, _ in PARTS:
        scratch += [vmem((r, 128), t)] * 3
    scratch += [pltpu.SemaphoreType.DMA(shape) for shape in (
        (3, n, 6), (3, n, 6), (4,), (3, 3), (3, 3), (3,), (3,), (3, 8), (3, 8), (27,))]
    return pl.pallas_call(
        reduce_kernel,
        out_shape=jax.ShapeDtypeStruct((72, 128, 256), jnp.bfloat16),
        in_specs=[full, full, hbm, full],
        out_specs=hbm,
        scratch_shapes=scratch,
        compiler_params=pltpu.CompilerParams(
            collective_id=1, has_side_effects=True, vmem_limit_bytes=58 << 20),
        name="reduce",
    )(lists, rows, pert, dep)


CHUNK = 256


def interp_kernel(lists_ref, mean_ref, coef_ref, pert_ref, near_ref, out_ref, held, near, done, near_sem, in_sem, out_sem):
    chunks = held.shape[1] // CHUNK
    a, b = lax.axis_index("lat"), lax.axis_index("lon")
    fetch_near = [pltpu.make_async_copy(near_ref.at[pl.ds(4 * k, 4)], near.at[pl.ds(4 * k, 4)], near_sem.at[k])
                  for k in range(9)]
    for copy in fetch_near:
        copy.start()

    def place(tile, corner):
        domain = lists_ref[corner, tile]
        lat, lon = domain // 64, (domain // 4) % 16
        return ((lat - a + 1) * 3 + (lon - b + 17) % 16) * 4 + domain % 4

    def fetch(c):
        span = pl.ds(pl.multiple_of(c * CHUNK, CHUNK), CHUNK)
        return pltpu.make_async_copy(pert_ref.at[:, span], held.at[:, span], in_sem.at[c])

    def write(c):
        span = pl.ds(pl.multiple_of(c * CHUNK, CHUNK), CHUNK)
        return pltpu.make_async_copy(done.at[:, span], out_ref.at[:, span], out_sem.at[c])

    for c in range(2):
        fetch(c).start()
    for copy in fetch_near:
        copy.wait()

    @pl.loop(2, chunks)
    def _(c):
        fetch(c).start()

    @pl.loop(0, chunks)
    def _(c):
        first = pl.multiple_of(c * CHUNK, CHUNK)
        fetch(c).wait()
        lane = lax.broadcasted_iota(jnp.int32, (8, 128), 1)
        level = lax.broadcasted_iota(jnp.int32, (8, 128), 0)

        def spread(value, group):
            value = jnp.where(lane // 32 == group, value, 0.0)
            value = value + pltpu.roll(value, 32, 1)
            return value + pltpu.roll(value, 64, 1)

        for tile in range(CHUNK // 32):
            span = pl.ds(pl.multiple_of(first + tile * 32, 32), 32)
            lanes = pl.ds(pl.multiple_of(first + tile // 4 * 128, 128), 128)
            means = spread(mean_ref[:, lanes], tile % 4)
            coef = coef_ref[:, lanes]
            coefs = spread(jnp.concatenate([coef, coef], axis=0), tile % 4)
            total = jnp.concatenate(
                [jnp.sum(jnp.where(level == lane // 32 + 4 * k, means, 0.0), axis=0, keepdims=True) for k in range(2)], axis=1)
            right = held[:, span, :].reshape(256, 256)
            for corner in range(4):
                prod = lax.dot_general(near[place(c * (CHUNK // 32) + tile, corner)], right, (((1,), (1,)), ((), ())), preferred_element_type=jnp.float32)
                row = coefs[corner:corner + 1]
                total = total + prod * jnp.concatenate([row, row], axis=1)
            done[:, span, :] = total.astype(jnp.bfloat16).T.reshape(8, 32, 256)
        write(c).start()

    @pl.loop(0, chunks)
    def _(c):
        write(c).wait()


def interpolate(lists, pert, mean, coef, near):
    hbm = pl.BlockSpec(memory_space=pltpu.HBM)
    full = pl.BlockSpec(memory_space=pltpu.VMEM)
    chunks = pert.shape[1] // CHUNK
    return pl.pallas_call(
        interp_kernel,
        out_shape=jax.ShapeDtypeStruct(pert.shape, jnp.bfloat16),
        in_specs=[pl.BlockSpec(memory_space=pltpu.SMEM), full, full, hbm, hbm],
        out_specs=hbm,
        scratch_shapes=[
            pltpu.VMEM(pert.shape, jnp.bfloat16),
            pltpu.VMEM(near.shape, jnp.bfloat16),
            pltpu.VMEM(pert.shape, jnp.bfloat16),
            pltpu.SemaphoreType.DMA((9,)),
            pltpu.SemaphoreType.DMA((chunks,)),
            pltpu.SemaphoreType.DMA((chunks,)),
        ],
        compiler_params=pltpu.CompilerParams(vmem_limit_bytes=58 << 20),
        name="interp",
    )(lists, mean, coef, pert, near)


def local(
    obs_pert, obs_dep, valid_rows, local_lists, state_mean, state_pert, interp_lists, interp_coef
):
    near = near_weights(local_lists, valid_rows[None, :], obs_pert, obs_dep)
    return interpolate(interp_lists.T, state_pert, state_mean, interp_coef, near.reshape(36, 256, 256))


def solution(mesh):
    in_specs = (
        P(("lat", "lon"), None, None),
        P(("lat", "lon"), None),
        P(("lat", "lon")),
        P(("lat", "lon"), None),
        P(None, ("lat", "lon")),
        P(None, ("lat", "lon"), None),
        P(("lat", "lon"), None),
        P(None, ("lat", "lon")),
    )
    out_specs = P(None, ("lat", "lon"), None)
    return jax.shard_map(local, mesh=mesh, in_specs=in_specs, out_specs=out_specs, check_vma=False)
```

```python
import functools

import jax
import jax.numpy as jnp
from jax import lax
from jax.experimental import pallas as pl
from jax.experimental.pallas import tpu as pltpu
from jax.sharding import PartitionSpec as P

NS_ITERS = 4
MESH = pl.DeviceIdType.MESH
BIG = 1 << 20
PARTS = ((400, jnp.bfloat16, "xyz"), (352, jnp.bfloat16, "yzx"), (272, jnp.bfloat16, "zxy"), (16, jnp.float32, "zxy"))
STARTS = (0, 400, 752)
SPANS = ((0, 2), (2, 1), (3, 1))


def coords():
    a = lax.axis_index("lat")
    b = lax.axis_index("lon")
    return {"y": a // 2, "c": a % 2, "x": b // 4, "z": b % 4}


def device(pos):
    return (pos["y"] * 2 + pos["c"], pos["x"] * 4 + pos["z"])


def shifted(pos, axis, step):
    size = 2 if axis == "c" else 4
    return device({**pos, axis: (pos[axis] + step) % size})


def greet(peers):
    barrier = pltpu.get_barrier_semaphore()
    for peer in peers:
        pl.semaphore_signal(barrier, inc=1, device_id=peer, device_id_type=MESH)
    pl.semaphore_wait(barrier, len(peers))


def split(value):
    high = value.astype(jnp.bfloat16)
    return high, (value - high.astype(jnp.float32)).astype(jnp.bfloat16)


def product(left, right):
    (lh, ll), (rh, rl) = left, right
    dot = functools.partial(jnp.dot, preferred_element_type=jnp.float32)
    return dot(lh, rh) + (dot(lh, rl) + dot(ll, rh))


def packed_weights(domains, members, between):
    half = members // 2
    row = lax.broadcasted_iota(jnp.int32, (half, half), 0)
    col = lax.broadcasted_iota(jnp.int32, (half, half), 1)
    wide_row = lax.broadcasted_iota(jnp.int32, (members, members), 0)
    wide_col = lax.broadcasted_iota(jnp.int32, (members, members), 1)
    identity = jnp.where(wide_row == wide_col, 1.0, 0.0).astype(jnp.float32)
    scales, approxes = [], []
    for g12, packed, extra in domains:
        turned = packed.T
        g11 = jnp.where(col > row, packed, turned)
        g22 = jnp.where(col < row, packed, turned)
        g11 = jnp.where(col == row, extra[0:1], g11)
        g22 = jnp.where(col == row, extra[1:2], g22)
        gram = jnp.concatenate(
            [jnp.concatenate([g11, g12], axis=1), jnp.concatenate([g12.T, g22], axis=1)], axis=0)
        system = (members - 1.0) * identity + gram
        scale = jnp.sqrt(jnp.sum(jnp.sum(system * system, axis=0, keepdims=True), axis=1, keepdims=True))
        scales.append(scale)
        approxes.append(system / scale)
    roots = [1.5 * identity - 0.5 * approx for approx in approxes]
    approxes = [product(split(approx), split(root)) for approx, root in zip(approxes, roots)]
    for sweep in range(1, NS_ITERS):
        root_parts = [split(root) for root in roots]
        factors = [split(1.5 * identity - 0.5 * product(parts, split(approx)))
                   for parts, approx in zip(root_parts, approxes)]
        if sweep < NS_ITERS - 1:
            approxes = [product(split(approx), factor) for approx, factor in zip(approxes, factors)]
        roots = [product(factor, parts) for factor, parts in zip(factors, root_parts)]
        if sweep == 2:
            between()
    root_parts = [split(root) for root in roots]
    innovs = [jnp.broadcast_to(jnp.concatenate([extra[2:3], extra[3:4]], axis=1), (8, members)) for _, _, extra in domains]
    inners = [product(split(innov), parts) for innov, parts in zip(innovs, root_parts)]
    means = [product(split(inner), parts) / scale for inner, parts, scale in zip(inners, root_parts, scales)]
    results = []
    for root, mean, scale in zip(roots, means, scales):
        root = jnp.sqrt((members - 1.0) / scale) * root
        t11, t12, t22 = root[:half, :half], root[:half, half:], root[half:, half:]
        exact = [jnp.sum(jnp.where(col == row, t, 0.0), axis=0, keepdims=True) for t in (t11, t22)]
        exact += [mean[:1, :half], mean[:1, half:]]
        highs = [value.astype(jnp.bfloat16).astype(jnp.float32) for value in exact]
        lows = [value - high for value, high in zip(exact, highs)]
        rest = jnp.concatenate(highs + lows + [jnp.zeros((8, half), jnp.float32)], axis=0)
        results.append((t12.astype(jnp.bfloat16), jnp.where(col >= row, t11, t22).astype(jnp.bfloat16),
                        rest.astype(jnp.bfloat16)))
    return results


def store_rows(refs, index, first, value):
    count = value.shape[0]
    for i, start in enumerate(STARTS):
        low, high = max(first, start), min(first + count, start + PARTS[i][0])
        if low < high:
            refs[i][index[i] + (pl.ds(low - start, high - low),)] = value[low - first:high - first]


def fill_server(place, keys_ref, valid_ref, blocks, deps, grams):
    px, py, pz = place
    server = (py * 4 + px) * 4 + pz
    index = ((px, py, pz), (py, pz, px), (pz, px, py))
    rows = lax.broadcasted_iota(jnp.int32, (128, 256), 0)
    row8 = lax.broadcasted_iota(jnp.int32, (8, 128), 0)
    tri_row = lax.broadcasted_iota(jnp.int32, (128, 128), 0)
    tri_col = lax.broadcasted_iota(jnp.int32, (128, 128), 1)
    held, turned, doms, departs = [], [], [], []
    for j in range(4):
        key = keys_ref[server, j]
        block = key & 127
        dom = key >> 12
        count = jnp.where(key < BIG, valid_ref[block >> 6, 4, block & 63], 0)
        values = jnp.where(rows < count, blocks[block], jnp.zeros((), jnp.bfloat16))
        held.append(values)
        turned.append(values.T)
        doms.append(dom)
        depart = jnp.broadcast_to(deps[pl.ds(block, 1), :], (8, 128))
        departs.append(jnp.where(row8 == dom, depart, 0.0).astype(jnp.bfloat16))
    stacked = jnp.concatenate(held, axis=0)
    inn = jnp.dot(jnp.concatenate(departs, axis=1), stacked, preferred_element_type=jnp.float32)
    for d in range(4):
        left = jnp.concatenate(
            [jnp.where(doms[j] == d, turned[j], jnp.zeros((), jnp.bfloat16)) for j in range(4)], axis=1)
        gram = jnp.dot(left, stacked, preferred_element_type=jnp.float32)
        g11, g12, g22 = gram[:128, :128], gram[:128, 128:], gram[128:, 128:]
        packed = jnp.where(tri_col >= tri_row, g11, g22).astype(jnp.bfloat16)
        g12 = g12.astype(jnp.bfloat16)
        d1 = jnp.sum(jnp.where(tri_col == tri_row, g11, 0.0), axis=0, keepdims=True)
        d2 = jnp.sum(jnp.where(tri_col == tri_row, g22, 0.0), axis=0, keepdims=True)
        store_rows(grams, index, d * 256, g12)
        store_rows(grams, index, d * 256 + 128, packed)
        grams[3][pz, px, py, pl.ds(d * 4, 4)] = jnp.concatenate(
            [d1, d2, inn[d:d + 1, :128], inn[d:d + 1, 128:]], axis=0)


def listed_keys(held, own, other):
    lane = lax.broadcasted_iota(jnp.int32, (64, 128), 1)
    dom = lane // 24
    entry = held[:, 0, :]
    owner, local_index = entry >> 6, entry & 63
    block = jnp.where(owner == own, local_index, local_index + 64)
    mine = ((owner == own) | (owner == other)) & (lane < 96)
    value = jnp.where(mine, dom * 4096 + (lane - 24 * dom) * 128 + block, BIG)
    out = jnp.full((64, 128), BIG, jnp.int32)
    for k in range(4):
        least = jnp.min(value, axis=1, keepdims=True)
        out = jnp.where(lane == k, least, out)
        value = jnp.where(value > least, value, BIG)
    return out


def full_weights(packed_ref, index, tiles, k):
    row = lax.broadcasted_iota(jnp.int32, (128, 128), 0)
    col = lax.broadcasted_iota(jnp.int32, (128, 128), 1)
    wide = packed_ref[index + (pl.ds(0, 128),)].astype(jnp.float32)
    packed = packed_ref[index + (pl.ds(128, 128),)].astype(jnp.float32)
    rest = packed_ref[index + (pl.ds(256, 16),)].astype(jnp.float32)
    rest = rest[:4] + rest[4:8]
    first, second = rest[2:3], rest[3:4]
    turned = packed.T
    t11 = jnp.where(col > row, packed, jnp.where(col == row, rest[0:1], turned))
    t22 = jnp.where(col < row, packed, jnp.where(col == row, rest[1:2], turned))
    left, right = pl.ds(0, 128), pl.ds(128, 128)
    tiles[2 * k, :, left] = (t11 + first).astype(jnp.bfloat16)
    tiles[2 * k, :, right] = (wide + second).astype(jnp.bfloat16)
    tiles[2 * k + 1, :, left] = (wide.T + first).astype(jnp.bfloat16)
    tiles[2 * k + 1, :, right] = (t22 + second).astype(jnp.bfloat16)


def reduce_kernel(lists_ref, rows_ref, pert_ref, dep_ref, out_ref, *scratch):
    n = len(PARTS)
    scratch = list(scratch)

    def take(count):
        taken, scratch[:count] = scratch[:count], []
        return taken
    tile_ref, held, keys_vmem, keys_ref, valid_ref, sib_tile, sib_dep, blocks, deps, near, fin, fin_extra = take(12)
    grams = take(n)
    bufs = [[take(4) for _ in range(n)] for _ in range(2)] + [[take(3) for _ in range(n)]]
    send_sem, recv_sem, load_sem, list_send, list_recv, sib_send, sib_recv, halo_send, halo_recv, out_sem = scratch

    pos = coords()
    x, y, z = pos["x"], pos["y"], pos["z"]
    a, b = lax.axis_index("lat"), lax.axis_index("lon")
    lat_up, lat_down = ((a + 1) % 8, b), ((a + 7) % 8, b)
    lon_up, lon_down = (a, (b + 1) % 16), (a, (b + 15) % 16)
    sibling = shifted(pos, "c", 1)
    load = pltpu.make_async_copy(pert_ref, blocks.at[pl.ds(0, 64)], load_sem.at[0])
    load.start()
    tile_ref[...] = jnp.zeros((8, 128), jnp.int32)
    tile_ref[pl.ds(0, 4), pl.ds(0, 24)] = lists_ref[...]
    tile_ref[pl.ds(4, 1), pl.ds(0, 64)] = rows_ref[...]
    own_valid = pltpu.make_async_copy(tile_ref, valid_ref.at[0], load_sem.at[1])
    own_valid.start()
    me = (y * 4 + x) * 4 + z
    entries = tile_ref[...]
    listed = entries
    for d in range(1, 4):
        listed = listed + pltpu.roll(jnp.roll(entries, -d, 0), 24 * d, 1)
    held[me] = listed[0:1]
    deps[pl.ds(0, 64)] = dep_ref[...].astype(jnp.float32)
    greet([shifted(pos, axis, step) for axis in "zxy" for step in (1, 2, 3)]
          + [sibling, lat_up, lat_down, lon_up, lon_down])

    sends = []

    def swap(k, src, dst):
        copy = pltpu.make_async_remote_copy(
            src_ref=src, dst_ref=dst, send_sem=sib_send.at[k], recv_sem=sib_recv.at[k],
            device_id=sibling, device_id_type=MESH)
        copy.start()
        sends.append(copy)
        return copy
    swaps = [swap(0, tile_ref, sib_tile), swap(1, dep_ref, sib_dep), swap(2, pert_ref, blocks.at[pl.ds(64, 64)])]
    for phase, (axis, first, count) in enumerate((("z", me, 1), ("x", (y * 4 + x) * 4, 4), ("y", y * 16, 16))):
        view = held.at[pl.ds(first, count)]
        copies = []
        for step in (1, 2, 3):
            copy = pltpu.make_async_remote_copy(
                src_ref=view, dst_ref=view, send_sem=list_send.at[phase, step - 1],
                recv_sem=list_recv.at[phase, step - 1],
                device_id=shifted(pos, axis, step), device_id_type=MESH)
            copy.start()
            copies.append(copy)
        for copy in copies:
            copy.wait_recv()
        sends += copies
    keys_vmem[...] = listed_keys(held, a * 16 + b, sibling[0] * 16 + sibling[1])
    keys_copy = pltpu.make_async_copy(keys_vmem, keys_ref, load_sem.at[2])
    keys_copy.start()
    swaps[0].wait_recv()
    sib_valid = pltpu.make_async_copy(sib_tile, valid_ref.at[1], load_sem.at[3])
    sib_valid.start()
    swaps[1].wait_recv()
    deps[pl.ds(64, 64)] = sib_dep[...].astype(jnp.float32)
    for copy in (own_valid, keys_copy, sib_valid, load):
        copy.wait()
    swaps[2].wait_recv()

    flights = [[[None] * 6 for _ in range(n)] for _ in range(2)]

    def prefix(i, phase):
        return tuple(pos[axis] for axis in PARTS[i][2][:phase])

    def half(i, phase, target, upper):
        return prefix(i, phase) + (target, pl.ds(2 * upper, 2))

    def landing(i, phase, k):
        if k < 2:
            return bufs[phase][i][k]
        which, upper = {2: (3, 1), 3: (3, 0), 4: (2, 0), 5: (2, 1)}[k]
        return bufs[phase][i][which].at[pl.ds(2 * upper, 2)]

    def start(i, phase, k, source, to_right):
        copy = pltpu.make_async_remote_copy(
            src_ref=source, dst_ref=landing(i, phase, k),
            send_sem=send_sem.at[phase, i, k], recv_sem=recv_sem.at[phase, i, k],
            device_id=shifted(pos, PARTS[i][2][phase], 1 if to_right else 3), device_id_type=MESH)
        copy.start()
        sends.append(copy)
        flights[phase][i][k] = copy

    def coord(i, phase):
        return pos[PARTS[i][2][phase]]

    def send_far(i, phase, sides=(0, 1)):
        target = (coord(i, phase) + 2) % 4
        for side in sides:
            start(i, phase, side, grams[i].at[half(i, phase, target, side)], side == 0)

    def send_right(i, phase):
        start(i, phase, 2, grams[i].at[half(i, phase, (coord(i, phase) + 1) % 4, 1)], True)

    def send_left(i, phase):
        start(i, phase, 3, grams[i].at[half(i, phase, (coord(i, phase) + 3) % 4, 0)], False)

    def each(phase, body):
        def step(j, carry):
            body((j // 4, j % 4) if phase == 0 else (j,))
            return carry
        lax.fori_loop(0, 8 if phase == 0 else 2, step, 0)

    def local_index(i, phase, target, upper, lead):
        return prefix(i, phase) + (target, 2 * upper + lead[0]) + lead[1:]

    def forward(i, phase):
        m = coord(i, phase)
        for k, (target, upper) in enumerate((((m + 1) % 4, 0), ((m + 3) % 4, 1))):
            flights[phase][i][k].wait_recv()
            got = bufs[phase][i][k]

            def body(lead, got=got, target=target, upper=upper):
                mine = grams[i][local_index(i, phase, target, upper, lead)]
                got[lead] = (got[lead].astype(jnp.float32) + mine.astype(jnp.float32)).astype(got.dtype)
            each(phase, body)
            start(i, phase, 4 + k, got, k == 0)

    def arrived(i, phase):
        for k in (2, 3, 4, 5):
            flights[phase][i][k].wait_recv()

    def finish(i, phase, target):
        pairs, singles = bufs[phase][i][2:]

        def body(lead):
            index = prefix(i, phase + 1) + lead
            total = (grams[i][index].astype(jnp.float32) + pairs[lead].astype(jnp.float32)
                     + singles[lead].astype(jnp.float32))
            grams[i][index] = total.astype(grams[i].dtype)
        if phase == 1:
            body((target,))
            return

        def step(j, carry):
            body((target, j))
            return carry
        lax.fori_loop(0, 4, step, 0)

    def send_last(i, step):
        copy = pltpu.make_async_remote_copy(
            src_ref=grams[i].at[prefix(i, 2) + ((coord(i, 2) + step) % 4,)], dst_ref=bufs[2][i][step - 1],
            send_sem=send_sem.at[2, i, step - 1], recv_sem=recv_sem.at[2, i, step - 1],
            device_id=shifted(pos, PARTS[i][2][2], step), device_id_type=MESH)
        copy.start()
        sends.append(copy)
        return copy

    def finish_last(i, copies):
        for copy in copies:
            copy.wait_recv()
        total = grams[i][prefix(i, 2) + (coord(i, 2),)].astype(jnp.float32)
        for got in bufs[2][i]:
            total = total + got[...].astype(jnp.float32)
        if i < 3:
            fin[pl.ds(STARTS[i], PARTS[i][0])] = total
        else:
            fin_extra[...] = total

    def fill(count, place):
        together = 3 if count % 3 == 0 else 2

        def step(j, carry):
            for k in range(together):
                fill_server(tuple(at % 4 for at in place(j * together + k)), keys_ref, valid_ref, blocks, deps, grams)
            return carry
        lax.fori_loop(0, count // together, step, 0)

    fill(8, lambda j: (x + 2, j // 4, z + j))
    send_far(0, 0, (0,))
    fill(8, lambda j: (x + 2, 2 + j // 4, z + j))
    send_far(0, 0, (1,))
    fill(6, lambda j: (x + 3 + j % 3, y + 2, j // 3))
    send_far(1, 0, (0,))
    fill(6, lambda j: (x + 3 + j % 3, y + 2, 2 + j // 3))
    send_far(1, 0, (1,))
    fill(9, lambda j: (x + 3 + j // 3, y + 3 + j % 3, z + 2))
    send_far(2, 0)
    send_far(3, 0)
    fill(9, lambda j: (x + 1, y + 3 + j // 3, z + 3 + j % 3))
    send_right(0, 0)
    fill(9, lambda j: (x + 3, y + 3 + j // 3, z + 3 + j % 3))
    send_left(0, 0)
    fill(3, lambda j: (x, y + 1, z + 3 + j))
    send_right(1, 0)
    fill(3, lambda j: (x, y + 3, z + 3 + j))
    send_left(1, 0)
    fill(3, lambda j: (x, y, z + 3 + j))
    for i in (2, 3):
        send_right(i, 0)
        send_left(i, 0)
    for i in range(n):
        forward(i, 0)
    for i in range(n):
        arrived(i, 0)
        m = coord(i, 1)
        finish(i, 0, (m + 2) % 4)
        send_far(i, 1)
        finish(i, 0, (m + 1) % 4)
        send_right(i, 1)
        finish(i, 0, (m + 3) % 4)
        send_left(i, 1)
    for i in range(n):
        finish(i, 0, coord(i, 1))
        forward(i, 1)
    last = []
    for i in range(n):
        arrived(i, 1)
        copies = []
        for step in (2, 1, 3):
            finish(i, 1, (coord(i, 2) + step) % 4)
            copies.append(send_last(i, step))
        finish(i, 1, coord(i, 2))
        last.append(copies)
    for i in range(n):
        finish_last(i, last[i])

    def solve(pair, between):
        domains = [(fin[pl.ds(d * 256, 128)], fin[pl.ds(d * 256 + 128, 128)], fin_extra[pl.ds(d * 4, 4)]) for d in pair]
        for d, (t12, triangles, rest) in zip(pair, packed_weights(domains, 256, between)):
            near[1, 1, d, pl.ds(0, 128)] = t12
            near[1, 1, d, pl.ds(128, 128)] = triangles
            near[1, 1, d, pl.ds(256, 16)] = rest

    halos = {}

    def halo(chunk, k, origin, to, target):
        span = pl.ds(*SPANS[chunk])
        copy = pltpu.make_async_remote_copy(
            src_ref=near.at[origin + (span,)], dst_ref=near.at[to + (span,)],
            send_sem=halo_send.at[chunk, k], recv_sem=halo_recv.at[chunk, k],
            device_id=target, device_id_type=MESH)
        copy.start()
        sends.append(copy)
        halos[chunk, to] = copy

    outs = []

    def unpack(chunk, at):
        start_dom, count = SPANS[chunk]
        first = (at[0] * 3 + at[1]) * 4 + start_dom
        for k in range(count):
            full_weights(near, at + (start_dom + k,), blocks, first + k)
        span = pl.ds(2 * first, 2 * count)
        copy = pltpu.make_async_copy(blocks.at[span], out_ref.at[span], out_sem.at[len(outs)])
        copy.start()
        outs.append(copy)

    def own_halo(chunk):
        halo(chunk, 0, (1, 1), (1, 0), lon_up)
        halo(chunk, 1, (1, 1), (1, 2), lon_down)
        halo(chunk, 2, (1, 1), (0, 1), lat_up)
        halo(chunk, 3, (1, 1), (2, 1), lat_down)

    def corner_halo(chunk):
        for column, k in ((0, 4), (2, 6)):
            halos[chunk, (1, column)].wait_recv()
            halo(chunk, k, (1, column), (0, column), lat_up)
            halo(chunk, k + 1, (1, column), (2, column), lat_down)

    solve((0, 1), lambda: None)
    own_halo(0)
    solve((2, 3), lambda: corner_halo(0))
    own_halo(1)
    own_halo(2)
    for chunk in range(3):
        unpack(chunk, (1, 1))
    for column in (0, 2):
        unpack(0, (1, column))
    for chunk in (1, 2):
        corner_halo(chunk)
        for column in (0, 2):
            unpack(chunk, (1, column))
    for chunk in range(3):
        for column in (1, 0, 2):
            for line in (0, 2):
                halos[chunk, (line, column)].wait_recv()
                unpack(chunk, (line, column))
    for copy in sends:
        copy.wait_send()
    for copy in outs:
        copy.wait()


def near_weights(lists, rows, pert, dep):
    n = len(PARTS)
    hbm = pl.BlockSpec(memory_space=pltpu.HBM)
    full = pl.BlockSpec(memory_space=pltpu.VMEM)

    def vmem(shape, kind):
        return pltpu.VMEM(shape, kind)
    scratch = [
        vmem((8, 128), jnp.int32),
        vmem((64, 1, 128), jnp.int32),
        vmem((64, 128), jnp.int32),
        pltpu.SMEM((64, 128), jnp.int32),
        pltpu.SMEM((2, 8, 128), jnp.int32),
        vmem((8, 128), jnp.int32),
        vmem((64, 128), jnp.bfloat16),
        vmem((128, 128, 256), jnp.bfloat16),
        vmem((128, 128), jnp.float32),
        vmem((3, 3, 4, 272, 128), jnp.bfloat16),
        vmem((1024, 128), jnp.float32),
        vmem((16, 128), jnp.float32),
    ]
    scratch += [vmem((4, 4, 4, r, 128), t) for r, t, _ in PARTS]
    for shape in ((2, 4), (2,)):
        for r, t, _ in PARTS:
            scratch += [vmem(shape + (r, 128), t)] * 2 + [vmem((4,) + shape[1:] + (r, 128), t)] * 2
    for r, t, _ in PARTS:
        scratch += [vmem((r, 128), t)] * 3
    scratch += [pltpu.SemaphoreType.DMA(shape) for shape in (
        (3, n, 6), (3, n, 6), (4,), (3, 3), (3, 3), (3,), (3,), (3, 8), (3, 8), (27,))]
    return pl.pallas_call(
        reduce_kernel,
        out_shape=jax.ShapeDtypeStruct((72, 128, 256), jnp.bfloat16),
        in_specs=[full, full, hbm, full],
        out_specs=hbm,
        scratch_shapes=scratch,
        compiler_params=pltpu.CompilerParams(
            collective_id=1, has_side_effects=True, vmem_limit_bytes=58 << 20),
        name="reduce",
    )(lists, rows, pert, dep)


CHUNK = 512


def interp_kernel(lists_ref, mean_ref, coef_ref, pert_ref, near_ref, out_ref, held, near, done, near_sem, in_sem, out_sem):
    chunks = held.shape[1] // CHUNK
    a, b = lax.axis_index("lat"), lax.axis_index("lon")
    fetch_near = [pltpu.make_async_copy(near_ref.at[pl.ds(4 * k, 4)], near.at[pl.ds(4 * k, 4)], near_sem.at[k])
                  for k in range(9)]
    for copy in fetch_near:
        copy.start()

    def place(tile, corner):
        domain = lists_ref[corner, tile]
        lat, lon = domain // 64, (domain // 4) % 16
        return ((lat - a + 1) * 3 + (lon - b + 17) % 16) * 4 + domain % 4

    def fetch(c):
        span = pl.ds(pl.multiple_of(c * CHUNK, CHUNK), CHUNK)
        return pltpu.make_async_copy(pert_ref.at[:, span], held.at[:, span], in_sem.at[c])

    def write(c):
        span = pl.ds(pl.multiple_of(c * CHUNK, CHUNK), CHUNK)
        return pltpu.make_async_copy(done.at[:, span], out_ref.at[:, span], out_sem.at[c])

    for c in range(2):
        fetch(c).start()
    for copy in fetch_near:
        copy.wait()

    @pl.loop(2, chunks)
    def _(c):
        fetch(c).start()

    @pl.loop(0, chunks)
    def _(c):
        first = pl.multiple_of(c * CHUNK, CHUNK)
        fetch(c).wait()
        lane = lax.broadcasted_iota(jnp.int32, (8, 128), 1)
        level = lax.broadcasted_iota(jnp.int32, (8, 128), 0)

        def spread(value, group):
            value = jnp.where(lane // 32 == group, value, 0.0)
            value = value + pltpu.roll(value, 32, 1)
            return value + pltpu.roll(value, 64, 1)

        for tile in range(CHUNK // 32):
            span = pl.ds(pl.multiple_of(first + tile * 32, 32), 32)
            lanes = pl.ds(pl.multiple_of(first + tile // 4 * 128, 128), 128)
            means = spread(mean_ref[:, lanes], tile % 4)
            coef = coef_ref[:, lanes]
            coefs = spread(jnp.concatenate([coef, coef], axis=0), tile % 4)
            total = jnp.concatenate(
                [jnp.sum(jnp.where(level == lane // 32 + 4 * k, means, 0.0), axis=0, keepdims=True) for k in range(2)], axis=1)
            right = held[:, span, :].reshape(256, 256)
            for corner in range(4):
                prod = lax.dot_general(near[place(c * (CHUNK // 32) + tile, corner)], right, (((1,), (1,)), ((), ())), preferred_element_type=jnp.float32)
                row = coefs[corner:corner + 1]
                total = total + prod * jnp.concatenate([row, row], axis=1)
            done[:, span, :] = total.astype(jnp.bfloat16).T.reshape(8, 32, 256)
        write(c).start()

    @pl.loop(0, chunks)
    def _(c):
        write(c).wait()


def interpolate(lists, pert, mean, coef, near):
    hbm = pl.BlockSpec(memory_space=pltpu.HBM)
    full = pl.BlockSpec(memory_space=pltpu.VMEM)
    chunks = pert.shape[1] // CHUNK
    return pl.pallas_call(
        interp_kernel,
        out_shape=jax.ShapeDtypeStruct(pert.shape, jnp.bfloat16),
        in_specs=[pl.BlockSpec(memory_space=pltpu.SMEM), full, full, hbm, hbm],
        out_specs=hbm,
        scratch_shapes=[
            pltpu.VMEM(pert.shape, jnp.bfloat16),
            pltpu.VMEM(near.shape, jnp.bfloat16),
            pltpu.VMEM(pert.shape, jnp.bfloat16),
            pltpu.SemaphoreType.DMA((9,)),
            pltpu.SemaphoreType.DMA((chunks,)),
            pltpu.SemaphoreType.DMA((chunks,)),
        ],
        compiler_params=pltpu.CompilerParams(vmem_limit_bytes=58 << 20),
        name="interp",
    )(lists, mean, coef, pert, near)


def local(
    obs_pert, obs_dep, valid_rows, local_lists, state_mean, state_pert, interp_lists, interp_coef
):
    near = near_weights(local_lists, valid_rows[None, :], obs_pert, obs_dep)
    return interpolate(interp_lists.T, state_pert, state_mean, interp_coef, near.reshape(36, 256, 256))


def solution(mesh):
    in_specs = (
        P(("lat", "lon"), None, None),
        P(("lat", "lon"), None),
        P(("lat", "lon")),
        P(("lat", "lon"), None),
        P(None, ("lat", "lon")),
        P(None, ("lat", "lon"), None),
        P(("lat", "lon"), None),
        P(None, ("lat", "lon")),
    )
    out_specs = P(None, ("lat", "lon"), None)
    return jax.shard_map(local, mesh=mesh, in_specs=in_specs, out_specs=out_specs, check_vma=False)
```
